256 devices in a mesh: rows: 64 (over y, z, core), feat: 4 (over x).
Axes of the slice: x: 4, y: 4, z: 8, core: 2. Of those that a mesh axis runs over, the one named last changes fastest.
Arguments:
- feats: bfloat16 [256, 131072], P('feat', 'rows'), may hold values from -6 to 6
- weight: bfloat16 [256, 256], P('feat'), may hold values from -0.375 to 0.375
- bias: float32 [256], P('feat'), may hold values from -3 to 3
- tile_cols: int32 [8192], P('rows'), may hold values from 0 to 1023, as said below
- tile_values: bfloat16 [8192, 128, 128], P('rows'), may hold values from -0.1875 to 0.1875
- cotangent: bfloat16 [256, 131072], P('feat', 'rows'), may hold values from -6 to 6
Outputs:
- hidden_out: bfloat16 [256, 131072], P('feat', 'rows')
- grad_input: float32 [256, 131072], P('feat', 'rows')
- grad_weight: float32 [256, 256], P('feat')
- grad_bias: float32 [256], P('feat')
The draws below stay inside these ranges and needn't reach their ends.
Inputs may be any that keep to these rules, and one draw needn't show every extreme that they name: `tile_cols`: column blocks of tiles. In each row block the first 4 tiles have column blocks on the same index of rows as the row block (index = column block // 16). Of the other tiles of one index of rows, at most 2 have column blocks on any one index, and in every draw one index receives exactly 2 such tiles from every index.
All inputs are finite; a program needn't handle non-finite values.
Results may differ from the reference program's by a relative error of at most 0.0058.
Values may be sent and summed in bfloat16 or wider, within the bound.
No kernel may reach another device: no remote copies, remote signals or barrier semaphores. Data moves between devices by JAX's collectives and lax.ppermute only.
A program may use at most 128 MiB of HBM per device.

```python
import math
import jax
import jax.numpy as jnp
from jax import lax

HID = 256
HID_IN = 256
BLK = 128
TB = 8
TL = 4
R_BLK = 16
REM_DEV = 64
CAP = 2
NTILES = 8192
NODES = 131072
N_ROWS = 64


def draw_tile_cols(key, part):
    common_key, device_key = jax.random.split(jax.random.fold_in(key, 17), 2)
    num_slots = N_ROWS * CAP
    penalty_key, hot_key = jax.random.split(common_key, 2)
    penalty = jax.random.randint(penalty_key, (N_ROWS,), 0, 3)
    hottest = jax.random.randint(hot_key, (), 0, N_ROWS)
    slot_owner = jnp.arange(num_slots) // CAP

    def one_device(dkey, device):
        rank_key, shuffle_key, within_key, local_key = jax.random.split(dkey, 4)
        ranks = jax.random.permutation(rank_key, num_slots)
        score = ranks + penalty[slot_owner] * num_slots
        score = jnp.where(slot_owner == hottest, -1 - jnp.arange(num_slots) % CAP, score)
        chosen = jnp.argsort(score)[:REM_DEV]
        chosen = jax.random.permutation(shuffle_key, chosen)
        owners = chosen // CAP
        within = jax.random.randint(within_key, (REM_DEV,), 0, R_BLK)
        remote = (owners * R_BLK + within).reshape(R_BLK, TB - TL)
        local = device * R_BLK + jax.random.randint(local_key, (R_BLK, TL), 0, R_BLK)
        return jnp.concatenate([local, remote], axis=1).reshape(-1)
    keys = jax.random.split(device_key, N_ROWS)
    result = jax.vmap(one_device)(keys, jnp.arange(N_ROWS))
    return result.reshape(-1).astype(jnp.int32)


def block_scale(key, shape, cuts, least, high):
    factor_of = 1.0
    for dim, shards_of in cuts:
        draws = jax.random.uniform(jax.random.fold_in(jax.random.fold_in(key, 6), dim), (shards_of,), jnp.float32, least / len(cuts), high / len(cuts))
        factor_of = factor_of * jnp.repeat(jnp.exp(draws), shape[dim] // shards_of).reshape((-1,) + (1,) * (len(shape) - 1 - dim))
    return factor_of


def normal_values(stream_key, dims, scale, bound, cuts=(), held_as=jnp.bfloat16):
    entries = jax.random.normal(stream_key, dims, jnp.float32) * scale
    if len(cuts) > 0:
        entries = block_scale(stream_key, dims, cuts, -0.22, 0.18) * entries
    return jnp.clip(entries, min=-bound, max=bound).astype(held_as)


def setup_inputs(seed: int = 0) -> dict:
    streams_of = jax.random.split(jax.random.key(seed), 7)
    return {
        "feats": normal_values(streams_of[0], (HID_IN, NODES), 1.0, 6.0, ((0, 4), (1, 64))),
        "weight": normal_values(streams_of[1], (HID_IN, HID), HID_IN ** -0.5, 0.375, ((0, 4),)),
        "bias": normal_values(streams_of[2], (HID,), 0.5, 3.0, ((0, 4),), jnp.float32),
        "tile_cols": draw_tile_cols(jax.random.fold_in(streams_of[6], 71), 0),
        "tile_values": normal_values(streams_of[4], (NTILES, BLK, BLK), (TB * BLK) ** -0.5, 0.1875, ((0, 64),)),
        "cotangent": normal_values(streams_of[5], (HID, NODES), 1.0, 6.0, ((0, 4), (1, 64))),
    }


def reference(feats, weight, bias, tile_cols, tile_values, cotangent):
    nodes = feats.shape[1]
    block_count = nodes // BLK
    proj = jnp.dot(weight.T, feats, preferred_element_type=jnp.float32).astype(jnp.bfloat16)
    proj_blocks = proj.reshape(HID, block_count, BLK).transpose(1, 0, 2)
    col_groups = tile_cols.reshape(N_ROWS, R_BLK, TB).astype(jnp.int32)
    value_groups = tile_values.reshape(N_ROWS, R_BLK, TB, BLK, BLK)

    def forward_group(pair):
        columns, values = pair
        fetched = proj_blocks[columns].astype(jnp.float32)
        return jnp.einsum('btfk,btnk->bfn', fetched, values.astype(jnp.float32))
    summed = lax.map(forward_group, (col_groups, value_groups)).reshape(block_count, HID, BLK)
    pre = summed.transpose(1, 0, 2).reshape(HID, nodes) + bias[:, None]
    hidden_out = jax.nn.silu(pre).astype(jnp.bfloat16)
    sigma = jax.nn.sigmoid(pre)
    grad_pre = cotangent.astype(jnp.float32) * (sigma * (1.0 + pre * (1.0 - sigma)))
    grad_blocks = grad_pre.astype(jnp.bfloat16).reshape(HID, block_count, BLK).transpose(1, 0, 2)
    grad_blocks = grad_blocks.reshape(N_ROWS, R_BLK, HID, BLK)

    def backward_group(total, triple):
        columns, values, grads = triple
        contrib = jnp.einsum('bfn,btnk->btfk', grads.astype(jnp.float32), values.astype(jnp.float32))
        return (total.at[columns.reshape(-1)].add(contrib.reshape(-1, HID, BLK)), None)
    start_total = jnp.zeros((block_count, HID, BLK), jnp.float32)
    grad_proj_blocks, _ = lax.scan(backward_group, start_total, (col_groups, value_groups, grad_blocks))
    grad_proj = grad_proj_blocks.transpose(1, 0, 2).reshape(HID, nodes).astype(jnp.bfloat16)
    grad_input = jnp.dot(weight, grad_proj, preferred_element_type=jnp.float32)
    grad_weight = jnp.dot(feats, grad_proj.T, preferred_element_type=jnp.float32) / math.sqrt(nodes)
    grad_bias = lax.optimization_barrier(jnp.sum(grad_pre, axis=1)) / math.sqrt(nodes)
    return (hidden_out, grad_input, grad_weight, grad_bias)
```

```python
import math

import jax
import jax.numpy as jnp
from jax import lax
from jax.experimental import pallas as pl
from jax.experimental.pallas import tpu as pltpu
from jax.sharding import PartitionSpec as P

TL = 4
BF = jnp.bfloat16
F32 = jnp.float32
VMEM = pl.BlockSpec(memory_space=pltpu.VMEM)
SMEM = pl.BlockSpec(memory_space=pltpu.SMEM)


def lanes(index, width):
    return pl.ds(pl.multiple_of(index * width, width), width)


def pack_kernel(wanted_ref, feats_ref, out_ref):
    block = out_ref.shape[2]

    def body(s, carry):
        w = jnp.maximum(wanted_ref[s], 0)
        out_ref[s] = feats_ref[:, lanes(w, block)]
        return carry

    lax.fori_loop(0, out_ref.shape[0], body, 0, unroll=8)


def pack(wanted, feats, block):
    slots = wanted.shape[0]
    return pl.pallas_call(
        pack_kernel,
        out_shape=jax.ShapeDtypeStruct((slots, feats.shape[0], block), feats.dtype),
        in_specs=[SMEM, VMEM],
        out_specs=VMEM,
        name="pack",
    )(wanted, feats)


def dot(a, b, dims):
    return lax.dot_general(a, b, ((dims[:1], dims[1:]), ((), ())), preferred_element_type=F32)


STEP = 4


def agg_local_kernel(cols_ref, feats_ref, tiles_ref, out_ref):
    i = pl.program_id(0)
    count, block = tiles_ref.shape[1], tiles_ref.shape[2]
    for rr in range(STEP):
        acc = None
        for t in range(0, count, 2):
            base = (i * STEP + rr) * count + t
            lhs = jnp.concatenate(
                [feats_ref[:, lanes(cols_ref[base + k], block)] for k in range(2)], axis=1
            )
            rhs = jnp.concatenate([tiles_ref[rr, t + k] for k in range(2)], axis=1)
            term = dot(lhs, rhs, (1, 1))
            acc = term if acc is None else acc + term
        out_ref[:, rr * block : (rr + 1) * block] = acc


def agg_local(cols, feats, tiles):
    row_blocks, _, block, _ = tiles.shape
    width = feats.shape[0]
    return pl.pallas_call(
        agg_local_kernel,
        grid=(row_blocks // STEP,),
        out_shape=jax.ShapeDtypeStruct((width, row_blocks * block), F32),
        in_specs=[
            SMEM,
            pl.BlockSpec(feats.shape, lambda i: (0, 0)),
            pl.BlockSpec((STEP, TL, block, block), lambda i: (i, 0, 0, 0)),
        ],
        out_specs=pl.BlockSpec((width, STEP * block), lambda i: (0, i)),
        name="agg_local",
        cost_estimate=pl.CostEstimate(
            flops=2 * width * row_blocks * TL * block * block, bytes_accessed=3 << 20, transcendentals=0
        ),
    )(cols, feats, tiles)


def agg_remote_kernel(slots_ref, recv_ref, tiles_ref, local_ref, out_ref):
    i = pl.program_id(0)
    count, block = tiles_ref.shape[1], tiles_ref.shape[2]
    for rr in range(STEP):
        acc = local_ref[:, rr * block : (rr + 1) * block]
        for t in range(0, count, 2):
            base = (i * STEP + rr) * count + t
            lhs = jnp.concatenate([recv_ref[slots_ref[base + k]] for k in range(2)], axis=1)
            rhs = jnp.concatenate([tiles_ref[rr, t + k] for k in range(2)], axis=1)
            acc = acc + dot(lhs, rhs, (1, 1))
        out_ref[:, rr * block : (rr + 1) * block] = acc.astype(out_ref.dtype)


def agg_remote(slots, recv, tiles, local):
    row_blocks, per_block, block, _ = tiles.shape
    rem = per_block - TL
    width = local.shape[0]
    return pl.pallas_call(
        agg_remote_kernel,
        grid=(row_blocks // STEP,),
        out_shape=jax.ShapeDtypeStruct(local.shape, BF),
        in_specs=[
            SMEM,
            pl.BlockSpec(recv.shape, lambda i: (0, 0, 0)),
            pl.BlockSpec((STEP, rem, block, block), lambda i: (i, 1, 0, 0)),
            pl.BlockSpec((width, STEP * block), lambda i: (0, i)),
        ],
        out_specs=pl.BlockSpec((width, STEP * block), lambda i: (0, i)),
        name="agg_remote",
        cost_estimate=pl.CostEstimate(
            flops=2 * width * row_blocks * rem * block * block, bytes_accessed=5 << 20, transcendentals=0
        ),
    )(slots, recv, tiles, local)


def mid_kernel(
    me_ref,
    own_ref,
    low_ref,
    high_ref,
    far_a_ref,
    far_b_ref,
    cot_ref,
    w_ref,
    bias_ref,
    wown_ref,
    hid_ref,
    g_ref,
    gw_ref,
    gb_ref,
    agg_scr,
    hid_scr,
    wt_scr,
    gb_scr,
):
    i = pl.program_id(0)
    width = own_ref.shape[0]
    half = width // 2
    me, below, above, far = me_ref[0], me_ref[1], me_ref[2], me_ref[3]

    def rows(index, size=width):
        return pl.ds(pl.multiple_of(index, half), size)

    @pl.when(i == 0)
    def _():
        wt_scr[...] = w_ref[...].astype(F32).T.astype(BF)
        gw_ref[...] = jnp.zeros_like(gw_ref)
        gb_scr[...] = jnp.zeros_like(gb_scr)

    agg_scr[rows(below * width)] = low_ref[...]
    agg_scr[rows(above * width)] = high_ref[...]
    agg_scr[rows(far * width, half)] = far_a_ref[...]
    agg_scr[rows(far * width + half, half)] = far_b_ref[...]
    agg_scr[rows(me * width)] = own_ref[...]
    pre = dot(wt_scr[...], agg_scr[...], (1, 0))
    bias = bias_ref[:, :3].astype(F32)
    pre = pre + ((bias[:, 2:3] + bias[:, 1:2]) + bias[:, 0:1])
    sigma = jax.nn.sigmoid(pre)
    hid_scr[...] = (pre * sigma).astype(BF)
    hid_ref[...] = hid_scr[rows(me * width)]
    grad_pre = cot_ref[...].astype(F32) * (sigma * (1.0 + pre * (1.0 - sigma)))
    total = grad_pre[:, :128]
    for k in range(1, grad_pre.shape[1] // 128):
        total = total + grad_pre[:, k * 128 : (k + 1) * 128]
    gb_scr[...] += total
    grad_b = grad_pre.astype(BF)
    g_ref[...] = dot(wown_ref[...], grad_b, (1, 0)).astype(BF)
    gw_ref[...] += dot(own_ref[...], grad_b, (1, 1))

    @pl.when(i == pl.num_programs(0) - 1)
    def _():
        gb_ref[...] = gb_scr[rows(me * width)]


def mid(me, pieces, packed, w_own):
    own, low, high, far_a, far_b = pieces
    width, nodes = own.shape
    hid_all = packed.shape[0]
    chunk = 512
    col = lambda i: (0, i)
    return pl.pallas_call(
        mid_kernel,
        grid=(nodes // chunk,),
        out_shape=(
            jax.ShapeDtypeStruct((width, nodes), BF),
            jax.ShapeDtypeStruct((width, nodes), BF),
            jax.ShapeDtypeStruct((width, hid_all), F32),
            jax.ShapeDtypeStruct((width, 128), F32),
        ),
        in_specs=[
            SMEM,
            pl.BlockSpec((width, chunk), col),
            pl.BlockSpec((width, chunk), col),
            pl.BlockSpec((width, chunk), col),
            pl.BlockSpec((width // 2, chunk), col),
            pl.BlockSpec((width // 2, chunk), col),
            pl.BlockSpec((hid_all, chunk), col),
            pl.BlockSpec((hid_all, hid_all), lambda i: (0, nodes // hid_all)),
            pl.BlockSpec((hid_all, 128), lambda i: (0, (nodes + hid_all) // 128)),
            pl.BlockSpec((width, hid_all), lambda i: (0, 0)),
        ],
        out_specs=(
            pl.BlockSpec((width, chunk), col),
            pl.BlockSpec((width, chunk), col),
            pl.BlockSpec((width, hid_all), lambda i: (0, 0)),
            pl.BlockSpec((width, 128), lambda i: (0, 0)),
        ),
        scratch_shapes=[
            pltpu.VMEM((hid_all, chunk), BF),
            pltpu.VMEM((hid_all, chunk), BF),
            pltpu.VMEM((hid_all, hid_all), BF),
            pltpu.VMEM((hid_all, 128), F32),
        ],
        name="mid",
        cost_estimate=pl.CostEstimate(
            flops=2 * nodes * hid_all * (hid_all + 2 * width),
            bytes_accessed=3 << 20,
            transcendentals=nodes * hid_all,
        ),
    )(me, own, low, high, far_a, far_b, packed, packed, packed, w_own)


def back_remote_kernel(slots_ref, g_ref, tiles_ref, out_ref):
    i = pl.program_id(0)
    count, block = tiles_ref.shape[1], tiles_ref.shape[2]

    @pl.when(i == 0)
    def _():
        out_ref[...] = jnp.zeros_like(out_ref)

    for rr in range(STEP):
        lhs = g_ref[:, rr * block : (rr + 1) * block]
        for t in range(0, count, 2):
            base = (i * STEP + rr) * count + t
            rhs = jnp.concatenate([tiles_ref[rr, t + k] for k in range(2)], axis=1)
            term = dot(lhs, rhs, (1, 0)).astype(BF)
            for k in range(2):
                out_ref[slots_ref[base + k]] = term[:, k * block : (k + 1) * block]


def back_remote(slots, g, tiles, num_slots):
    row_blocks, per_block, block, _ = tiles.shape
    rem = per_block - TL
    width = g.shape[0]
    return pl.pallas_call(
        back_remote_kernel,
        grid=(row_blocks // STEP,),
        out_shape=jax.ShapeDtypeStruct((num_slots, width, block), BF),
        in_specs=[
            SMEM,
            pl.BlockSpec((width, STEP * block), lambda i: (0, i)),
            pl.BlockSpec((STEP, rem, block, block), lambda i: (i, 1, 0, 0)),
        ],
        out_specs=pl.BlockSpec((num_slots, width, block), lambda i: (0, 0, 0)),
        name="back_remote",
        cost_estimate=pl.CostEstimate(
            flops=2 * width * row_blocks * rem * block * block, bytes_accessed=5 << 20, transcendentals=0
        ),
    )(slots, g, tiles)


def back_local_kernel(cols_ref, g_ref, tiles_ref, out_ref):
    i = pl.program_id(0)
    count, block = tiles_ref.shape[1], tiles_ref.shape[2]

    @pl.when(i == 0)
    def _():
        out_ref[...] = jnp.zeros_like(out_ref)

    for rr in range(STEP):
        lhs = g_ref[:, rr * block : (rr + 1) * block]
        for t in range(0, count, 2):
            base = (i * STEP + rr) * count + t
            rhs = jnp.concatenate([tiles_ref[rr, t + k] for k in range(2)], axis=1)
            term = dot(lhs, rhs, (1, 0))
            for k in range(2):
                out_ref[:, lanes(cols_ref[base + k], block)] += term[:, k * block : (k + 1) * block]


def back_local(cols, g, tiles):
    row_blocks, _, block, _ = tiles.shape
    width = g.shape[0]
    return pl.pallas_call(
        back_local_kernel,
        grid=(row_blocks // STEP,),
        out_shape=jax.ShapeDtypeStruct(g.shape, F32),
        in_specs=[
            SMEM,
            pl.BlockSpec((width, STEP * block), lambda i: (0, i)),
            pl.BlockSpec((STEP, TL, block, block), lambda i: (i, 0, 0, 0)),
        ],
        out_specs=pl.BlockSpec(g.shape, lambda i: (0, 0)),
        name="back_local",
        cost_estimate=pl.CostEstimate(
            flops=2 * width * row_blocks * TL * block * block, bytes_accessed=3 << 20, transcendentals=0
        ),
    )(cols, g, tiles)


def finish_kernel(wanted_ref, recv_ref, local_ref, out_ref):
    block = recv_ref.shape[2]
    out_ref[...] = local_ref[...]

    def body(s, carry):
        w = wanted_ref[s]

        @pl.when(w >= 0)
        def _():
            out_ref[:, lanes(w, block)] += recv_ref[s].astype(F32)

        return carry

    lax.fori_loop(0, recv_ref.shape[0], body, 0, unroll=4)


def finish(wanted, recv, local):
    return pl.pallas_call(
        finish_kernel,
        out_shape=jax.ShapeDtypeStruct(local.shape, F32),
        in_specs=[SMEM, VMEM, VMEM],
        out_specs=VMEM,
        name="finish",
    )(wanted, recv, local)


def split_bf16(x, terms):
    parts = []
    for _ in range(terms):
        part = lax.reduce_precision(x, 8, 7)
        parts.append(part.astype(BF))
        x = x - part
    return parts


def local(feats, weight, bias, tile_cols, tile_values, cotangent):
    width, nodes_dev = feats.shape
    hid_all = weight.shape[1]
    block = tile_values.shape[1]
    row_blocks = nodes_dev // block
    peers = lax.axis_size("rows")
    fpeers = lax.axis_size("feat")
    per_block = tile_cols.shape[0] // row_blocks
    remote_count = row_blocks * (per_block - TL)
    capacity = 2 * remote_count // peers
    num_slots = peers * capacity

    bias_cols = jnp.pad(jnp.stack(split_bf16(bias, 3), axis=1), ((0, 0), (0, 125)))
    packed = jnp.concatenate([cotangent, weight, bias_cols], axis=1)
    packed = lax.all_gather(packed, "feat", axis=0, tiled=True)

    grid = tile_cols.reshape(row_blocks, per_block)
    tiles = tile_values.reshape(row_blocks, per_block, block, block)
    local_cols = (grid[:, :TL] % row_blocks).reshape(-1)
    remote_cols = grid[:, TL:].reshape(-1)
    owner = remote_cols // row_blocks
    order = jnp.arange(remote_count)
    earlier = (owner[:, None] == owner[None, :]) & (order[None, :] < order[:, None])
    slots = owner * capacity + jnp.sum(earlier.astype(jnp.int32), axis=1)
    hit = slots[None, :] == jnp.arange(num_slots)[:, None]
    request = jnp.max(jnp.where(hit, (remote_cols % row_blocks)[None, :], -1), axis=1)
    wanted = lax.all_to_all(
        request.reshape(peers, capacity), "rows", split_axis=0, concat_axis=0, tiled=True
    ).reshape(-1)

    def exchange(x):
        x = x.reshape(peers, capacity, width, block)
        x = lax.all_to_all(x, "rows", split_axis=0, concat_axis=0, tiled=True)
        return x.reshape(num_slots, width, block)

    fetched = exchange(pack(wanted, feats, block))
    agg = agg_local(local_cols, feats, tiles)
    agg = agg_remote(slots, fetched, tiles, agg)

    up = [(k, (k + 1) % fpeers) for k in range(fpeers)]
    down = [(k, (k - 1) % fpeers) for k in range(fpeers)]
    low = lax.ppermute(agg, "feat", up)
    high = lax.ppermute(agg, "feat", down)
    far_a = lax.ppermute(low[: width // 2], "feat", up)
    far_b = lax.ppermute(high[width // 2 :], "feat", down)
    x = lax.axis_index("feat")
    me = jnp.stack([x, (x - 1) % fpeers, (x + 1) % fpeers, (x + 2) % fpeers]).astype(jnp.int32)
    hidden_out, g, grad_w, grad_b = mid(me, (agg, low, high, far_a, far_b), packed, weight)

    returned = exchange(back_remote(slots, g, tiles, num_slots))
    own = back_local(local_cols, g, tiles)
    grad_input = finish(wanted, returned, own)

    divisor = math.sqrt(nodes_dev * peers)
    sums = jnp.concatenate([grad_w.reshape(peers, -1), jnp.sum(grad_b, axis=1).reshape(peers, -1)], axis=1)
    sums = lax.all_to_all(sums, "rows", split_axis=0, concat_axis=0, tiled=True)
    total = jnp.sum(sums, axis=0, keepdims=True) / divisor
    total = jnp.broadcast_to(total, sums.shape)
    total = lax.all_to_all(total, "rows", split_axis=0, concat_axis=0, tiled=True)
    per = grad_w.size // peers
    return (
        hidden_out,
        grad_input,
        total[:, :per].reshape(width, hid_all),
        total[:, per:].reshape(width),
    )


def solution(mesh):
    placed = (
        P("feat", "rows"),
        P("feat", None),
        P("feat"),
        P("rows"),
        P("rows", None, None),
        P("feat", "rows"),
    )
    return jax.shard_map(
        local,
        mesh=mesh,
        in_specs=placed,
        out_specs=(P("feat", "rows"), P("feat", "rows"), P("feat", None), P("feat")),
        check_vma=False,
    )
```

```python
import functools
import math

import jax
import jax.numpy as jnp
from jax import lax
from jax.experimental import pallas as pl
from jax.experimental.pallas import tpu as pltpu
from jax.sharding import PartitionSpec as P

TL = 4
BF = jnp.bfloat16
F32 = jnp.float32
VMEM = pl.BlockSpec(memory_space=pltpu.VMEM)
ANY = pl.BlockSpec(memory_space=pl.ANY)
SMEM = pl.BlockSpec(memory_space=pltpu.SMEM)


def lanes(index, width):
    return pl.ds(pl.multiple_of(index * width, width), width)


NY, NZ, NC = 4, 8, 2
CAP = 2
ORDER = (0, 1, 7, 2, 6, 3, 5, 4)
GROUPS = ((0, 3), (3, 5), (5, 8))
PER = NZ * CAP


def shift(x, dy=0, dz=0, dc=0):
    pairs = []
    for y in range(NY):
        for z in range(NZ):
            for c in range(NC):
                to = ((y + dy) % NY * NZ + (z + dz) % NZ) * NC + (c + dc) % NC
                pairs.append(((y * NZ + z) * NC + c, to))
    return lax.ppermute(x, "rows", pairs)


def pack_kernel(first, count, split, *refs):
    wanted_ref, sources, outs = refs[0], refs[1 : 1 + count + split], refs[-NY:]
    width, block = outs[0].shape[2], outs[0].shape[3]
    for ys in range(NY):
        for cs in range(NC):
            for q in range(count * CAP):
                w = wanted_ref[(ys * NC + cs) * PER + first * CAP + q]
                where = lanes(jnp.maximum(w, 0), block)
                j = q // CAP
                if split and j == count - 1:
                    outs[ys][cs, q, : width // 2] = sources[j][:, where]
                    outs[ys][cs, q, width // 2 :] = sources[j + 1][:, where]
                else:
                    outs[ys][cs, q] = sources[j][:, where]


def pack(group, wanted, sources, block, after):
    first, last = group
    count = last - first
    width = sources[0].shape[0]
    shape = jax.ShapeDtypeStruct((NC, count * CAP, width, block), BF)
    return pl.pallas_call(
        functools.partial(pack_kernel, first, count, len(sources) > count),
        out_shape=[shape] * NY,
        in_specs=[SMEM] + [VMEM] * len(sources) + [ANY] * len(after),
        out_specs=[VMEM] * NY,
        name="pack",
        cost_estimate=pl.CostEstimate(flops=0, bytes_accessed=3 << 20, transcendentals=0),
    )(wanted, *sources, *after)


def dot(a, b, dims):
    return lax.dot_general(a, b, ((dims[:1], dims[1:]), ((), ())), preferred_element_type=F32)


STEP = 4


def agg_local_kernel(cols_ref, feats_ref, tiles_ref, out_ref):
    i = pl.program_id(0)
    count, block = tiles_ref.shape[1], tiles_ref.shape[2]
    for rr in range(STEP):
        acc = None
        for t in range(0, count, 2):
            base = (i * STEP + rr) * count + t
            lhs = jnp.concatenate(
                [feats_ref[:, lanes(cols_ref[base + k], block)] for k in range(2)], axis=1
            )
            rhs = jnp.concatenate([tiles_ref[rr, t + k] for k in range(2)], axis=1)
            term = dot(lhs, rhs, (1, 1))
            acc = term if acc is None else acc + term
        out_ref[:, rr * block : (rr + 1) * block] = acc


def agg_local(cols, feats, tiles):
    row_blocks, _, block, _ = tiles.shape
    width = feats.shape[0]
    return pl.pallas_call(
        agg_local_kernel,
        grid=(row_blocks // STEP,),
        out_shape=jax.ShapeDtypeStruct((width, row_blocks * block), F32),
        in_specs=[
            SMEM,
            pl.BlockSpec(feats.shape, lambda i: (0, 0)),
            pl.BlockSpec((STEP, TL, block, block), lambda i: (i, 0, 0, 0)),
        ],
        out_specs=pl.BlockSpec((width, STEP * block), lambda i: (0, i)),
        name="agg_local",
        cost_estimate=pl.CostEstimate(
            flops=2 * width * row_blocks * TL * block * block, bytes_accessed=3 << 20, transcendentals=0
        ),
    )(cols, feats, tiles)


def agg_remote_kernel(slots_ref, tiles_ref, local_ref, *refs):
    parts, out_ref, recv_ref = refs[:-2], refs[-2], refs[-1]
    i = pl.program_id(0)
    count, block = tiles_ref.shape[1], tiles_ref.shape[2]

    @pl.when(i == 0)
    def _():
        n = 0
        for first, last in GROUPS:
            size = (last - first) * CAP
            for ys in range(NY):
                recv_ref[pl.ds(ys * PER + first * CAP, size)] = parts[n + ys][0]
                recv_ref[pl.ds((NY + ys) * PER + first * CAP, size)] = parts[n + NY][ys]
            n += NY + 1

    for rr in range(STEP):
        acc = local_ref[:, rr * block : (rr + 1) * block]
        for t in range(0, count, 2):
            base = (i * STEP + rr) * count + t
            lhs = jnp.concatenate([recv_ref[slots_ref[base + k]] for k in range(2)], axis=1)
            rhs = jnp.concatenate([tiles_ref[rr, t + k] for k in range(2)], axis=1)
            acc = acc + dot(lhs, rhs, (1, 1))
        out_ref[:, rr * block : (rr + 1) * block] = acc.astype(out_ref.dtype)


def agg_remote(slots, parts, tiles, local):
    row_blocks, per_block, block, _ = tiles.shape
    rem = per_block - TL
    width = local.shape[0]
    specs = []
    for n, part in enumerate(parts):
        lead = 1 if n % (NY + 1) < NY else NY
        specs.append(pl.BlockSpec((lead,) + part.shape[1:], lambda i: (0, 0, 0, 0)))
    return pl.pallas_call(
        agg_remote_kernel,
        grid=(row_blocks // STEP,),
        out_shape=jax.ShapeDtypeStruct(local.shape, BF),
        in_specs=[
            SMEM,
            pl.BlockSpec((STEP, rem, block, block), lambda i: (i, 1, 0, 0)),
            pl.BlockSpec((width, STEP * block), lambda i: (0, i)),
        ]
        + specs,
        out_specs=pl.BlockSpec((width, STEP * block), lambda i: (0, i)),
        scratch_shapes=[pltpu.VMEM((NY * NC * PER, width, block), BF)],
        name="agg_remote",
        cost_estimate=pl.CostEstimate(
            flops=2 * width * row_blocks * rem * block * block, bytes_accessed=5 << 20, transcendentals=0
        ),
    )(slots, tiles, local, *parts)


def mid_kernel(
    me_ref,
    own_ref,
    low_ref,
    high_ref,
    far_ref,
    cot_ref,
    w_ref,
    bias_ref,
    wown_ref,
    hid_ref,
    g_ref,
    gw_ref,
    gb_ref,
    agg_scr,
    hid_scr,
    wt_scr,
    gb_scr,
):
    i = pl.program_id(0)
    width = own_ref.shape[0]
    count = agg_scr.shape[0] // width
    me = me_ref[0]

    def rows(ahead):
        return pl.ds(pl.multiple_of(lax.rem(me + ahead, count) * width, width), width)

    @pl.when(i == 0)
    def _():
        wt_scr[...] = w_ref[...].astype(F32).T.astype(BF)
        gw_ref[...] = jnp.zeros_like(gw_ref)
        gb_scr[...] = jnp.zeros_like(gb_scr)

    agg_scr[rows(3)] = low_ref[...]
    agg_scr[rows(1)] = high_ref[...]
    agg_scr[rows(2)] = far_ref[...]
    agg_scr[rows(0)] = own_ref[...]
    pre = dot(wt_scr[...], agg_scr[...], (1, 0))
    bias = bias_ref[:, :3].astype(F32)
    pre = pre + ((bias[:, 2:3] + bias[:, 1:2]) + bias[:, 0:1])
    sigma = jax.nn.sigmoid(pre)
    hid_scr[...] = (pre * sigma).astype(BF)
    hid_ref[...] = hid_scr[rows(0)]
    grad_pre = cot_ref[...].astype(F32) * (sigma * (1.0 + pre * (1.0 - sigma)))
    total = grad_pre[:, :128]
    for k in range(1, grad_pre.shape[1] // 128):
        total = total + grad_pre[:, k * 128 : (k + 1) * 128]
    gb_scr[...] += total
    grad_b = grad_pre.astype(BF)
    g_ref[...] = dot(wown_ref[...], grad_b, (1, 0)).astype(BF)
    gw_ref[...] += dot(own_ref[...], grad_b, (1, 1))

    @pl.when(i == pl.num_programs(0) - 1)
    def _():
        gb_ref[...] = gb_scr[rows(0)]


def mid(me, pieces, packed, w_own):
    own, low, high, far = pieces
    width, nodes = own.shape
    hid_all = packed.shape[0]
    chunk = 512
    col = lambda i: (0, i)
    return pl.pallas_call(
        mid_kernel,
        grid=(nodes // chunk,),
        out_shape=(
            jax.ShapeDtypeStruct((width, nodes), BF),
            jax.ShapeDtypeStruct((width, nodes), BF),
            jax.ShapeDtypeStruct((width, hid_all), F32),
            jax.ShapeDtypeStruct((width, 128), F32),
        ),
        in_specs=[
            SMEM,
            pl.BlockSpec((width, chunk), col),
            pl.BlockSpec((width, chunk), col),
            pl.BlockSpec((width, chunk), col),
            pl.BlockSpec((width, chunk), col),
            pl.BlockSpec((hid_all, chunk), col),
            pl.BlockSpec((hid_all, hid_all), lambda i: (0, nodes // hid_all)),
            pl.BlockSpec((hid_all, 128), lambda i: (0, (nodes + hid_all) // 128)),
            pl.BlockSpec((width, hid_all), lambda i: (0, 0)),
        ],
        out_specs=(
            pl.BlockSpec((width, chunk), col),
            pl.BlockSpec((width, chunk), col),
            pl.BlockSpec((width, hid_all), lambda i: (0, 0)),
            pl.BlockSpec((width, 128), lambda i: (0, 0)),
        ),
        scratch_shapes=[
            pltpu.VMEM((hid_all, chunk), BF),
            pltpu.VMEM((hid_all, chunk), BF),
            pltpu.VMEM((hid_all, hid_all), BF),
            pltpu.VMEM((hid_all, 128), F32),
        ],
        name="mid",
        cost_estimate=pl.CostEstimate(
            flops=2 * nodes * hid_all * (hid_all + 2 * width),
            bytes_accessed=3 << 20,
            transcendentals=nodes * hid_all,
        ),
    )(me, own, low, high, far, packed, packed, packed, w_own)


def back_remote_kernel(slots_ref, g_ref, tiles_ref, out_ref):
    i = pl.program_id(0)
    width = g_ref.shape[0]
    count, block = tiles_ref.shape[1], tiles_ref.shape[2]

    @pl.when(i == 0)
    def _():
        out_ref[...] = jnp.zeros_like(out_ref)

    for rr in range(STEP):
        lhs = g_ref[:, rr * block : (rr + 1) * block]
        for t in range(0, count, 2):
            base = (i * STEP + rr) * count + t
            rhs = jnp.concatenate([tiles_ref[rr, t + k] for k in range(2)], axis=1)
            term = dot(lhs, rhs, (1, 0)).astype(BF)
            for k in range(2):
                slot = slots_ref[base + k]
                row = pl.multiple_of((slot % CAP) * width, width)
                out_ref[slot // CAP, pl.ds(row, width)] = term[:, k * block : (k + 1) * block]


def back_remote(slots, g, tiles, peers, extra):
    row_blocks, per_block, block, _ = tiles.shape
    rem = per_block - TL
    width = g.shape[0]
    return pl.pallas_call(
        back_remote_kernel,
        grid=(row_blocks // STEP,),
        out_shape=jax.ShapeDtypeStruct((peers, CAP * width + extra, block), BF),
        in_specs=[
            SMEM,
            pl.BlockSpec((width, STEP * block), lambda i: (0, i)),
            pl.BlockSpec((STEP, rem, block, block), lambda i: (i, 1, 0, 0)),
        ],
        out_specs=pl.BlockSpec((peers, CAP * width + extra, block), lambda i: (0, 0, 0)),
        name="back_remote",
        cost_estimate=pl.CostEstimate(
            flops=2 * width * row_blocks * rem * block * block, bytes_accessed=5 << 20, transcendentals=0
        ),
    )(slots, g, tiles)


def back_local_kernel(cols_ref, g_ref, tiles_ref, out_ref):
    i = pl.program_id(0)
    count, block = tiles_ref.shape[1], tiles_ref.shape[2]

    @pl.when(i == 0)
    def _():
        out_ref[...] = jnp.zeros_like(out_ref)

    for rr in range(STEP):
        lhs = g_ref[:, rr * block : (rr + 1) * block]
        for t in range(0, count, 2):
            base = (i * STEP + rr) * count + t
            rhs = jnp.concatenate([tiles_ref[rr, t + k] for k in range(2)], axis=1)
            term = dot(lhs, rhs, (1, 0))
            for k in range(2):
                out_ref[:, lanes(cols_ref[base + k], block)] += term[:, k * block : (k + 1) * block]


def back_local(cols, g, tiles):
    row_blocks, _, block, _ = tiles.shape
    width = g.shape[0]
    return pl.pallas_call(
        back_local_kernel,
        grid=(row_blocks // STEP,),
        out_shape=jax.ShapeDtypeStruct(g.shape, F32),
        in_specs=[
            SMEM,
            pl.BlockSpec((width, STEP * block), lambda i: (0, i)),
            pl.BlockSpec((STEP, TL, block, block), lambda i: (i, 0, 0, 0)),
        ],
        out_specs=pl.BlockSpec(g.shape, lambda i: (0, 0)),
        name="back_local",
        cost_estimate=pl.CostEstimate(
            flops=2 * width * row_blocks * TL * block * block, bytes_accessed=3 << 20, transcendentals=0
        ),
    )(cols, g, tiles)


def finish_kernel(wanted_ref, recv_ref, local_ref, out_ref, odd_scr):
    width, block = out_ref.shape[0], recv_ref.shape[2]
    out_ref[...] = local_ref[...]
    odd_scr[...] = jnp.zeros_like(odd_scr)

    def body(p, carry):
        even = lanes(jnp.maximum(wanted_ref[p * CAP], 0), block)
        odd = lanes(jnp.maximum(wanted_ref[p * CAP + 1], 0), block)
        out_ref[:, even] += recv_ref[p, :width].astype(F32)
        odd_scr[:, odd] += recv_ref[p, width : 2 * width].astype(F32)
        return carry

    lax.fori_loop(0, recv_ref.shape[0], body, 0, unroll=4)
    out_ref[...] += odd_scr[...]


def finish(wanted, recv, local):
    return pl.pallas_call(
        finish_kernel,
        out_shape=jax.ShapeDtypeStruct(local.shape, F32),
        in_specs=[SMEM, VMEM, VMEM],
        out_specs=VMEM,
        scratch_shapes=[pltpu.VMEM(local.shape, F32)],
        name="finish",
        cost_estimate=pl.CostEstimate(flops=recv.size, bytes_accessed=4 << 20, transcendentals=0),
    )(wanted, recv, local)


def split_bf16(x, terms):
    parts = []
    for _ in range(terms):
        part = lax.reduce_precision(x, 8, 7)
        parts.append(part.astype(BF))
        x = x - part
    return parts


def local(feats, weight, bias, tile_cols, tile_values, cotangent):
    width, nodes_dev = feats.shape
    hid_all = weight.shape[1]
    block = tile_values.shape[1]
    row_blocks = nodes_dev // block
    peers = lax.axis_size("rows")
    fpeers = lax.axis_size("feat")
    per_block = tile_cols.shape[0] // row_blocks
    remote_count = row_blocks * (per_block - TL)
    place = lax.axis_index("rows")
    y, z, c = place // (NZ * NC), place // NC % NZ, place % NC

    grid = tile_cols.reshape(row_blocks, per_block)
    tiles = tile_values.reshape(row_blocks, per_block, block, block)
    local_cols = (grid[:, :TL] % row_blocks).reshape(-1)
    remote_cols = grid[:, TL:].reshape(-1)
    owner = remote_cols // row_blocks
    inside = remote_cols % row_blocks
    order = jnp.arange(remote_count)
    earlier = (owner[:, None] == owner[None, :]) & (order[None, :] < order[:, None])
    rank = jnp.sum(earlier.astype(jnp.int32), axis=1)
    slots = owner * CAP + rank
    ahead = (owner // NC - z) & (NZ - 1)
    pos = jnp.maximum(jnp.where(ahead <= NZ // 2, 2 * ahead - 1, 2 * (NZ - ahead)), 0)
    back = (y - owner // (NZ * NC)) & (NY - 1)
    other = (owner ^ c) & 1
    near = ((other * NY + back) * NZ + pos) * CAP + rank

    def table(index):
        hit = index[None, :] == jnp.arange(peers * CAP)[:, None]
        return jnp.max(jnp.where(hit, inside[None, :], -1), axis=1)

    asked = table(near).reshape(NC, NY, PER)
    asked = jnp.stack([asked[0], shift(asked[1], dc=1)], axis=1)
    wanted = [asked[0]] + [shift(asked[ys], dy=-ys) for ys in range(1, NY)]
    wanted = jnp.stack(wanted).reshape(-1)

    up, down, parts = [feats], [feats], []
    for k in range(1, NZ // 2):
        up.append(shift(up[-1], dz=1))
        down.append(shift(down[-1], dz=-1))
    far_up = shift(up[-1][: width // 2], dz=1)
    far_down = shift(down[-1][width // 2 :], dz=-1)
    groups = ((feats, down[1], up[1]), (down[2], up[2]), (down[3], up[3], far_up, far_down))
    after = []
    agg = agg_local(local_cols, feats, tiles)
    for group, sources in zip(GROUPS, groups):
        packs = pack(group, wanted, sources, block, after)
        after = [packs[0], agg]
        moved = [packs[0]] + [shift(packs[ys], dy=ys) for ys in range(1, NY)]
        parts += moved
        parts.append(shift(jnp.concatenate([m[1:] for m in moved]), dc=1))

    bias_cols = jnp.pad(jnp.stack(split_bf16(bias, 3), axis=1), ((0, 0), (0, 125)))
    packed = jnp.concatenate([cotangent, weight, bias_cols], axis=1)
    packed = lax.all_gather(packed, "feat", axis=0, tiled=True)

    agg = agg_remote(near, parts, tiles, agg)

    pieces = [agg] + [
        lax.ppermute(agg, "feat", [(k, (k + s) % fpeers) for k in range(fpeers)]) for s in (1, 3, 2)
    ]
    me = lax.axis_index("feat").astype(jnp.int32).reshape(1)
    hidden_out, g, grad_w, grad_b = mid(me, pieces, packed, weight)

    divisor = math.sqrt(nodes_dev * peers)
    per = grad_w.size // peers
    per_b = width // peers
    sums = jnp.concatenate(
        [
            grad_w.reshape(peers, per),
            jnp.sum(grad_b, axis=1).reshape(peers, per_b),
            table(slots).reshape(peers, CAP).astype(F32),
        ],
        axis=1,
    )
    sums = lax.all_to_all(sums, "rows", split_axis=0, concat_axis=0, tiled=True)
    holders = sums[:, per + per_b :].astype(jnp.int32).reshape(-1)
    total = jnp.sum(sums[:, : per + per_b], axis=0) / divisor
    span = -(-total.size // block)
    total = jnp.pad(total, (0, span * block - total.size)).reshape(span, block)
    extra = -(-2 * span // 8) * 8
    rider = jnp.concatenate(split_bf16(total, 2) + [jnp.zeros((extra - 2 * span, block), BF)])

    send = back_remote(slots, g, tiles, peers, extra)
    send = send.at[:, CAP * width :].set(jnp.broadcast_to(rider, (peers, extra, block)))
    recv = lax.all_to_all(send, "rows", split_axis=0, concat_axis=0, tiled=True)
    own = back_local(local_cols, g, tiles)
    grad_input = finish(holders, recv, own)
    totals = recv[:, CAP * width :].astype(F32)
    totals = (totals[:, :span] + totals[:, span : 2 * span]).reshape(peers, -1)
    return (
        hidden_out,
        grad_input,
        totals[:, :per].reshape(width, hid_all),
        totals[:, per : per + per_b].reshape(width),
    )


def solution(mesh):
    placed = (
        P("feat", "rows"),
        P("feat", None),
        P("feat"),
        P("rows"),
        P("rows", None, None),
        P("feat", "rows"),
    )
    return jax.shard_map(
        local,
        mesh=mesh,
        in_specs=placed,
        out_specs=(P("feat", "rows"), P("feat", "rows"), P("feat", None), P("feat")),
        check_vma=False,
    )
```

```python
import functools
import math

import jax
import jax.numpy as jnp
from jax import lax
from jax.experimental import pallas as pl
from jax.experimental.pallas import tpu as pltpu
from jax.sharding import PartitionSpec as P

TL = 4
BF = jnp.bfloat16
F32 = jnp.float32
VMEM = pl.BlockSpec(memory_space=pltpu.VMEM)
ANY = pl.BlockSpec(memory_space=pl.ANY)
SMEM = pl.BlockSpec(memory_space=pltpu.SMEM)


def lanes(index, width):
    return pl.ds(pl.multiple_of(index * width, width), width)


NY, NZ, NC = 4, 8, 2
CAP = 2
ORDER = (0, 1, 7, 2, 6, 3, 5, 4)
GROUPS = ((0, 5), (5, 8))
PEERS = NY * NC
PER = NZ * CAP


def shift(x, dz):
    pairs = []
    for y in range(NY):
        for z in range(NZ):
            for c in range(NC):
                pairs.append(((y * NZ + z) * NC + c, (y * NZ + (z + dz) % NZ) * NC + c))
    return lax.ppermute(x, "rows", pairs)


def swap(x):
    groups = [[(y * NZ + z) * NC + c for y in range(NY) for c in range(NC)] for z in range(NZ)]
    return lax.all_to_all(
        x, "rows", split_axis=0, concat_axis=0, tiled=True, axis_index_groups=groups
    )


def pack_kernel(first, count, split, *refs):
    wanted_ref, sources, out_ref = refs[0], refs[1 : 1 + count + split], refs[-1]
    width, block = out_ref.shape[2], out_ref.shape[3]
    for p in range(PEERS):
        for q in range(count * CAP):
            w = wanted_ref[p * PER + first * CAP + q]
            where = lanes(jnp.maximum(w, 0), block)
            j = q // CAP
            if split and j == count - 1:
                out_ref[p, q, : width // 2] = sources[j][:, where]
                out_ref[p, q, width // 2 :] = sources[j + 1][:, where]
            else:
                out_ref[p, q] = sources[j][:, where]


def pack(group, wanted, sources, block, after):
    first, last = group
    count = last - first
    width = sources[0].shape[0]
    return pl.pallas_call(
        functools.partial(pack_kernel, first, count, len(sources) > count),
        out_shape=jax.ShapeDtypeStruct((PEERS, count * CAP, width, block), BF),
        in_specs=[SMEM] + [VMEM] * len(sources) + [ANY] * len(after),
        out_specs=VMEM,
        name="pack",
        cost_estimate=pl.CostEstimate(flops=0, bytes_accessed=3 << 20, transcendentals=0),
    )(wanted, *sources, *after)


def dot(a, b, dims):
    return lax.dot_general(a, b, ((dims[:1], dims[1:]), ((), ())), preferred_element_type=F32)


STEP = 4


def agg_local_kernel(cols_ref, feats_ref, tiles_ref, out_ref):
    i = pl.program_id(0)
    count, block = tiles_ref.shape[1], tiles_ref.shape[2]
    for rr in range(STEP):
        acc = None
        for t in range(0, count, 2):
            base = (i * STEP + rr) * count + t
            lhs = jnp.concatenate(
                [feats_ref[:, lanes(cols_ref[base + k], block)] for k in range(2)], axis=1
            )
            rhs = jnp.concatenate([tiles_ref[rr, t + k] for k in range(2)], axis=1)
            term = dot(lhs, rhs, (1, 1))
            acc = term if acc is None else acc + term
        out_ref[:, rr * block : (rr + 1) * block] = acc


def agg_local(cols, feats, tiles):
    row_blocks, _, block, _ = tiles.shape
    width = feats.shape[0]
    return pl.pallas_call(
        agg_local_kernel,
        grid=(row_blocks // STEP,),
        out_shape=jax.ShapeDtypeStruct((width, row_blocks * block), F32),
        in_specs=[
            SMEM,
            pl.BlockSpec(feats.shape, lambda i: (0, 0)),
            pl.BlockSpec((STEP, TL, block, block), lambda i: (i, 0, 0, 0)),
        ],
        out_specs=pl.BlockSpec((width, STEP * block), lambda i: (0, i)),
        name="agg_local",
        cost_estimate=pl.CostEstimate(
            flops=2 * width * row_blocks * TL * block * block, bytes_accessed=3 << 20, transcendentals=0
        ),
    )(cols, feats, tiles)


def agg_remote_kernel(slots_ref, tiles_ref, local_ref, *refs):
    parts, out_ref, recv_ref = refs[:-2], refs[-2], refs[-1]
    i = pl.program_id(0)
    count, block = tiles_ref.shape[1], tiles_ref.shape[2]

    @pl.when(i == 0)
    def _():
        for part, (first, last) in zip(parts, GROUPS):
            for p in range(PEERS):
                recv_ref[pl.ds(p * PER + first * CAP, (last - first) * CAP)] = part[p]

    for rr in range(STEP):
        acc = local_ref[:, rr * block : (rr + 1) * block]
        for t in range(0, count, 2):
            base = (i * STEP + rr) * count + t
            lhs = jnp.concatenate([recv_ref[slots_ref[base + k]] for k in range(2)], axis=1)
            rhs = jnp.concatenate([tiles_ref[rr, t + k] for k in range(2)], axis=1)
            acc = acc + dot(lhs, rhs, (1, 1))
        out_ref[:, rr * block : (rr + 1) * block] = acc.astype(out_ref.dtype)


def agg_remote(slots, parts, tiles, local):
    row_blocks, per_block, block, _ = tiles.shape
    rem = per_block - TL
    width = local.shape[0]
    specs = [pl.BlockSpec(part.shape, lambda i: (0, 0, 0, 0)) for part in parts]
    return pl.pallas_call(
        agg_remote_kernel,
        grid=(row_blocks // STEP,),
        out_shape=jax.ShapeDtypeStruct(local.shape, BF),
        in_specs=[
            SMEM,
            pl.BlockSpec((STEP, rem, block, block), lambda i: (i, 1, 0, 0)),
            pl.BlockSpec((width, STEP * block), lambda i: (0, i)),
        ]
        + specs,
        out_specs=pl.BlockSpec((width, STEP * block), lambda i: (0, i)),
        scratch_shapes=[pltpu.VMEM((PEERS * PER, width, block), BF)],
        name="agg_remote",
        cost_estimate=pl.CostEstimate(
            flops=2 * width * row_blocks * rem * block * block, bytes_accessed=5 << 20, transcendentals=0
        ),
    )(slots, tiles, local, *parts)


def mid_kernel(
    me_ref,
    own_ref,
    low_ref,
    high_ref,
    far_ref,
    cot_ref,
    w_ref,
    bias_ref,
    wown_ref,
    hid_ref,
    g_ref,
    gw_ref,
    gb_ref,
    agg_scr,
    hid_scr,
    wt_scr,
    gb_scr,
):
    i = pl.program_id(0)
    width = own_ref.shape[0]
    count = agg_scr.shape[0] // width
    me = me_ref[0]

    def rows(ahead):
        return pl.ds(pl.multiple_of(lax.rem(me + ahead, count) * width, width), width)

    @pl.when(i == 0)
    def _():
        wt_scr[...] = w_ref[...].astype(F32).T.astype(BF)
        gw_ref[...] = jnp.zeros_like(gw_ref)
        gb_scr[...] = jnp.zeros_like(gb_scr)

    agg_scr[rows(3)] = low_ref[...]
    agg_scr[rows(1)] = high_ref[...]
    agg_scr[rows(2)] = far_ref[...]
    agg_scr[rows(0)] = own_ref[...]
    pre = dot(wt_scr[...], agg_scr[...], (1, 0))
    bias = bias_ref[:, :3].astype(F32)
    pre = pre + ((bias[:, 2:3] + bias[:, 1:2]) + bias[:, 0:1])
    sigma = jax.nn.sigmoid(pre)
    hid_scr[...] = (pre * sigma).astype(BF)
    hid_ref[...] = hid_scr[rows(0)]
    grad_pre = cot_ref[...].astype(F32) * (sigma * (1.0 + pre * (1.0 - sigma)))
    total = grad_pre[:, :128]
    for k in range(1, grad_pre.shape[1] // 128):
        total = total + grad_pre[:, k * 128 : (k + 1) * 128]
    gb_scr[...] += total
    grad_b = grad_pre.astype(BF)
    g_ref[...] = dot(wown_ref[...], grad_b, (1, 0)).astype(BF)
    gw_ref[...] += dot(own_ref[...], grad_b, (1, 1))

    @pl.when(i == pl.num_programs(0) - 1)
    def _():
        gb_ref[...] = gb_scr[rows(0)]


def mid(me, pieces, packed, w_own):
    own, low, high, far = pieces
    width, nodes = own.shape
    hid_all = packed.shape[0]
    chunk = 512
    col = lambda i: (0, i)
    return pl.pallas_call(
        mid_kernel,
        grid=(nodes // chunk,),
        out_shape=(
            jax.ShapeDtypeStruct((width, nodes), BF),
            jax.ShapeDtypeStruct((width, nodes), BF),
            jax.ShapeDtypeStruct((width, hid_all), F32),
            jax.ShapeDtypeStruct((width, 128), F32),
        ),
        in_specs=[
            SMEM,
            pl.BlockSpec((width, chunk), col),
            pl.BlockSpec((width, chunk), col),
            pl.BlockSpec((width, chunk), col),
            pl.BlockSpec((width, chunk), col),
            pl.BlockSpec((hid_all, chunk), col),
            pl.BlockSpec((hid_all, hid_all), lambda i: (0, nodes // hid_all)),
            pl.BlockSpec((hid_all, 128), lambda i: (0, (nodes + hid_all) // 128)),
            pl.BlockSpec((width, hid_all), lambda i: (0, 0)),
        ],
        out_specs=(
            pl.BlockSpec((width, chunk), col),
            pl.BlockSpec((width, chunk), col),
            pl.BlockSpec((width, hid_all), lambda i: (0, 0)),
            pl.BlockSpec((width, 128), lambda i: (0, 0)),
        ),
        scratch_shapes=[
            pltpu.VMEM((hid_all, chunk), BF),
            pltpu.VMEM((hid_all, chunk), BF),
            pltpu.VMEM((hid_all, hid_all), BF),
            pltpu.VMEM((hid_all, 128), F32),
        ],
        name="mid",
        cost_estimate=pl.CostEstimate(
            flops=2 * nodes * hid_all * (hid_all + 2 * width),
            bytes_accessed=3 << 20,
            transcendentals=nodes * hid_all,
        ),
    )(me, own, low, high, far, packed, packed, packed, w_own)


def back_remote_kernel(slots_ref, g_ref, tiles_ref, out_ref):
    i = pl.program_id(0)
    width = g_ref.shape[0]
    count, block = tiles_ref.shape[1], tiles_ref.shape[2]

    @pl.when(i == 0)
    def _():
        out_ref[...] = jnp.zeros_like(out_ref)

    for rr in range(STEP):
        lhs = g_ref[:, rr * block : (rr + 1) * block]
        for t in range(0, count, 2):
            base = (i * STEP + rr) * count + t
            rhs = jnp.concatenate([tiles_ref[rr, t + k] for k in range(2)], axis=1)
            term = dot(lhs, rhs, (1, 0)).astype(BF)
            for k in range(2):
                slot = slots_ref[base + k]
                row = pl.multiple_of((slot % CAP) * width, width)
                out_ref[slot // CAP, pl.ds(row, width)] = term[:, k * block : (k + 1) * block]


def back_remote(slots, g, tiles, peers, extra):
    row_blocks, per_block, block, _ = tiles.shape
    rem = per_block - TL
    width = g.shape[0]
    return pl.pallas_call(
        back_remote_kernel,
        grid=(row_blocks // STEP,),
        out_shape=jax.ShapeDtypeStruct((peers, CAP * width + extra, block), BF),
        in_specs=[
            SMEM,
            pl.BlockSpec((width, STEP * block), lambda i: (0, i)),
            pl.BlockSpec((STEP, rem, block, block), lambda i: (i, 1, 0, 0)),
        ],
        out_specs=pl.BlockSpec((peers, CAP * width + extra, block), lambda i: (0, 0, 0)),
        name="back_remote",
        cost_estimate=pl.CostEstimate(
            flops=2 * width * row_blocks * rem * block * block, bytes_accessed=5 << 20, transcendentals=0
        ),
    )(slots, g, tiles)


def back_local_kernel(cols_ref, g_ref, tiles_ref, out_ref):
    i = pl.program_id(0)
    count, block = tiles_ref.shape[1], tiles_ref.shape[2]

    @pl.when(i == 0)
    def _():
        out_ref[...] = jnp.zeros_like(out_ref)

    for rr in range(STEP):
        lhs = g_ref[:, rr * block : (rr + 1) * block]
        for t in range(0, count, 2):
            base = (i * STEP + rr) * count + t
            rhs = jnp.concatenate([tiles_ref[rr, t + k] for k in range(2)], axis=1)
            term = dot(lhs, rhs, (1, 0))
            for k in range(2):
                out_ref[:, lanes(cols_ref[base + k], block)] += term[:, k * block : (k + 1) * block]


def back_local(cols, g, tiles):
    row_blocks, _, block, _ = tiles.shape
    width = g.shape[0]
    return pl.pallas_call(
        back_local_kernel,
        grid=(row_blocks // STEP,),
        out_shape=jax.ShapeDtypeStruct(g.shape, F32),
        in_specs=[
            SMEM,
            pl.BlockSpec((width, STEP * block), lambda i: (0, i)),
            pl.BlockSpec((STEP, TL, block, block), lambda i: (i, 0, 0, 0)),
        ],
        out_specs=pl.BlockSpec(g.shape, lambda i: (0, 0)),
        name="back_local",
        cost_estimate=pl.CostEstimate(
            flops=2 * width * row_blocks * TL * block * block, bytes_accessed=3 << 20, transcendentals=0
        ),
    )(cols, g, tiles)


def finish_kernel(wanted_ref, recv_ref, local_ref, out_ref, odd_scr):
    width, block = out_ref.shape[0], recv_ref.shape[2]
    out_ref[...] = local_ref[...]
    odd_scr[...] = jnp.zeros_like(odd_scr)

    def body(p, carry):
        even = lanes(jnp.maximum(wanted_ref[p * CAP], 0), block)
        odd = lanes(jnp.maximum(wanted_ref[p * CAP + 1], 0), block)
        out_ref[:, even] += recv_ref[p, :width].astype(F32)
        odd_scr[:, odd] += recv_ref[p, width : 2 * width].astype(F32)
        return carry

    lax.fori_loop(0, recv_ref.shape[0], body, 0, unroll=4)
    out_ref[...] += odd_scr[...]


def finish(wanted, recv, local):
    return pl.pallas_call(
        finish_kernel,
        out_shape=jax.ShapeDtypeStruct(local.shape, F32),
        in_specs=[SMEM, VMEM, VMEM],
        out_specs=VMEM,
        scratch_shapes=[pltpu.VMEM(local.shape, F32)],
        name="finish",
        cost_estimate=pl.CostEstimate(flops=recv.size, bytes_accessed=4 << 20, transcendentals=0),
    )(wanted, recv, local)


def split_bf16(x, terms):
    parts = []
    for _ in range(terms):
        part = lax.reduce_precision(x, 8, 7)
        parts.append(part.astype(BF))
        x = x - part
    return parts


def local(feats, weight, bias, tile_cols, tile_values, cotangent):
    width, nodes_dev = feats.shape
    hid_all = weight.shape[1]
    block = tile_values.shape[1]
    row_blocks = nodes_dev // block
    peers = lax.axis_size("rows")
    fpeers = lax.axis_size("feat")
    per_block = tile_cols.shape[0] // row_blocks
    remote_count = row_blocks * (per_block - TL)
    place = lax.axis_index("rows")
    z = place // NC % NZ

    grid = tile_cols.reshape(row_blocks, per_block)
    tiles = tile_values.reshape(row_blocks, per_block, block, block)
    local_cols = (grid[:, :TL] % row_blocks).reshape(-1)
    remote_cols = grid[:, TL:].reshape(-1)
    owner = remote_cols // row_blocks
    inside = remote_cols % row_blocks
    order = jnp.arange(remote_count)
    earlier = (owner[:, None] == owner[None, :]) & (order[None, :] < order[:, None])
    rank = jnp.sum(earlier.astype(jnp.int32), axis=1)
    slots = owner * CAP + rank
    ahead = (owner // NC - z) & (NZ - 1)
    pos = jnp.maximum(jnp.where(ahead <= NZ // 2, 2 * ahead - 1, 2 * (NZ - ahead)), 0)
    near = ((owner // (NZ * NC) * NC + owner % NC) * NZ + pos) * CAP + rank

    def table(index):
        hit = index[None, :] == jnp.arange(peers * CAP)[:, None]
        return jnp.max(jnp.where(hit, inside[None, :], -1), axis=1)

    wanted = swap(table(near).reshape(PEERS, PER)).reshape(-1)

    up, down = [feats], [feats]
    for k in range(1, NZ // 2):
        if k == 3:
            up[2], down[2], wanted = lax.optimization_barrier((up[2], down[2], wanted))
        up.append(shift(up[-1], 1))
        down.append(shift(down[-1], -1))
    far_up = shift(up[-1][: width // 2], 1)
    far_down = shift(down[-1][width // 2 :], -1)

    bias_cols = jnp.pad(jnp.stack(split_bf16(bias, 3), axis=1), ((0, 0), (0, 125)))
    packed = jnp.concatenate([cotangent, weight, bias_cols], axis=1)
    packed = lax.all_gather(packed, "feat", axis=0, tiled=True)

    agg = agg_local(local_cols, feats, tiles)
    near_sources = (feats, down[1], up[1], down[2], up[2])
    far_sources = (down[3], up[3], far_up, far_down)
    first = swap(pack(GROUPS[0], wanted, near_sources, block, []))
    second = swap(pack(GROUPS[1], wanted, far_sources, block, [first, agg, packed]))
    parts = [first, second]

    agg = agg_remote(near, parts, tiles, agg)

    pieces = [agg] + [
        lax.ppermute(agg, "feat", [(k, (k + s) % fpeers) for k in range(fpeers)]) for s in (1, 3, 2)
    ]
    me = lax.axis_index("feat").astype(jnp.int32).reshape(1)
    hidden_out, g, grad_w, grad_b = mid(me, pieces, packed, weight)

    divisor = math.sqrt(nodes_dev * peers)
    per = grad_w.size // peers
    per_b = width // peers
    sums = jnp.concatenate(
        [
            grad_w.reshape(peers, per),
            jnp.sum(grad_b, axis=1).reshape(peers, per_b),
            table(slots).reshape(peers, CAP).astype(F32),
        ],
        axis=1,
    )
    sums = lax.all_to_all(sums, "rows", split_axis=0, concat_axis=0, tiled=True)
    holders = sums[:, per + per_b :].astype(jnp.int32).reshape(-1)
    total = jnp.sum(sums[:, : per + per_b], axis=0) / divisor
    span = -(-total.size // block)
    total = jnp.pad(total, (0, span * block - total.size)).reshape(span, block)
    extra = -(-2 * span // 8) * 8
    rider = jnp.concatenate(split_bf16(total, 2) + [jnp.zeros((extra - 2 * span, block), BF)])

    send = back_remote(slots, g, tiles, peers, extra)
    own = back_local(local_cols, g, tiles)
    own, rider = lax.optimization_barrier((own, rider))
    send = send.at[:, CAP * width :].set(jnp.broadcast_to(rider, (peers, extra, block)))
    recv = lax.all_to_all(send, "rows", split_axis=0, concat_axis=0, tiled=True)
    grad_input = finish(holders, recv, own)
    totals = recv[:, CAP * width :].astype(F32)
    totals = (totals[:, :span] + totals[:, span : 2 * span]).reshape(peers, -1)
    return (
        hidden_out,
        grad_input,
        totals[:, :per].reshape(width, hid_all),
        totals[:, per : per + per_b].reshape(width),
    )


def solution(mesh):
    placed = (
        P("feat", "rows"),
        P("feat", None),
        P("feat"),
        P("rows"),
        P("rows", None, None),
        P("feat", "rows"),
    )
    return jax.shard_map(
        local,
        mesh=mesh,
        in_specs=placed,
        out_specs=(P("feat", "rows"), P("feat", "rows"), P("feat", None), P("feat")),
        check_vma=False,
    )
```

```python
import functools
import math

import jax
import jax.numpy as jnp
from jax import lax
from jax.experimental import pallas as pl
from jax.experimental.pallas import tpu as pltpu
from jax.sharding import PartitionSpec as P

TL = 4
BF = jnp.bfloat16
F32 = jnp.float32
VMEM = pl.BlockSpec(memory_space=pltpu.VMEM)
ANY = pl.BlockSpec(memory_space=pl.ANY)
SMEM = pl.BlockSpec(memory_space=pltpu.SMEM)


def lanes(index, width):
    return pl.ds(pl.multiple_of(index * width, width), width)


NY, NZ, NC = 4, 8, 2
CAP = 2
COLUMN = NZ * NC
PER = COLUMN * CAP


def move(x, dy=0, dc=0, flip=0):
    pairs = []
    for y in range(NY):
        for z in range(NZ):
            for c in range(NC):
                to = ((y + dy) % NY * NZ + (z ^ flip)) * NC + (c + dc) % NC
                pairs.append(((y * NZ + z) * NC + c, to))
    return lax.ppermute(x, "rows", pairs)


def pack_kernel(y_ref, wanted_ref, column_ref, *refs):
    i = pl.program_id(0)
    outs = refs[-NY:]
    block = outs[0].shape[2]
    slots = outs[0].shape[0]
    for k in range(NY):
        base = lax.rem(y_ref[0] + k, NY) * PER + i * slots
        for q in range(slots):
            w = jnp.maximum(wanted_ref[base + q], 0)
            outs[k][q] = column_ref[q // CAP, :, lanes(w, block)]


def pack(y, wanted, column, block, after):
    _, width, nodes = column.shape
    steps = 4
    shape = jax.ShapeDtypeStruct((PER, width, block), BF)
    out = pl.BlockSpec((PER // steps, width, block), lambda i: (i, 0, 0))
    return pl.pallas_call(
        pack_kernel,
        grid=(steps,),
        out_shape=[shape] * NY,
        in_specs=[SMEM, SMEM, pl.BlockSpec((COLUMN // steps, width, nodes), lambda i: (i, 0, 0))]
        + [ANY] * len(after),
        out_specs=[out] * NY,
        name="pack",
        cost_estimate=pl.CostEstimate(flops=0, bytes_accessed=6 << 20, transcendentals=0),
    )(y, wanted, column, *after)


def dot(a, b, dims):
    return lax.dot_general(a, b, ((dims[:1], dims[1:]), ((), ())), preferred_element_type=F32)


STEP = 4


def agg_local_kernel(cols_ref, feats_ref, tiles_ref, out_ref):
    i = pl.program_id(0)
    count, block = tiles_ref.shape[1], tiles_ref.shape[2]
    for rr in range(STEP):
        acc = None
        for t in range(0, count, 2):
            base = (i * STEP + rr) * count + t
            lhs = jnp.concatenate(
                [feats_ref[:, lanes(cols_ref[base + k], block)] for k in range(2)], axis=1
            )
            rhs = jnp.concatenate([tiles_ref[rr, t + k] for k in range(2)], axis=1)
            term = dot(lhs, rhs, (1, 1))
            acc = term if acc is None else acc + term
        out_ref[:, rr * block : (rr + 1) * block] = acc


def agg_local(cols, feats, tiles):
    row_blocks, _, block, _ = tiles.shape
    width = feats.shape[0]
    return pl.pallas_call(
        agg_local_kernel,
        grid=(row_blocks // STEP,),
        out_shape=jax.ShapeDtypeStruct((width, row_blocks * block), F32),
        in_specs=[
            SMEM,
            pl.BlockSpec(feats.shape, lambda i: (0, 0)),
            pl.BlockSpec((STEP, TL, block, block), lambda i: (i, 0, 0, 0)),
        ],
        out_specs=pl.BlockSpec((width, STEP * block), lambda i: (0, i)),
        name="agg_local",
        cost_estimate=pl.CostEstimate(
            flops=2 * width * row_blocks * TL * block * block, bytes_accessed=3 << 20, transcendentals=0
        ),
    )(cols, feats, tiles)


def agg_remote_kernel(slots_ref, tiles_ref, local_ref, *refs):
    parts, out_ref, recv_ref = refs[:-2], refs[-2], refs[-1]
    i = pl.program_id(0)
    count, block = tiles_ref.shape[1], tiles_ref.shape[2]

    @pl.when(i == 0)
    def _():
        for k, part in enumerate(parts):
            recv_ref[pl.ds(k * PER, PER)] = part[...]

    for rr in range(STEP):
        acc = local_ref[:, rr * block : (rr + 1) * block]
        for t in range(0, count, 2):
            base = (i * STEP + rr) * count + t
            lhs = jnp.concatenate([recv_ref[slots_ref[base + k]] for k in range(2)], axis=1)
            rhs = jnp.concatenate([tiles_ref[rr, t + k] for k in range(2)], axis=1)
            acc = acc + dot(lhs, rhs, (1, 1))
        out_ref[:, rr * block : (rr + 1) * block] = acc.astype(out_ref.dtype)


def agg_remote(slots, parts, tiles, local):
    row_blocks, per_block, block, _ = tiles.shape
    rem = per_block - TL
    width = local.shape[0]
    specs = [pl.BlockSpec(part.shape, lambda i: (0, 0, 0)) for part in parts]
    return pl.pallas_call(
        agg_remote_kernel,
        grid=(row_blocks // STEP,),
        out_shape=jax.ShapeDtypeStruct(local.shape, BF),
        in_specs=[
            SMEM,
            pl.BlockSpec((STEP, rem, block, block), lambda i: (i, 1, 0, 0)),
            pl.BlockSpec((width, STEP * block), lambda i: (0, i)),
        ]
        + specs,
        out_specs=pl.BlockSpec((width, STEP * block), lambda i: (0, i)),
        scratch_shapes=[pltpu.VMEM((NY * PER, width, block), BF)],
        name="agg_remote",
        cost_estimate=pl.CostEstimate(
            flops=2 * width * row_blocks * rem * block * block, bytes_accessed=5 << 20, transcendentals=0
        ),
    )(slots, tiles, local, *parts)


def mid_kernel(
    me_ref,
    own_ref,
    low_ref,
    high_ref,
    far_ref,
    cot_ref,
    w_ref,
    bias_ref,
    wown_ref,
    hid_ref,
    g_ref,
    sums_ref,
    agg_scr,
    hid_scr,
    wt_scr,
    gb_scr,
):
    i = pl.program_id(0)
    width = own_ref.shape[0]
    count = agg_scr.shape[0] // width
    me = me_ref[0]

    def rows(ahead):
        return pl.ds(pl.multiple_of(lax.rem(me + ahead, count) * width, width), width)

    @pl.when(i == 0)
    def _():
        wt_scr[...] = w_ref[...].astype(F32).T.astype(BF)
        sums_ref[...] = jnp.zeros_like(sums_ref)
        gb_scr[...] = jnp.zeros_like(gb_scr)

    agg_scr[rows(3)] = low_ref[...]
    agg_scr[rows(1)] = high_ref[...]
    agg_scr[rows(2)] = far_ref[...]
    agg_scr[rows(0)] = own_ref[...]
    pre = dot(wt_scr[...], agg_scr[...], (1, 0))
    bias = bias_ref[:, :3].astype(F32)
    pre = pre + ((bias[:, 2:3] + bias[:, 1:2]) + bias[:, 0:1])
    sigma = jax.nn.sigmoid(pre)
    hid_scr[...] = (pre * sigma).astype(BF)
    hid_ref[...] = hid_scr[rows(0)]
    grad_pre = cot_ref[...].astype(F32) * (sigma * (1.0 + pre * (1.0 - sigma)))
    total = grad_pre[:, :128]
    for k in range(1, grad_pre.shape[1] // 128):
        total = total + grad_pre[:, k * 128 : (k + 1) * 128]
    gb_scr[...] += total
    grad_b = grad_pre.astype(BF)
    g_ref[...] = dot(wown_ref[...], grad_b, (1, 0)).astype(BF)
    grad_w = dot(own_ref[...], grad_b, (1, 1))
    for k in range(grad_w.shape[1] // 128):
        sums_ref[k * width : (k + 1) * width] += grad_w[:, k * 128 : (k + 1) * 128]

    @pl.when(i == pl.num_programs(0) - 1)
    def _():
        sums_ref[-width:] = gb_scr[rows(0)]


def mid(me, pieces, packed, w_own):
    own, low, high, far = pieces
    width, nodes = own.shape
    hid_all = packed.shape[0]
    chunk = 512
    col = lambda i: (0, i)
    return pl.pallas_call(
        mid_kernel,
        grid=(nodes // chunk,),
        out_shape=(
            jax.ShapeDtypeStruct((width, nodes), BF),
            jax.ShapeDtypeStruct((width, nodes), BF),
            jax.ShapeDtypeStruct((width * (hid_all // 128 + 1), 128), F32),
        ),
        in_specs=[
            SMEM,
            pl.BlockSpec((width, chunk), col),
            pl.BlockSpec((width, chunk), col),
            pl.BlockSpec((width, chunk), col),
            pl.BlockSpec((width, chunk), col),
            pl.BlockSpec((hid_all, chunk), col),
            pl.BlockSpec((hid_all, hid_all), lambda i: (0, nodes // hid_all)),
            pl.BlockSpec((hid_all, 128), lambda i: (0, (nodes + hid_all) // 128)),
            pl.BlockSpec((width, hid_all), lambda i: (0, 0)),
        ],
        out_specs=(
            pl.BlockSpec((width, chunk), col),
            pl.BlockSpec((width, chunk), col),
            pl.BlockSpec((width * (hid_all // 128 + 1), 128), lambda i: (0, 0)),
        ),
        scratch_shapes=[
            pltpu.VMEM((hid_all, chunk), BF),
            pltpu.VMEM((hid_all, chunk), BF),
            pltpu.VMEM((hid_all, hid_all), BF),
            pltpu.VMEM((hid_all, 128), F32),
        ],
        name="mid",
        cost_estimate=pl.CostEstimate(
            flops=2 * nodes * hid_all * (hid_all + 2 * width),
            bytes_accessed=3 << 20,
            transcendentals=nodes * hid_all,
        ),
    )(me, own, low, high, far, packed, packed, packed, w_own)


def back_remote_kernel(slots_ref, g_ref, tiles_ref, out_ref):
    i = pl.program_id(0)
    width = g_ref.shape[0]
    count, block = tiles_ref.shape[1], tiles_ref.shape[2]

    @pl.when(i == 0)
    def _():
        out_ref[...] = jnp.zeros_like(out_ref)

    for rr in range(STEP):
        lhs = g_ref[:, rr * block : (rr + 1) * block]
        for t in range(0, count, 2):
            base = (i * STEP + rr) * count + t
            rhs = jnp.concatenate([tiles_ref[rr, t + k] for k in range(2)], axis=1)
            term = dot(lhs, rhs, (1, 0)).astype(BF)
            for k in range(2):
                slot = slots_ref[base + k]
                row = pl.multiple_of((slot % CAP) * width, width)
                out_ref[slot // CAP, pl.ds(row, width)] = term[:, k * block : (k + 1) * block]


def back_remote(slots, g, tiles, peers):
    row_blocks, per_block, block, _ = tiles.shape
    rem = per_block - TL
    width = g.shape[0]
    return pl.pallas_call(
        back_remote_kernel,
        grid=(row_blocks // STEP,),
        out_shape=jax.ShapeDtypeStruct((peers, CAP * width, block), BF),
        in_specs=[
            SMEM,
            pl.BlockSpec((width, STEP * block), lambda i: (0, i)),
            pl.BlockSpec((STEP, rem, block, block), lambda i: (i, 1, 0, 0)),
        ],
        out_specs=pl.BlockSpec((peers, CAP * width, block), lambda i: (0, 0, 0)),
        name="back_remote",
        cost_estimate=pl.CostEstimate(
            flops=2 * width * row_blocks * rem * block * block, bytes_accessed=5 << 20, transcendentals=0
        ),
    )(slots, g, tiles)


def back_local_kernel(cols_ref, g_ref, tiles_ref, _, out_ref):
    i = pl.program_id(0)
    count, block = tiles_ref.shape[1], tiles_ref.shape[2]

    @pl.when(i == 0)
    def _():
        out_ref[...] = jnp.zeros_like(out_ref)

    for rr in range(STEP):
        lhs = g_ref[:, rr * block : (rr + 1) * block]
        for t in range(0, count, 2):
            base = (i * STEP + rr) * count + t
            rhs = jnp.concatenate([tiles_ref[rr, t + k] for k in range(2)], axis=1)
            term = dot(lhs, rhs, (1, 0))
            for k in range(2):
                out_ref[:, lanes(cols_ref[base + k], block)] += term[:, k * block : (k + 1) * block]


def back_local(cols, g, tiles, after):
    row_blocks, _, block, _ = tiles.shape
    width = g.shape[0]
    return pl.pallas_call(
        back_local_kernel,
        grid=(row_blocks // STEP,),
        out_shape=jax.ShapeDtypeStruct(g.shape, F32),
        in_specs=[
            SMEM,
            pl.BlockSpec((width, STEP * block), lambda i: (0, i)),
            pl.BlockSpec((STEP, TL, block, block), lambda i: (i, 0, 0, 0)),
            ANY,
        ],
        out_specs=pl.BlockSpec(g.shape, lambda i: (0, 0)),
        name="back_local",
        cost_estimate=pl.CostEstimate(
            flops=2 * width * row_blocks * TL * block * block, bytes_accessed=3 << 20, transcendentals=0
        ),
    )(cols, g, tiles, after)


def finish_kernel(wanted_ref, recv_ref, local_ref, out_ref, odd_scr):
    width, block = out_ref.shape[0], recv_ref.shape[2]
    out_ref[...] = local_ref[...]
    odd_scr[...] = jnp.zeros_like(odd_scr)

    def body(p, carry):
        even = lanes(jnp.maximum(wanted_ref[p * CAP], 0), block)
        odd = lanes(jnp.maximum(wanted_ref[p * CAP + 1], 0), block)
        out_ref[:, even] += recv_ref[p, :width].astype(F32)
        odd_scr[:, odd] += recv_ref[p, width : 2 * width].astype(F32)
        return carry

    lax.fori_loop(0, recv_ref.shape[0], body, 0, unroll=4)
    out_ref[...] += odd_scr[...]


def finish(wanted, recv, local):
    return pl.pallas_call(
        finish_kernel,
        out_shape=jax.ShapeDtypeStruct(local.shape, F32),
        in_specs=[SMEM, VMEM, VMEM],
        out_specs=VMEM,
        scratch_shapes=[pltpu.VMEM(local.shape, F32)],
        name="finish",
        cost_estimate=pl.CostEstimate(flops=recv.size, bytes_accessed=4 << 20, transcendentals=0),
    )(wanted, recv, local)


def split_bf16(x, terms):
    parts = []
    for _ in range(terms):
        part = lax.reduce_precision(x, 8, 7)
        parts.append(part.astype(BF))
        x = x - part
    return parts


def local(feats, weight, bias, tile_cols, tile_values, cotangent):
    width, nodes_dev = feats.shape
    hid_all = weight.shape[1]
    block = tile_values.shape[1]
    row_blocks = nodes_dev // block
    peers = lax.axis_size("rows")
    fpeers = lax.axis_size("feat")
    per_block = tile_cols.shape[0] // row_blocks
    remote_count = row_blocks * (per_block - TL)
    place = lax.axis_index("rows")
    y, c = place // COLUMN, place % NC

    grid = tile_cols.reshape(row_blocks, per_block)
    tiles = tile_values.reshape(row_blocks, per_block, block, block)
    local_cols = (grid[:, :TL] % row_blocks).reshape(-1)
    remote_cols = grid[:, TL:].reshape(-1)
    owner = remote_cols // row_blocks
    inside = remote_cols % row_blocks
    order = jnp.arange(remote_count)
    earlier = (owner[:, None] == owner[None, :]) & (order[None, :] < order[:, None])
    rank = jnp.sum(earlier.astype(jnp.int32), axis=1)
    slots = owner * CAP + rank
    near = ((y - owner // COLUMN) & (NY - 1)) * PER + slots % PER

    hit = slots[None, :] == jnp.arange(peers * CAP)[:, None]
    request = jnp.max(jnp.where(hit, inside[None, :], -1), axis=1)

    columns = [[y0 * COLUMN + k for k in range(COLUMN)] for y0 in range(NY)]
    column = lax.all_gather(feats, "rows", axis_index_groups=columns)
    along_y = [[y0 * COLUMN + k for y0 in range(NY)] for k in range(COLUMN)]
    wanted = lax.all_to_all(
        request.reshape(NY, PER), "rows", 0, 0, tiled=True, axis_index_groups=along_y
    ).reshape(-1)
    holders = lax.all_to_all(request.reshape(peers, CAP), "rows", 0, 0, tiled=True).reshape(-1)
    agg = agg_local(local_cols, feats, tiles)

    bias_cols = jnp.pad(jnp.stack(split_bf16(bias, 3), axis=1), ((0, 0), (0, 125)))
    packed = jnp.concatenate([cotangent, weight, bias_cols], axis=1)
    packed = lax.all_gather(packed, "feat", axis=0, tiled=True)

    packs = pack(y.reshape(1), wanted, column, block, [holders, agg])
    parts = [packs[0]] + [move(packs[k], dy=k) for k in range(1, NY)]
    agg = agg_remote(near, parts, tiles, agg)

    pieces = [agg] + [
        lax.ppermute(agg, "feat", [(k, (k + s) % fpeers) for k in range(fpeers)]) for s in (1, 3, 2)
    ]
    me = lax.axis_index("feat").astype(jnp.int32).reshape(1)
    hidden_out, g, sums = mid(me, pieces, packed, weight)

    send = back_remote(slots, g, tiles, peers)
    recv = lax.all_to_all(send, "rows", split_axis=0, concat_axis=0, tiled=True)
    own = back_local(local_cols, g, tiles, send)

    own, sums = lax.optimization_barrier((own, sums))
    n_half = sums.shape[0] // NC
    n = n_half // NY

    def piece(x, index, size):
        return lax.dynamic_slice_in_dim(x, index * size, size, 0)

    half = piece(sums, c, n_half) + move(piece(sums, 1 - c, n_half), dc=1)
    part = piece(half, y, n)
    for k in range(1, NY):
        part = part + move(piece(half, (y + k) & (NY - 1), n), dy=k)
    for bit in (1, 2, 4):
        part = part + move(part, flip=bit)
    ring = [move(part, dy=k) for k in range(NY - 1, 0, -1)] + [part]
    half = lax.dynamic_slice_in_dim(jnp.concatenate(ring + ring), ((NY - 1 - y) & (NY - 1)) * n, n_half, 0)
    other = move(half, dc=1)
    total = lax.dynamic_slice_in_dim(
        jnp.concatenate([other, half, other]), (1 - c) * n_half, NC * n_half, 0
    ) / math.sqrt(nodes_dev * peers)
    grad_w = jnp.concatenate(
        [total[k * width : (k + 1) * width] for k in range(hid_all // 128)], axis=1
    )
    grad_b = jnp.sum(total[-width:], axis=1)

    grad_input = finish(holders, recv, own)
    return hidden_out, grad_input, grad_w, grad_b


def solution(mesh):
    placed = (
        P("feat", "rows"),
        P("feat", None),
        P("feat"),
        P("rows"),
        P("rows", None, None),
        P("feat", "rows"),
    )
    return jax.shard_map(
        local,
        mesh=mesh,
        in_specs=placed,
        out_specs=(P("feat", "rows"), P("feat", "rows"), P("feat", None), P("feat")),
        check_vma=False,
    )
```

```python
import functools
import math

import jax
import jax.numpy as jnp
from jax import lax
from jax.experimental import pallas as pl
from jax.experimental.pallas import tpu as pltpu
from jax.sharding import PartitionSpec as P

TL = 4
BF = jnp.bfloat16
F32 = jnp.float32
VMEM = pl.BlockSpec(memory_space=pltpu.VMEM)
ANY = pl.BlockSpec(memory_space=pl.ANY)
SMEM = pl.BlockSpec(memory_space=pltpu.SMEM)


def lanes(index, width):
    return pl.ds(pl.multiple_of(index * width, width), width)


NY, NZ, NC = 4, 8, 2
CAP = 2
ORDER = (0, 1, 7, 2, 6, 3, 5, 4)
GROUPS = ((0, 5), (5, 8))
PER = NZ * CAP


def shift(x, dy=0, dz=0, dc=0):
    pairs = []
    for y in range(NY):
        for z in range(NZ):
            for c in range(NC):
                to = ((y + dy) % NY * NZ + (z + dz) % NZ) * NC + (c + dc) % NC
                pairs.append(((y * NZ + z) * NC + c, to))
    return lax.ppermute(x, "rows", pairs)


def pack_kernel(first, count, split, *refs):
    wanted_ref, sources, outs = refs[0], refs[1 : 1 + count + split], refs[-NY:]
    width, block = outs[0].shape[2], outs[0].shape[3]
    for ys in range(NY):
        for cs in range(NC):
            for q in range(count * CAP):
                w = wanted_ref[(ys * NC + cs) * PER + first * CAP + q]
                where = lanes(jnp.maximum(w, 0), block)
                j = q // CAP
                if split and j == count - 1:
                    outs[ys][cs, q, : width // 2] = sources[j][:, where]
                    outs[ys][cs, q, width // 2 :] = sources[j + 1][:, where]
                else:
                    outs[ys][cs, q] = sources[j][:, where]


def pack(group, wanted, sources, block, after):
    first, last = group
    count = last - first
    width = sources[0].shape[0]
    shape = jax.ShapeDtypeStruct((NC, count * CAP, width, block), BF)
    return pl.pallas_call(
        functools.partial(pack_kernel, first, count, len(sources) > count),
        out_shape=[shape] * NY,
        in_specs=[SMEM] + [VMEM] * len(sources) + [ANY] * len(after),
        out_specs=[VMEM] * NY,
        name="pack",
        cost_estimate=pl.CostEstimate(flops=0, bytes_accessed=12 << 20, transcendentals=0),
    )(wanted, *sources, *after)


def dot(a, b, dims):
    return lax.dot_general(a, b, ((dims[:1], dims[1:]), ((), ())), preferred_element_type=F32)


STEP = 4


def agg_local_kernel(cols_ref, feats_ref, tiles_ref, _, out_ref):
    i = pl.program_id(0)
    count, block = tiles_ref.shape[1], tiles_ref.shape[2]
    for rr in range(STEP):
        acc = None
        for t in range(0, count, 2):
            base = (i * STEP + rr) * count + t
            lhs = jnp.concatenate(
                [feats_ref[:, lanes(cols_ref[base + k], block)] for k in range(2)], axis=1
            )
            rhs = jnp.concatenate([tiles_ref[rr, t + k] for k in range(2)], axis=1)
            term = dot(lhs, rhs, (1, 1))
            acc = term if acc is None else acc + term
        out_ref[:, rr * block : (rr + 1) * block] = acc


def agg_local(cols, feats, tiles, after):
    row_blocks, _, block, _ = tiles.shape
    width = feats.shape[0]
    return pl.pallas_call(
        agg_local_kernel,
        grid=(row_blocks // STEP,),
        out_shape=jax.ShapeDtypeStruct((width, row_blocks * block), F32),
        in_specs=[
            SMEM,
            pl.BlockSpec(feats.shape, lambda i: (0, 0)),
            pl.BlockSpec((STEP, TL, block, block), lambda i: (i, 0, 0, 0)),
            ANY,
        ],
        out_specs=pl.BlockSpec((width, STEP * block), lambda i: (0, i)),
        name="agg_local",
        cost_estimate=pl.CostEstimate(
            flops=2 * width * row_blocks * TL * block * block, bytes_accessed=3 << 20, transcendentals=0
        ),
    )(cols, feats, tiles, after)


def agg_remote_kernel(slots_ref, tiles_ref, local_ref, *refs):
    parts, out_ref, recv_ref = refs[:-2], refs[-2], refs[-1]
    i = pl.program_id(0)
    count, block = tiles_ref.shape[1], tiles_ref.shape[2]

    @pl.when(i == 0)
    def _():
        n = 0
        for first, last in GROUPS:
            size = (last - first) * CAP
            for ys in range(NY):
                recv_ref[pl.ds(ys * PER + first * CAP, size)] = parts[n + ys][0]
                recv_ref[pl.ds((NY + ys) * PER + first * CAP, size)] = parts[n + NY][ys]
            n += NY + 1

    for rr in range(STEP):
        acc = local_ref[:, rr * block : (rr + 1) * block]
        for t in range(0, count, 2):
            base = (i * STEP + rr) * count + t
            lhs = jnp.concatenate([recv_ref[slots_ref[base + k]] for k in range(2)], axis=1)
            rhs = jnp.concatenate([tiles_ref[rr, t + k] for k in range(2)], axis=1)
            acc = acc + dot(lhs, rhs, (1, 1))
        out_ref[:, rr * block : (rr + 1) * block] = acc.astype(out_ref.dtype)


def agg_remote(slots, parts, tiles, local):
    row_blocks, per_block, block, _ = tiles.shape
    rem = per_block - TL
    width = local.shape[0]
    specs = []
    for n, part in enumerate(parts):
        lead = 1 if n % (NY + 1) < NY else NY
        specs.append(pl.BlockSpec((lead,) + part.shape[1:], lambda i: (0, 0, 0, 0)))
    return pl.pallas_call(
        agg_remote_kernel,
        grid=(row_blocks // STEP,),
        out_shape=jax.ShapeDtypeStruct(local.shape, BF),
        in_specs=[
            SMEM,
            pl.BlockSpec((STEP, rem, block, block), lambda i: (i, 1, 0, 0)),
            pl.BlockSpec((width, STEP * block), lambda i: (0, i)),
        ]
        + specs,
        out_specs=pl.BlockSpec((width, STEP * block), lambda i: (0, i)),
        scratch_shapes=[pltpu.VMEM((NY * NC * PER, width, block), BF)],
        name="agg_remote",
        cost_estimate=pl.CostEstimate(
            flops=2 * width * row_blocks * rem * block * block, bytes_accessed=5 << 20, transcendentals=0
        ),
    )(slots, tiles, local, *parts)


def mid_kernel(
    me_ref,
    own_ref,
    low_ref,
    high_ref,
    far_ref,
    cot_ref,
    w_ref,
    bias_ref,
    wown_ref,
    request_ref,
    hid_ref,
    g_ref,
    sums_ref,
    agg_scr,
    hid_scr,
    wt_scr,
    gb_scr,
    gw_scr,
):
    i = pl.program_id(0)
    width = own_ref.shape[0]
    count = agg_scr.shape[0] // width
    me = me_ref[0]

    def rows(ahead):
        return pl.ds(pl.multiple_of(lax.rem(me + ahead, count) * width, width), width)

    @pl.when(i == 0)
    def _():
        wt_scr[...] = w_ref[...].astype(F32).T.astype(BF)
        gw_scr[...] = jnp.zeros_like(gw_scr)
        gb_scr[...] = jnp.zeros_like(gb_scr)

    agg_scr[rows(3)] = low_ref[...]
    agg_scr[rows(1)] = high_ref[...]
    agg_scr[rows(2)] = far_ref[...]
    agg_scr[rows(0)] = own_ref[...]
    pre = dot(wt_scr[...], agg_scr[...], (1, 0))
    bias = bias_ref[:, :3].astype(F32)
    pre = pre + ((bias[:, 2:3] + bias[:, 1:2]) + bias[:, 0:1])
    sigma = jax.nn.sigmoid(pre)
    hid_scr[...] = (pre * sigma).astype(BF)
    hid_ref[...] = hid_scr[rows(0)]
    grad_pre = cot_ref[...].astype(F32) * (sigma * (1.0 + pre * (1.0 - sigma)))
    total = grad_pre[:, :128]
    for k in range(1, grad_pre.shape[1] // 128):
        total = total + grad_pre[:, k * 128 : (k + 1) * 128]
    gb_scr[...] += total
    grad_b = grad_pre.astype(BF)
    g_ref[...] = dot(wown_ref[...], grad_b, (1, 0)).astype(BF)
    gw_scr[...] += dot(own_ref[...], grad_b, (1, 1))

    @pl.when(i == pl.num_programs(0) - 1)
    def _():
        hid_all = gw_scr.shape[1]
        sums_ref[:, 0, :hid_all] = gw_scr[...]
        sums_ref[:, 0, hid_all : hid_all + 128] = gb_scr[rows(0)]
        sums_ref[:, 0, hid_all + 128 :] = request_ref[...]


def mid(me, pieces, packed, w_own, request):
    own, low, high, far = pieces
    width, nodes = own.shape
    hid_all = packed.shape[0]
    chunk = 512
    col = lambda i: (0, i)
    return pl.pallas_call(
        mid_kernel,
        grid=(nodes // chunk,),
        out_shape=(
            jax.ShapeDtypeStruct((width, nodes), BF),
            jax.ShapeDtypeStruct((width, nodes), BF),
            jax.ShapeDtypeStruct((width, 1, hid_all + 256), F32),
        ),
        in_specs=[
            SMEM,
            pl.BlockSpec((width, chunk), col),
            pl.BlockSpec((width, chunk), col),
            pl.BlockSpec((width, chunk), col),
            pl.BlockSpec((width, chunk), col),
            pl.BlockSpec((hid_all, chunk), col),
            pl.BlockSpec((hid_all, hid_all), lambda i: (0, nodes // hid_all)),
            pl.BlockSpec((hid_all, 128), lambda i: (0, (nodes + hid_all) // 128)),
            pl.BlockSpec((width, hid_all), lambda i: (0, 0)),
            pl.BlockSpec((width, 128), lambda i: (0, 0)),
        ],
        out_specs=(
            pl.BlockSpec((width, chunk), col),
            pl.BlockSpec((width, chunk), col),
            pl.BlockSpec((width, 1, hid_all + 256), lambda i: (0, 0, 0)),
        ),
        scratch_shapes=[
            pltpu.VMEM((hid_all, chunk), BF),
            pltpu.VMEM((hid_all, chunk), BF),
            pltpu.VMEM((hid_all, hid_all), BF),
            pltpu.VMEM((hid_all, 128), F32),
            pltpu.VMEM((width, hid_all), F32),
        ],
        name="mid",
        cost_estimate=pl.CostEstimate(
            flops=2 * nodes * hid_all * (hid_all + 2 * width),
            bytes_accessed=3 << 20,
            transcendentals=nodes * hid_all,
        ),
    )(me, own, low, high, far, packed, packed, packed, w_own, request)


def back_remote_kernel(slots_ref, g_ref, tiles_ref, out_ref):
    i = pl.program_id(0)
    width = g_ref.shape[0]
    count, block = tiles_ref.shape[1], tiles_ref.shape[2]

    @pl.when(i == 0)
    def _():
        out_ref[...] = jnp.zeros_like(out_ref)

    for rr in range(STEP):
        lhs = g_ref[:, rr * block : (rr + 1) * block]
        for t in range(0, count, 2):
            base = (i * STEP + rr) * count + t
            rhs = jnp.concatenate([tiles_ref[rr, t + k] for k in range(2)], axis=1)
            term = dot(lhs, rhs, (1, 0)).astype(BF)
            for k in range(2):
                slot = slots_ref[base + k]
                row = pl.multiple_of((slot % CAP) * width, width)
                out_ref[slot // CAP, pl.ds(row, width)] = term[:, k * block : (k + 1) * block]


def back_remote(slots, g, tiles, peers, extra):
    row_blocks, per_block, block, _ = tiles.shape
    rem = per_block - TL
    width = g.shape[0]
    return pl.pallas_call(
        back_remote_kernel,
        grid=(row_blocks // STEP,),
        out_shape=jax.ShapeDtypeStruct((peers, CAP * width + extra, block), BF),
        in_specs=[
            SMEM,
            pl.BlockSpec((width, STEP * block), lambda i: (0, i)),
            pl.BlockSpec((STEP, rem, block, block), lambda i: (i, 1, 0, 0)),
        ],
        out_specs=pl.BlockSpec((peers, CAP * width + extra, block), lambda i: (0, 0, 0)),
        name="back_remote",
        cost_estimate=pl.CostEstimate(
            flops=2 * width * row_blocks * rem * block * block, bytes_accessed=5 << 20, transcendentals=0
        ),
    )(slots, g, tiles)


def back_local_kernel(cols_ref, g_ref, tiles_ref, out_ref):
    i = pl.program_id(0)
    count, block = tiles_ref.shape[1], tiles_ref.shape[2]

    @pl.when(i == 0)
    def _():
        out_ref[...] = jnp.zeros_like(out_ref)

    for rr in range(STEP):
        lhs = g_ref[:, rr * block : (rr + 1) * block]
        for t in range(0, count, 2):
            base = (i * STEP + rr) * count + t
            rhs = jnp.concatenate([tiles_ref[rr, t + k] for k in range(2)], axis=1)
            term = dot(lhs, rhs, (1, 0))
            for k in range(2):
                out_ref[:, lanes(cols_ref[base + k], block)] += term[:, k * block : (k + 1) * block]


def back_local(cols, g, tiles):
    row_blocks, _, block, _ = tiles.shape
    width = g.shape[0]
    return pl.pallas_call(
        back_local_kernel,
        grid=(row_blocks // STEP,),
        out_shape=jax.ShapeDtypeStruct(g.shape, F32),
        in_specs=[
            SMEM,
            pl.BlockSpec((width, STEP * block), lambda i: (0, i)),
            pl.BlockSpec((STEP, TL, block, block), lambda i: (i, 0, 0, 0)),
        ],
        out_specs=pl.BlockSpec(g.shape, lambda i: (0, 0)),
        name="back_local",
        cost_estimate=pl.CostEstimate(
            flops=2 * width * row_blocks * TL * block * block, bytes_accessed=3 << 20, transcendentals=0
        ),
    )(cols, g, tiles)


EXTRA = 8


def ride_kernel(divisor, sums_ref, _, send_ref, rider_scr, sem):
    span = sums_ref.shape[2] // 128 - 1
    total = jnp.sum(sums_ref[...], axis=0) / divisor
    rider_scr[...] = jnp.zeros_like(rider_scr)
    for k in range(span):
        row = total[:, k * 128 : (k + 1) * 128]
        high = row.astype(BF)
        low = (row - high.astype(F32)).astype(BF)
        peers = rider_scr.shape[0]
        rider_scr[:, k : k + 1] = jnp.broadcast_to(high[None], (peers, 1, 128))
        rider_scr[:, span + k : span + k + 1] = jnp.broadcast_to(low[None], (peers, 1, 128))
    rows = send_ref.shape[1] - EXTRA
    copy = pltpu.make_async_copy(rider_scr, send_ref.at[:, pl.ds(rows, EXTRA)], sem)
    copy.start()
    copy.wait()


def ride(divisor, sums, send):
    return pl.pallas_call(
        functools.partial(ride_kernel, divisor),
        out_shape=jax.ShapeDtypeStruct(send.shape, send.dtype),
        in_specs=[VMEM, ANY],
        out_specs=ANY,
        scratch_shapes=[pltpu.VMEM((send.shape[0], EXTRA, 128), BF), pltpu.SemaphoreType.DMA],
        input_output_aliases={1: 0},
        name="ride",
    )(sums, send)


def finish_kernel(wanted_ref, recv_ref, local_ref, out_ref, gw_ref, gb_ref, odd_scr):
    width, block = out_ref.shape[0], recv_ref.shape[2]
    out_ref[...] = local_ref[...]
    odd_scr[...] = jnp.zeros_like(odd_scr)

    def body(p, carry):
        even = lanes(jnp.maximum(wanted_ref[p * CAP], 0), block)
        odd = lanes(jnp.maximum(wanted_ref[p * CAP + 1], 0), block)
        out_ref[:, even] += recv_ref[p, :width].astype(F32)
        odd_scr[:, odd] += recv_ref[p, width : 2 * width].astype(F32)
        return carry

    lax.fori_loop(0, recv_ref.shape[0], body, 0, unroll=4)
    out_ref[...] += odd_scr[...]
    rider = recv_ref[:, CAP * width :].astype(F32)
    span = gw_ref.shape[1] // 128 + 1
    for k in range(span - 1):
        gw_ref[:, k * 128 : (k + 1) * 128] = rider[:, k] + rider[:, span + k]
    gb_ref[...] = rider[:, span - 1] + rider[:, 2 * span - 1]


def finish(wanted, recv, local, hid_all):
    width = local.shape[0]
    return pl.pallas_call(
        finish_kernel,
        out_shape=(
            jax.ShapeDtypeStruct(local.shape, F32),
            jax.ShapeDtypeStruct((width, hid_all), F32),
            jax.ShapeDtypeStruct((width, 128), F32),
        ),
        in_specs=[SMEM, VMEM, VMEM],
        out_specs=(VMEM, VMEM, VMEM),
        scratch_shapes=[pltpu.VMEM(local.shape, F32)],
        name="finish",
        cost_estimate=pl.CostEstimate(flops=recv.size, bytes_accessed=4 << 20, transcendentals=0),
    )(wanted, recv, local)


def split_bf16(x, terms):
    parts = []
    for _ in range(terms):
        part = lax.reduce_precision(x, 8, 7)
        parts.append(part.astype(BF))
        x = x - part
    return parts


def local(feats, weight, bias, tile_cols, tile_values, cotangent):
    width, nodes_dev = feats.shape
    hid_all = weight.shape[1]
    block = tile_values.shape[1]
    row_blocks = nodes_dev // block
    peers = lax.axis_size("rows")
    fpeers = lax.axis_size("feat")
    per_block = tile_cols.shape[0] // row_blocks
    remote_count = row_blocks * (per_block - TL)
    place = lax.axis_index("rows")
    y, z, c = place // (NZ * NC), place // NC % NZ, place % NC

    grid = tile_cols.reshape(row_blocks, per_block)
    tiles = tile_values.reshape(row_blocks, per_block, block, block)
    local_cols = (grid[:, :TL] % row_blocks).reshape(-1)
    remote_cols = grid[:, TL:].reshape(-1)
    owner = remote_cols // row_blocks
    inside = remote_cols % row_blocks
    order = jnp.arange(remote_count)
    earlier = (owner[:, None] == owner[None, :]) & (order[None, :] < order[:, None])
    rank = jnp.sum(earlier.astype(jnp.int32), axis=1)
    slots = owner * CAP + rank
    ahead = (owner // NC - z) & (NZ - 1)
    pos = jnp.maximum(jnp.where(ahead <= NZ // 2, 2 * ahead - 1, 2 * (NZ - ahead)), 0)
    back = (y - owner // (NZ * NC)) & (NY - 1)
    other = (owner ^ c) & 1
    near = ((other * NY + back) * NZ + pos) * CAP + rank

    def table(index):
        hit = index[None, :] == jnp.arange(peers * CAP)[:, None]
        return jnp.max(jnp.where(hit, inside[None, :], -1), axis=1)

    asked = table(near).reshape(NC, NY, PER)
    asked = jnp.stack([asked[0], shift(asked[1], dc=1)], axis=1)
    wanted = [asked[0]] + [shift(asked[ys], dy=-ys) for ys in range(1, NY)]
    wanted = jnp.stack(wanted).reshape(-1)

    up, down, parts = [feats], [feats], []
    for k in range(1, NZ // 2):
        late = (k == 3) & (wanted[0] > 1 << 20)
        up.append(shift(jnp.where(late, jnp.zeros_like(feats), up[-1]) if k == 3 else up[-1], dz=1))
        down.append(shift(jnp.where(late, jnp.zeros_like(feats), down[-1]) if k == 3 else down[-1], dz=-1))
    far_up = shift(up[-1][: width // 2], dz=1)
    far_down = shift(down[-1][width // 2 :], dz=-1)

    bias_cols = jnp.pad(jnp.stack(split_bf16(bias, 3), axis=1), ((0, 0), (0, 125)))
    packed = jnp.concatenate([cotangent, weight, bias_cols], axis=1)
    packed = lax.all_gather(packed, "feat", axis=0, tiled=True)

    after = []
    groups = ((feats, down[1], up[1], down[2], up[2]), (down[3], up[3], far_up, far_down))
    for group, sources in zip(GROUPS, groups):
        packs = pack(group, wanted, sources, block, after)
        moved = [packs[0]] + [shift(packs[ys], dy=ys) for ys in range(1, NY)]
        parts += moved
        parts.append(shift(jnp.concatenate([m[1:] for m in moved]), dc=1))
        after = [packs[0]]
    agg = agg_local(local_cols, feats, tiles, after[0])
    agg = agg_remote(near, parts, tiles, agg)

    pieces = [agg] + [
        lax.ppermute(agg, "feat", [(k, (k + s) % fpeers) for k in range(fpeers)]) for s in (1, 3, 2)
    ]
    me = lax.axis_index("feat").astype(jnp.int32).reshape(1)
    holding = jnp.pad(table(slots).reshape(peers, CAP).astype(F32), ((0, 0), (0, 128 - CAP)))
    hidden_out, g, sums = mid(me, pieces, packed, weight, holding)

    sums = lax.all_to_all(sums, "rows", split_axis=0, concat_axis=0, tiled=True)
    holders = sums[:, 0, hid_all + 128 : hid_all + 128 + CAP].astype(jnp.int32).reshape(-1)
    send = back_remote(slots, g, tiles, peers, EXTRA)
    own = back_local(local_cols, g, tiles)
    own, sums = lax.optimization_barrier((own, sums))
    send = ride(math.sqrt(nodes_dev * peers), sums, send)
    recv = lax.all_to_all(send, "rows", split_axis=0, concat_axis=0, tiled=True)
    grad_input, grad_w, grad_b = finish(holders, recv, own, hid_all)
    return hidden_out, grad_input, grad_w, jnp.sum(grad_b, axis=1)


def solution(mesh):
    placed = (
        P("feat", "rows"),
        P("feat", None),
        P("feat"),
        P("rows"),
        P("rows", None, None),
        P("feat", "rows"),
    )
    return jax.shard_map(
        local,
        mesh=mesh,
        in_specs=placed,
        out_specs=(P("feat", "rows"), P("feat", "rows"), P("feat", None), P("feat")),
        check_vma=False,
    )
```

```python
import functools
import math

import jax
import jax.numpy as jnp
from jax import lax
from jax.experimental import pallas as pl
from jax.experimental.pallas import tpu as pltpu
from jax.sharding import PartitionSpec as P

TL = 4
BF = jnp.bfloat16
F32 = jnp.float32
VMEM = pl.BlockSpec(memory_space=pltpu.VMEM)
ANY = pl.BlockSpec(memory_space=pl.ANY)
SMEM = pl.BlockSpec(memory_space=pltpu.SMEM)


def lanes(index, width):
    return pl.ds(pl.multiple_of(index * width, width), width)


NY, NZ, NC = 4, 8, 2
CAP = 2
ORDER = (0, 1, 7, 2, 6, 3, 5, 4)
GROUPS = ((0, 3), (3, 5), (5, 8))
PER = NZ * CAP


def shift(x, dy=0, dz=0, dc=0, flip_y=0, flip_z=0):
    pairs = []
    for y in range(NY):
        for z in range(NZ):
            for c in range(NC):
                to_y, to_z = ((y ^ flip_y) + dy) % NY, ((z ^ flip_z) + dz) % NZ
                pairs.append(((y * NZ + z) * NC + c, (to_y * NZ + to_z) * NC + (c + dc) % NC))
    return lax.ppermute(x, "rows", pairs)


def pack_kernel(first, count, split, *refs):
    wanted_ref, sources, outs = refs[0], refs[1 : 1 + count + split], refs[-NY:]
    width, block = outs[0].shape[2], outs[0].shape[3]
    for ys in range(NY):
        for cs in range(NC):
            for q in range(count * CAP):
                w = wanted_ref[(ys * NC + cs) * PER + first * CAP + q]
                where = lanes(jnp.maximum(w, 0), block)
                j = q // CAP
                if split and j == count - 1:
                    outs[ys][cs, q, : width // 2] = sources[j][:, where]
                    outs[ys][cs, q, width // 2 :] = sources[j + 1][:, where]
                else:
                    outs[ys][cs, q] = sources[j][:, where]


def pack(group, wanted, sources, block, after):
    first, last = group
    count = last - first
    width = sources[0].shape[0]
    shape = jax.ShapeDtypeStruct((NC, count * CAP, width, block), BF)
    return pl.pallas_call(
        functools.partial(pack_kernel, first, count, len(sources) > count),
        out_shape=[shape] * NY,
        in_specs=[SMEM] + [VMEM] * len(sources) + [ANY] * len(after),
        out_specs=[VMEM] * NY,
        name="pack",
        cost_estimate=pl.CostEstimate(flops=0, bytes_accessed=3 << 20, transcendentals=0),
    )(wanted, *sources, *after)


def dot(a, b, dims):
    return lax.dot_general(a, b, ((dims[:1], dims[1:]), ((), ())), preferred_element_type=F32)


STEP = 4


def agg_local_kernel(cols_ref, feats_ref, tiles_ref, out_ref):
    i = pl.program_id(0)
    count, block = tiles_ref.shape[1], tiles_ref.shape[2]
    for rr in range(STEP):
        acc = None
        for t in range(0, count, 2):
            base = (i * STEP + rr) * count + t
            lhs = jnp.concatenate(
                [feats_ref[:, lanes(cols_ref[base + k], block)] for k in range(2)], axis=1
            )
            rhs = jnp.concatenate([tiles_ref[rr, t + k] for k in range(2)], axis=1)
            term = dot(lhs, rhs, (1, 1))
            acc = term if acc is None else acc + term
        out_ref[:, rr * block : (rr + 1) * block] = acc


def agg_local(cols, feats, tiles):
    row_blocks, _, block, _ = tiles.shape
    width = feats.shape[0]
    return pl.pallas_call(
        agg_local_kernel,
        grid=(row_blocks // STEP,),
        out_shape=jax.ShapeDtypeStruct((width, row_blocks * block), F32),
        in_specs=[
            SMEM,
            pl.BlockSpec(feats.shape, lambda i: (0, 0)),
            pl.BlockSpec((STEP, TL, block, block), lambda i: (i, 0, 0, 0)),
        ],
        out_specs=pl.BlockSpec((width, STEP * block), lambda i: (0, i)),
        name="agg_local",
        cost_estimate=pl.CostEstimate(
            flops=2 * width * row_blocks * TL * block * block, bytes_accessed=3 << 20, transcendentals=0
        ),
    )(cols, feats, tiles)


def agg_remote_kernel(slots_ref, tiles_ref, local_ref, *refs):
    parts, out_ref, recv_ref = refs[:-2], refs[-2], refs[-1]
    i = pl.program_id(0)
    count, block = tiles_ref.shape[1], tiles_ref.shape[2]

    @pl.when(i == 0)
    def _():
        n = 0
        for first, last in GROUPS:
            size = (last - first) * CAP
            for ys in range(NY):
                recv_ref[pl.ds(ys * PER + first * CAP, size)] = parts[n + ys][0]
                recv_ref[pl.ds((NY + ys) * PER + first * CAP, size)] = parts[n + NY][ys]
            n += NY + 1

    for rr in range(STEP):
        acc = local_ref[:, rr * block : (rr + 1) * block]
        for t in range(0, count, 2):
            base = (i * STEP + rr) * count + t
            lhs = jnp.concatenate([recv_ref[slots_ref[base + k]] for k in range(2)], axis=1)
            rhs = jnp.concatenate([tiles_ref[rr, t + k] for k in range(2)], axis=1)
            acc = acc + dot(lhs, rhs, (1, 1))
        out_ref[:, rr * block : (rr + 1) * block] = acc.astype(out_ref.dtype)


def agg_remote(slots, parts, tiles, local):
    row_blocks, per_block, block, _ = tiles.shape
    rem = per_block - TL
    width = local.shape[0]
    specs = []
    for n, part in enumerate(parts):
        lead = 1 if n % (NY + 1) < NY else NY
        specs.append(pl.BlockSpec((lead,) + part.shape[1:], lambda i: (0, 0, 0, 0)))
    return pl.pallas_call(
        agg_remote_kernel,
        grid=(row_blocks // STEP,),
        out_shape=jax.ShapeDtypeStruct(local.shape, BF),
        in_specs=[
            SMEM,
            pl.BlockSpec((STEP, rem, block, block), lambda i: (i, 1, 0, 0)),
            pl.BlockSpec((width, STEP * block), lambda i: (0, i)),
        ]
        + specs,
        out_specs=pl.BlockSpec((width, STEP * block), lambda i: (0, i)),
        scratch_shapes=[pltpu.VMEM((NY * NC * PER, width, block), BF)],
        name="agg_remote",
        cost_estimate=pl.CostEstimate(
            flops=2 * width * row_blocks * rem * block * block, bytes_accessed=5 << 20, transcendentals=0
        ),
    )(slots, tiles, local, *parts)


def mid_kernel(
    me_ref,
    _,
    own_ref,
    low_ref,
    high_ref,
    far_ref,
    cot_ref,
    w_ref,
    bias_ref,
    wown_ref,
    hid_ref,
    g_ref,
    keep_ref,
    give_ref,
    agg_scr,
    hid_scr,
    wt_scr,
    gb_scr,
    sums_scr,
):
    i = pl.program_id(0)
    width = own_ref.shape[0]
    count = agg_scr.shape[0] // width
    me = me_ref[0]

    def rows(ahead):
        return pl.ds(pl.multiple_of(lax.rem(me + ahead, count) * width, width), width)

    @pl.when(i == 0)
    def _():
        wt_scr[...] = w_ref[...].astype(F32).T.astype(BF)
        sums_scr[...] = jnp.zeros_like(sums_scr)
        gb_scr[...] = jnp.zeros_like(gb_scr)

    agg_scr[rows(3)] = low_ref[...]
    agg_scr[rows(1)] = high_ref[...]
    agg_scr[rows(2)] = far_ref[...]
    agg_scr[rows(0)] = own_ref[...]
    pre = dot(wt_scr[...], agg_scr[...], (1, 0))
    bias = bias_ref[:, :3].astype(F32)
    pre = pre + ((bias[:, 2:3] + bias[:, 1:2]) + bias[:, 0:1])
    sigma = jax.nn.sigmoid(pre)
    hid_scr[...] = (pre * sigma).astype(BF)
    hid_ref[...] = hid_scr[rows(0)]
    grad_pre = cot_ref[...].astype(F32) * (sigma * (1.0 + pre * (1.0 - sigma)))
    total = grad_pre[:, :128]
    for k in range(1, grad_pre.shape[1] // 128):
        total = total + grad_pre[:, k * 128 : (k + 1) * 128]
    gb_scr[...] += total
    grad_b = grad_pre.astype(BF)
    g_ref[...] = dot(wown_ref[...], grad_b, (1, 0)).astype(BF)
    grad_w = dot(own_ref[...], grad_b, (1, 1))
    for k in range(grad_w.shape[1] // 128):
        sums_scr[k * width : (k + 1) * width] += grad_w[:, k * 128 : (k + 1) * 128]

    @pl.when(i == pl.num_programs(0) - 1)
    def _():
        half = keep_ref.shape[0]
        sums_scr[-width:] = gb_scr[rows(0)]
        keep_ref[...] = sums_scr[pl.ds(pl.multiple_of(me_ref[1] * half, half), half)]
        give_ref[...] = sums_scr[pl.ds(pl.multiple_of((1 - me_ref[1]) * half, half), half)]


def mid(me, pieces, packed, w_own, after):
    own, low, high, far = pieces
    width, nodes = own.shape
    hid_all = packed.shape[0]
    chunk = 512
    half = width * (hid_all // 128 + 1) // NC
    col = lambda i: (0, i)
    return pl.pallas_call(
        mid_kernel,
        grid=(nodes // chunk,),
        out_shape=(
            jax.ShapeDtypeStruct((width, nodes), BF),
            jax.ShapeDtypeStruct((width, nodes), BF),
            jax.ShapeDtypeStruct((half, 128), F32),
            jax.ShapeDtypeStruct((half, 128), F32),
        ),
        in_specs=[
            SMEM,
            ANY,
            pl.BlockSpec((width, chunk), col),
            pl.BlockSpec((width, chunk), col),
            pl.BlockSpec((width, chunk), col),
            pl.BlockSpec((width, chunk), col),
            pl.BlockSpec((hid_all, chunk), col),
            pl.BlockSpec((hid_all, hid_all), lambda i: (0, nodes // hid_all)),
            pl.BlockSpec((hid_all, 128), lambda i: (0, (nodes + hid_all) // 128)),
            pl.BlockSpec((width, hid_all), lambda i: (0, 0)),
        ],
        out_specs=(
            pl.BlockSpec((width, chunk), col),
            pl.BlockSpec((width, chunk), col),
            pl.BlockSpec((half, 128), lambda i: (0, 0)),
            pl.BlockSpec((half, 128), lambda i: (0, 0)),
        ),
        scratch_shapes=[
            pltpu.VMEM((hid_all, chunk), BF),
            pltpu.VMEM((hid_all, chunk), BF),
            pltpu.VMEM((hid_all, hid_all), BF),
            pltpu.VMEM((hid_all, 128), F32),
            pltpu.VMEM((NC * half, 128), F32),
        ],
        name="mid",
        cost_estimate=pl.CostEstimate(
            flops=2 * nodes * hid_all * (hid_all + 2 * width),
            bytes_accessed=3 << 20,
            transcendentals=nodes * hid_all,
        ),
    )(me, after, own, low, high, far, packed, packed, packed, w_own)


def back_remote_kernel(slots_ref, g_ref, tiles_ref, _, out_ref):
    i = pl.program_id(0)
    width = g_ref.shape[0]
    count, block = tiles_ref.shape[1], tiles_ref.shape[2]

    @pl.when(i == 0)
    def _():
        out_ref[...] = jnp.zeros_like(out_ref)

    for rr in range(STEP):
        lhs = g_ref[:, rr * block : (rr + 1) * block]
        for t in range(0, count, 2):
            base = (i * STEP + rr) * count + t
            rhs = jnp.concatenate([tiles_ref[rr, t + k] for k in range(2)], axis=1)
            term = dot(lhs, rhs, (1, 0)).astype(BF)
            for k in range(2):
                slot = slots_ref[base + k]
                row = pl.multiple_of((slot % CAP) * width, width)
                out_ref[slot // CAP, pl.ds(row, width)] = term[:, k * block : (k + 1) * block]


def back_remote(slots, g, tiles, peers, after):
    row_blocks, per_block, block, _ = tiles.shape
    rem = per_block - TL
    width = g.shape[0]
    return pl.pallas_call(
        back_remote_kernel,
        grid=(row_blocks // STEP,),
        out_shape=jax.ShapeDtypeStruct((peers, CAP * width, block), BF),
        in_specs=[
            SMEM,
            pl.BlockSpec((width, STEP * block), lambda i: (0, i)),
            pl.BlockSpec((STEP, rem, block, block), lambda i: (i, 1, 0, 0)),
            ANY,
        ],
        out_specs=pl.BlockSpec((peers, CAP * width, block), lambda i: (0, 0, 0)),
        name="back_remote",
        cost_estimate=pl.CostEstimate(
            flops=2 * width * row_blocks * rem * block * block, bytes_accessed=5 << 20, transcendentals=0
        ),
    )(slots, g, tiles, after)


def back_local_kernel(cols_ref, g_ref, tiles_ref, _, out_ref):
    i = pl.program_id(0)
    count, block = tiles_ref.shape[1], tiles_ref.shape[2]

    @pl.when(i == 0)
    def _():
        out_ref[...] = jnp.zeros_like(out_ref)

    for rr in range(STEP):
        lhs = g_ref[:, rr * block : (rr + 1) * block]
        for t in range(0, count, 2):
            base = (i * STEP + rr) * count + t
            rhs = jnp.concatenate([tiles_ref[rr, t + k] for k in range(2)], axis=1)
            term = dot(lhs, rhs, (1, 0))
            for k in range(2):
                out_ref[:, lanes(cols_ref[base + k], block)] += term[:, k * block : (k + 1) * block]


def back_local(cols, g, tiles, after):
    row_blocks, _, block, _ = tiles.shape
    width = g.shape[0]
    return pl.pallas_call(
        back_local_kernel,
        grid=(row_blocks // STEP,),
        out_shape=jax.ShapeDtypeStruct(g.shape, F32),
        in_specs=[
            SMEM,
            pl.BlockSpec((width, STEP * block), lambda i: (0, i)),
            pl.BlockSpec((STEP, TL, block, block), lambda i: (i, 0, 0, 0)),
            ANY,
        ],
        out_specs=pl.BlockSpec(g.shape, lambda i: (0, 0)),
        name="back_local",
        cost_estimate=pl.CostEstimate(
            flops=2 * width * row_blocks * TL * block * block, bytes_accessed=3 << 20, transcendentals=0
        ),
    )(cols, g, tiles, after)


def finish_kernel(place_ref, wanted_ref, recv_ref, local_ref, out_ref, odd_scr):
    width, block = out_ref.shape[0], recv_ref.shape[2]
    out_ref[...] = local_ref[...]
    odd_scr[...] = jnp.zeros_like(odd_scr)

    def body(p, carry):
        back = (p // (NZ * NC) - place_ref[0]) & (NY - 1)
        base = ((p // NC % NZ * NY + back) * NC + ((p ^ place_ref[1]) & 1)) * CAP
        even = lanes(jnp.maximum(wanted_ref[base], 0), block)
        odd = lanes(jnp.maximum(wanted_ref[base + 1], 0), block)
        out_ref[:, even] += recv_ref[p, :width].astype(F32)
        odd_scr[:, odd] += recv_ref[p, width : 2 * width].astype(F32)
        return carry

    lax.fori_loop(0, recv_ref.shape[0], body, 0, unroll=4)
    out_ref[...] += odd_scr[...]


def finish(place, wanted, recv, local):
    return pl.pallas_call(
        finish_kernel,
        out_shape=jax.ShapeDtypeStruct(local.shape, F32),
        in_specs=[SMEM, SMEM, VMEM, VMEM],
        out_specs=VMEM,
        scratch_shapes=[pltpu.VMEM(local.shape, F32)],
        name="finish",
        cost_estimate=pl.CostEstimate(flops=recv.size, bytes_accessed=4 << 20, transcendentals=0),
    )(place, wanted, recv, local)


def split_bf16(x, terms):
    parts = []
    for _ in range(terms):
        part = lax.reduce_precision(x, 8, 7)
        parts.append(part.astype(BF))
        x = x - part
    return parts


def local(feats, weight, bias, tile_cols, tile_values, cotangent):
    width, nodes_dev = feats.shape
    hid_all = weight.shape[1]
    block = tile_values.shape[1]
    row_blocks = nodes_dev // block
    peers = lax.axis_size("rows")
    fpeers = lax.axis_size("feat")
    per_block = tile_cols.shape[0] // row_blocks
    remote_count = row_blocks * (per_block - TL)
    place = lax.axis_index("rows")
    y, z, c = place // (NZ * NC), place // NC % NZ, place % NC

    grid = tile_cols.reshape(row_blocks, per_block)
    tiles = tile_values.reshape(row_blocks, per_block, block, block)
    local_cols = (grid[:, :TL] % row_blocks).reshape(-1)
    remote_cols = grid[:, TL:].reshape(-1)
    owner = remote_cols // row_blocks
    inside = remote_cols % row_blocks
    order = jnp.arange(remote_count)
    earlier = (owner[:, None] == owner[None, :]) & (order[None, :] < order[:, None])
    rank = jnp.sum(earlier.astype(jnp.int32), axis=1)
    slots = owner * CAP + rank
    ahead = (owner // NC - z) & (NZ - 1)

    def place_of(ahead):
        return jnp.maximum(jnp.where(ahead <= NZ // 2, 2 * ahead - 1, 2 * (NZ - ahead)), 0)

    pos = place_of(ahead)
    back = (y - owner // (NZ * NC)) & (NY - 1)
    other = (owner ^ c) & 1
    near = ((other * NY + back) * NZ + pos) * CAP + rank

    def table(index):
        hit = index[None, :] == jnp.arange(peers * CAP)[:, None]
        return jnp.max(jnp.where(hit, inside[None, :], -1), axis=1)

    asked = table(near).reshape(NC, NY, PER)
    asked = jnp.stack([asked[0], shift(asked[1], dc=1)], axis=1)
    wanted = [asked[0]] + [shift(asked[ys], dy=-ys) for ys in range(1, NY)]
    wanted = jnp.stack(wanted).reshape(-1)

    up, down, parts = [feats], [feats], []
    for k in range(1, NZ // 2):
        up.append(shift(up[-1], dz=1))
        down.append(shift(down[-1], dz=-1))
    far_up = shift(up[-1][: width // 2], dz=1)
    far_down = shift(down[-1][width // 2 :], dz=-1)
    groups = ((feats, down[1], up[1]), (down[2], up[2]), (down[3], up[3], far_up, far_down))
    after = []
    agg = agg_local(local_cols, feats, tiles)
    for group, sources in zip(GROUPS, groups):
        packs = pack(group, wanted, sources, block, after)
        after = [packs[0], agg]
        moved = [packs[0]] + [shift(packs[ys], dy=ys) for ys in range(1, NY)]
        parts += moved
        parts.append(shift(jnp.concatenate([m[1:] for m in moved]), dc=1))

    bias_cols = jnp.pad(jnp.stack(split_bf16(bias, 3), axis=1), ((0, 0), (0, 125)))
    packed = jnp.concatenate([cotangent, weight, bias_cols], axis=1)
    packed = lax.all_gather(packed, "feat", axis=0, tiled=True)

    agg = agg_remote(near, parts, tiles, agg)

    pieces = [agg] + [
        lax.ppermute(agg, "feat", [(k, (k + s) % fpeers) for k in range(fpeers)]) for s in (1, 3, 2)
    ]
    by_owner = wanted.reshape(NY * NC, NZ, CAP)
    steps = (jnp.arange(NZ) - z) & (NZ - 1)
    match = (place_of(steps)[:, None] == jnp.arange(NZ)[None, :])[:, None, :, None]
    held = jnp.sum(jnp.where(match, by_owner[None], 0), axis=2).reshape(NZ, NY * NC * CAP)
    held = jnp.where(agg[0, 0].astype(F32) > jnp.inf, 0, held)
    along_z = [[(y0 * NZ + z0) * NC + c0 for z0 in range(NZ)] for y0 in range(NY) for c0 in range(NC)]
    held = lax.all_to_all(held, "rows", 0, 0, tiled=True, axis_index_groups=along_z).reshape(-1)

    me = jnp.stack([lax.axis_index("feat"), c]).astype(jnp.int32)
    hidden_out, g, keep, give = mid(me, pieces, packed, weight, held)

    part = keep + shift(give, dc=1)
    part = part + shift(part, flip_z=1)
    pairs = [part] + [shift(part, flip_z=k) for k in (2, 4, 6)]
    send = back_remote(slots, g, tiles, peers, part)
    send, pairs = lax.optimization_barrier((send, pairs))
    part = (pairs[0] + pairs[1]) + (pairs[2] + pairs[3])
    recv = lax.all_to_all(send, "rows", split_axis=0, concat_axis=0, tiled=True)
    own = back_local(local_cols, g, tiles, send)

    own, part = lax.optimization_barrier((own, part))
    pairs = [part] + [shift(part, flip_y=k) for k in (1, 2, 3)]
    part = (pairs[0] + pairs[1]) + (pairs[2] + pairs[3])
    other = shift(part, dc=1)
    total = jnp.where(c == 0, jnp.concatenate([part, other]), jnp.concatenate([other, part]))
    total = total / math.sqrt(nodes_dev * peers)
    grad_w = jnp.concatenate([total[k * width : (k + 1) * width] for k in range(hid_all // 128)], axis=1)
    grad_b = jnp.sum(total[-width:], axis=1)

    grad_input = finish(jnp.stack([y, c]).astype(jnp.int32), held, recv, own)
    return hidden_out, grad_input, grad_w, grad_b


def solution(mesh):
    placed = (
        P("feat", "rows"),
        P("feat", None),
        P("feat"),
        P("rows"),
        P("rows", None, None),
        P("feat", "rows"),
    )
    return jax.shard_map(
        local,
        mesh=mesh,
        in_specs=placed,
        out_specs=(P("feat", "rows"), P("feat", "rows"), P("feat", None), P("feat")),
        check_vma=False,
    )
```

```python
import functools
import math

import jax
import jax.numpy as jnp
from jax import lax
from jax.experimental import pallas as pl
from jax.experimental.pallas import tpu as pltpu
from jax.sharding import PartitionSpec as P

TL = 4
BF = jnp.bfloat16
F32 = jnp.float32
VMEM = pl.BlockSpec(memory_space=pltpu.VMEM)
ANY = pl.BlockSpec(memory_space=pl.ANY)
SMEM = pl.BlockSpec(memory_space=pltpu.SMEM)


def lanes(index, width):
    return pl.ds(pl.multiple_of(index * width, width), width)


NY, NZ, NC = 4, 8, 2
CAP = 2
COLUMN = NZ * NC
PER = COLUMN * CAP


def shift(x, dy=0, dz=0, dc=0, flip_y=0, flip_z=0):
    pairs = []
    for y in range(NY):
        for z in range(NZ):
            for c in range(NC):
                to_y, to_z = ((y ^ flip_y) + dy) % NY, ((z ^ flip_z) + dz) % NZ
                pairs.append(((y * NZ + z) * NC + c, (to_y * NZ + to_z) * NC + (c + dc) % NC))
    return lax.ppermute(x, "rows", pairs)


def pack_kernel(ks, wanted_ref, column_ref, *refs):
    outs = refs[-len(ks) :]
    slots, _, block = outs[0].shape
    for k, out_ref in zip(ks, outs):
        base = k * PER + pl.program_id(0) * slots
        for q in range(slots):
            w = jnp.maximum(wanted_ref[base + q], 0)
            out_ref[q] = column_ref[q // CAP, :, lanes(w, block)]


def pack(ks, wanted, column, block, after):
    _, width, nodes = column.shape
    steps = 4
    return pl.pallas_call(
        functools.partial(pack_kernel, ks),
        grid=(steps,),
        out_shape=[jax.ShapeDtypeStruct((PER, width, block), BF)] * len(ks),
        in_specs=[SMEM, pl.BlockSpec((COLUMN // steps, width, nodes), lambda i: (i, 0, 0))]
        + [ANY] * len(after),
        out_specs=[pl.BlockSpec((PER // steps, width, block), lambda i: (i, 0, 0))] * len(ks),
        name="pack",
        cost_estimate=pl.CostEstimate(flops=0, bytes_accessed=5 << 20, transcendentals=0),
    )(wanted, column, *after)


def dot(a, b, dims):
    return lax.dot_general(a, b, ((dims[:1], dims[1:]), ((), ())), preferred_element_type=F32)


STEP = 4


def agg_local_kernel(cols_ref, feats_ref, tiles_ref, out_ref):
    i = pl.program_id(0)
    count, block = tiles_ref.shape[1], tiles_ref.shape[2]
    for rr in range(STEP):
        acc = None
        for t in range(0, count, 2):
            base = (i * STEP + rr) * count + t
            lhs = jnp.concatenate(
                [feats_ref[:, lanes(cols_ref[base + k], block)] for k in range(2)], axis=1
            )
            rhs = jnp.concatenate([tiles_ref[rr, t + k] for k in range(2)], axis=1)
            term = dot(lhs, rhs, (1, 1))
            acc = term if acc is None else acc + term
        out_ref[:, rr * block : (rr + 1) * block] = acc


def agg_local(cols, feats, tiles):
    row_blocks, _, block, _ = tiles.shape
    width = feats.shape[0]
    return pl.pallas_call(
        agg_local_kernel,
        grid=(row_blocks // STEP,),
        out_shape=jax.ShapeDtypeStruct((width, row_blocks * block), F32),
        in_specs=[
            SMEM,
            pl.BlockSpec(feats.shape, lambda i: (0, 0)),
            pl.BlockSpec((STEP, TL, block, block), lambda i: (i, 0, 0, 0)),
        ],
        out_specs=pl.BlockSpec((width, STEP * block), lambda i: (0, i)),
        name="agg_local",
        cost_estimate=pl.CostEstimate(
            flops=2 * width * row_blocks * TL * block * block, bytes_accessed=3 << 20, transcendentals=0
        ),
    )(cols, feats, tiles)


def agg_remote_kernel(slots_ref, tiles_ref, local_ref, *refs):
    parts, out_ref, recv_ref = refs[:-2], refs[-2], refs[-1]
    i = pl.program_id(0)
    count, block = tiles_ref.shape[1], tiles_ref.shape[2]

    @pl.when(i == 0)
    def _():
        for k, part in enumerate(parts):
            recv_ref[pl.ds(k * PER, PER)] = part[...]

    for rr in range(STEP):
        acc = local_ref[:, rr * block : (rr + 1) * block]
        for t in range(0, count, 2):
            base = (i * STEP + rr) * count + t
            lhs = jnp.concatenate([recv_ref[slots_ref[base + k]] for k in range(2)], axis=1)
            rhs = jnp.concatenate([tiles_ref[rr, t + k] for k in range(2)], axis=1)
            acc = acc + dot(lhs, rhs, (1, 1))
        out_ref[:, rr * block : (rr + 1) * block] = acc.astype(out_ref.dtype)


def agg_remote(slots, parts, tiles, local):
    row_blocks, per_block, block, _ = tiles.shape
    rem = per_block - TL
    width = local.shape[0]
    specs = [pl.BlockSpec(part.shape, lambda i: (0, 0, 0)) for part in parts]
    return pl.pallas_call(
        agg_remote_kernel,
        grid=(row_blocks // STEP,),
        out_shape=jax.ShapeDtypeStruct(local.shape, BF),
        in_specs=[
            SMEM,
            pl.BlockSpec((STEP, rem, block, block), lambda i: (i, 1, 0, 0)),
            pl.BlockSpec((width, STEP * block), lambda i: (0, i)),
        ]
        + specs,
        out_specs=pl.BlockSpec((width, STEP * block), lambda i: (0, i)),
        scratch_shapes=[pltpu.VMEM((NY * PER, width, block), BF)],
        name="agg_remote",
        cost_estimate=pl.CostEstimate(
            flops=2 * width * row_blocks * rem * block * block, bytes_accessed=5 << 20, transcendentals=0
        ),
    )(slots, tiles, local, *parts)


def mid_kernel(
    me_ref,
    _,
    own_ref,
    low_ref,
    high_ref,
    far_ref,
    cot_ref,
    w_ref,
    bias_ref,
    wown_ref,
    hid_ref,
    g_ref,
    keep_ref,
    give_ref,
    agg_scr,
    hid_scr,
    wt_scr,
    gb_scr,
    sums_scr,
):
    i = pl.program_id(0)
    width = own_ref.shape[0]
    count = agg_scr.shape[0] // width
    me = me_ref[0]

    def rows(ahead):
        return pl.ds(pl.multiple_of(lax.rem(me + ahead, count) * width, width), width)

    @pl.when(i == 0)
    def _():
        wt_scr[...] = w_ref[...].astype(F32).T.astype(BF)
        sums_scr[...] = jnp.zeros_like(sums_scr)
        gb_scr[...] = jnp.zeros_like(gb_scr)

    agg_scr[rows(3)] = low_ref[...]
    agg_scr[rows(1)] = high_ref[...]
    agg_scr[rows(2)] = far_ref[...]
    agg_scr[rows(0)] = own_ref[...]
    pre = dot(wt_scr[...], agg_scr[...], (1, 0))
    bias = bias_ref[:, :3].astype(F32)
    pre = pre + ((bias[:, 2:3] + bias[:, 1:2]) + bias[:, 0:1])
    sigma = jax.nn.sigmoid(pre)
    hid_scr[...] = (pre * sigma).astype(BF)
    hid_ref[...] = hid_scr[rows(0)]
    grad_pre = cot_ref[...].astype(F32) * (sigma * (1.0 + pre * (1.0 - sigma)))
    total = grad_pre[:, :128]
    for k in range(1, grad_pre.shape[1] // 128):
        total = total + grad_pre[:, k * 128 : (k + 1) * 128]
    gb_scr[...] += total
    grad_b = grad_pre.astype(BF)
    g_ref[...] = dot(wown_ref[...], grad_b, (1, 0)).astype(BF)
    grad_w = dot(own_ref[...], grad_b, (1, 1))
    for k in range(grad_w.shape[1] // 128):
        sums_scr[k * width : (k + 1) * width] += grad_w[:, k * 128 : (k + 1) * 128]

    @pl.when(i == pl.num_programs(0) - 1)
    def _():
        half = keep_ref.shape[0]
        sums_scr[-width:] = gb_scr[rows(0)]
        keep_ref[...] = sums_scr[pl.ds(pl.multiple_of(me_ref[1] * half, half), half)]
        give_ref[...] = sums_scr[pl.ds(pl.multiple_of((1 - me_ref[1]) * half, half), half)]


def mid(me, pieces, packed, w_own, after):
    own, low, high, far = pieces
    width, nodes = own.shape
    hid_all = packed.shape[0]
    chunk = 512
    half = width * (hid_all // 128 + 1) // NC
    col = lambda i: (0, i)
    return pl.pallas_call(
        mid_kernel,
        grid=(nodes // chunk,),
        out_shape=(
            jax.ShapeDtypeStruct((width, nodes), BF),
            jax.ShapeDtypeStruct((width, nodes), BF),
            jax.ShapeDtypeStruct((half, 128), F32),
            jax.ShapeDtypeStruct((half, 128), F32),
        ),
        in_specs=[
            SMEM,
            ANY,
            pl.BlockSpec((width, chunk), col),
            pl.BlockSpec((width, chunk), col),
            pl.BlockSpec((width, chunk), col),
            pl.BlockSpec((width, chunk), col),
            pl.BlockSpec((hid_all, chunk), col),
            pl.BlockSpec((hid_all, hid_all), lambda i: (0, nodes // hid_all)),
            pl.BlockSpec((hid_all, 128), lambda i: (0, (nodes + hid_all) // 128)),
            pl.BlockSpec((width, hid_all), lambda i: (0, 0)),
        ],
        out_specs=(
            pl.BlockSpec((width, chunk), col),
            pl.BlockSpec((width, chunk), col),
            pl.BlockSpec((half, 128), lambda i: (0, 0)),
            pl.BlockSpec((half, 128), lambda i: (0, 0)),
        ),
        scratch_shapes=[
            pltpu.VMEM((hid_all, chunk), BF),
            pltpu.VMEM((hid_all, chunk), BF),
            pltpu.VMEM((hid_all, hid_all), BF),
            pltpu.VMEM((hid_all, 128), F32),
            pltpu.VMEM((NC * half, 128), F32),
        ],
        name="mid",
        cost_estimate=pl.CostEstimate(
            flops=2 * nodes * hid_all * (hid_all + 2 * width),
            bytes_accessed=3 << 20,
            transcendentals=nodes * hid_all,
        ),
    )(me, after, own, low, high, far, packed, packed, packed, w_own)


def back_remote_kernel(slots_ref, g_ref, tiles_ref, _, out_ref):
    i = pl.program_id(0)
    width = g_ref.shape[0]
    count, block = tiles_ref.shape[1], tiles_ref.shape[2]

    @pl.when(i == 0)
    def _():
        out_ref[...] = jnp.zeros_like(out_ref)

    for rr in range(STEP):
        lhs = g_ref[:, rr * block : (rr + 1) * block]
        for t in range(0, count, 2):
            base = (i * STEP + rr) * count + t
            rhs = jnp.concatenate([tiles_ref[rr, t + k] for k in range(2)], axis=1)
            term = dot(lhs, rhs, (1, 0)).astype(BF)
            for k in range(2):
                slot = slots_ref[base + k]
                row = pl.multiple_of((slot % CAP) * width, width)
                out_ref[slot // CAP, pl.ds(row, width)] = term[:, k * block : (k + 1) * block]


def back_remote(slots, g, tiles, peers, after):
    row_blocks, per_block, block, _ = tiles.shape
    rem = per_block - TL
    width = g.shape[0]
    return pl.pallas_call(
        back_remote_kernel,
        grid=(row_blocks // STEP,),
        out_shape=jax.ShapeDtypeStruct((peers, CAP * width, block), BF),
        in_specs=[
            SMEM,
            pl.BlockSpec((width, STEP * block), lambda i: (0, i)),
            pl.BlockSpec((STEP, rem, block, block), lambda i: (i, 1, 0, 0)),
            ANY,
        ],
        out_specs=pl.BlockSpec((peers, CAP * width, block), lambda i: (0, 0, 0)),
        name="back_remote",
        cost_estimate=pl.CostEstimate(
            flops=2 * width * row_blocks * rem * block * block, bytes_accessed=5 << 20, transcendentals=0
        ),
    )(slots, g, tiles, after)


def back_local_kernel(cols_ref, g_ref, tiles_ref, _, out_ref):
    i = pl.program_id(0)
    count, block = tiles_ref.shape[1], tiles_ref.shape[2]

    @pl.when(i == 0)
    def _():
        out_ref[...] = jnp.zeros_like(out_ref)

    for rr in range(STEP):
        lhs = g_ref[:, rr * block : (rr + 1) * block]
        for t in range(0, count, 2):
            base = (i * STEP + rr) * count + t
            rhs = jnp.concatenate([tiles_ref[rr, t + k] for k in range(2)], axis=1)
            term = dot(lhs, rhs, (1, 0))
            for k in range(2):
                out_ref[:, lanes(cols_ref[base + k], block)] += term[:, k * block : (k + 1) * block]


def back_local(cols, g, tiles, after):
    row_blocks, _, block, _ = tiles.shape
    width = g.shape[0]
    return pl.pallas_call(
        back_local_kernel,
        grid=(row_blocks // STEP,),
        out_shape=jax.ShapeDtypeStruct(g.shape, F32),
        in_specs=[
            SMEM,
            pl.BlockSpec((width, STEP * block), lambda i: (0, i)),
            pl.BlockSpec((STEP, TL, block, block), lambda i: (i, 0, 0, 0)),
            ANY,
        ],
        out_specs=pl.BlockSpec(g.shape, lambda i: (0, 0)),
        name="back_local",
        cost_estimate=pl.CostEstimate(
            flops=2 * width * row_blocks * TL * block * block, bytes_accessed=3 << 20, transcendentals=0
        ),
    )(cols, g, tiles, after)


def finish_kernel(place_ref, wanted_ref, recv_ref, local_ref, out_ref, odd_scr):
    width, block = out_ref.shape[0], recv_ref.shape[2]
    out_ref[...] = local_ref[...]
    odd_scr[...] = jnp.zeros_like(odd_scr)

    def body(p, carry):
        back = (p // COLUMN - place_ref[0]) & (NY - 1)
        base = (p % COLUMN * NY + back) * CAP
        even = lanes(jnp.maximum(wanted_ref[base], 0), block)
        odd = lanes(jnp.maximum(wanted_ref[base + 1], 0), block)
        out_ref[:, even] += recv_ref[p, :width].astype(F32)
        odd_scr[:, odd] += recv_ref[p, width : 2 * width].astype(F32)
        return carry

    lax.fori_loop(0, recv_ref.shape[0], body, 0, unroll=4)
    out_ref[...] += odd_scr[...]


def finish(place, wanted, recv, local):
    return pl.pallas_call(
        finish_kernel,
        out_shape=jax.ShapeDtypeStruct(local.shape, F32),
        in_specs=[SMEM, SMEM, VMEM, VMEM],
        out_specs=VMEM,
        scratch_shapes=[pltpu.VMEM(local.shape, F32)],
        name="finish",
        cost_estimate=pl.CostEstimate(flops=recv.size, bytes_accessed=4 << 20, transcendentals=0),
    )(place, wanted, recv, local)


def join_kernel(a_ref, b_ref, _, out_ref):
    out_ref[...] = a_ref[...] + b_ref[...]


def join(a, b, after):
    return pl.pallas_call(
        join_kernel,
        out_shape=jax.ShapeDtypeStruct(a.shape, a.dtype),
        in_specs=[VMEM, VMEM, ANY],
        out_specs=VMEM,
        name="join",
        cost_estimate=pl.CostEstimate(flops=a.size, bytes_accessed=1 << 17, transcendentals=0),
    )(a, b, after)


def split_bf16(x, terms):
    parts = []
    for _ in range(terms):
        part = lax.reduce_precision(x, 8, 7)
        parts.append(part.astype(BF))
        x = x - part
    return parts


def local(feats, weight, bias, tile_cols, tile_values, cotangent):
    width, nodes_dev = feats.shape
    hid_all = weight.shape[1]
    block = tile_values.shape[1]
    row_blocks = nodes_dev // block
    peers = lax.axis_size("rows")
    fpeers = lax.axis_size("feat")
    per_block = tile_cols.shape[0] // row_blocks
    remote_count = row_blocks * (per_block - TL)
    place = lax.axis_index("rows")
    y, c = place // COLUMN, place % NC

    grid = tile_cols.reshape(row_blocks, per_block)
    tiles = tile_values.reshape(row_blocks, per_block, block, block)
    local_cols = (grid[:, :TL] % row_blocks).reshape(-1)
    remote_cols = grid[:, TL:].reshape(-1)
    owner = remote_cols // row_blocks
    inside = remote_cols % row_blocks
    order = jnp.arange(remote_count)
    earlier = (owner[:, None] == owner[None, :]) & (order[None, :] < order[:, None])
    rank = jnp.sum(earlier.astype(jnp.int32), axis=1)
    slots = owner * CAP + rank
    near = ((y - owner // COLUMN) & (NY - 1)) * PER + slots % PER
    hit = near[None, :] == jnp.arange(NY * PER)[:, None]
    asked = jnp.max(jnp.where(hit, inside[None, :], -1), axis=1).reshape(NY, PER)

    columns = [[y0 * COLUMN + k for k in range(COLUMN)] for y0 in range(NY)]
    column = lax.all_gather(feats, "rows", axis_index_groups=columns)
    wanted = jnp.stack([asked[0]] + [shift(asked[k], dy=-k) for k in range(1, NY)])
    held = wanted.reshape(NY, COLUMN, CAP).transpose(1, 0, 2).reshape(COLUMN, 1, NY * CAP)
    held = lax.all_to_all(held, "rows", 0, 0, tiled=True, axis_index_groups=columns)
    wanted = wanted.reshape(-1)
    agg = agg_local(local_cols, feats, tiles)

    bias_cols = jnp.pad(jnp.stack(split_bf16(bias, 3), axis=1), ((0, 0), (0, 125)))
    packed = jnp.concatenate([cotangent, weight, bias_cols], axis=1)
    packed = lax.all_gather(packed, "feat", axis=0, tiled=True)

    away = pack(range(1, NY), wanted, column, block, [held, agg])
    parts = pack((0,), wanted, column, block, [away[0]])
    parts = list(parts) + [shift(blocks, dy=k) for k, blocks in enumerate(away, 1)]
    agg = agg_remote(near, parts, tiles, agg)

    pieces = [agg] + [
        lax.ppermute(agg, "feat", [(k, (k + s) % fpeers) for k in range(fpeers)]) for s in (1, 3, 2)
    ]
    me = jnp.stack([lax.axis_index("feat"), c]).astype(jnp.int32)
    hidden_out, g, keep, give = mid(me, pieces, packed, weight, held)

    send = back_remote(slots, g, tiles, peers, keep)
    recv = lax.all_to_all(send, "rows", split_axis=0, concat_axis=0, tiled=True)
    own = back_local(local_cols, g, tiles, send)

    own, keep, give = lax.optimization_barrier((own, keep, give))
    part = keep + shift(give, dc=1)
    pairs = [part] + [shift(part, flip_y=k) for k in (1, 2, 3)]
    part = (pairs[0] + pairs[1]) + (pairs[2] + pairs[3])
    part = join(part, shift(part, flip_z=1), recv)
    pairs = [part] + [shift(part, flip_z=k) for k in (2, 4, 6)]
    part = (pairs[0] + pairs[1]) + (pairs[2] + pairs[3])
    other = shift(part, dc=1)
    total = jnp.where(c == 0, jnp.concatenate([part, other]), jnp.concatenate([other, part]))
    total = total / math.sqrt(nodes_dev * peers)
    grad_w = jnp.concatenate([total[k * width : (k + 1) * width] for k in range(hid_all // 128)], axis=1)
    grad_b = jnp.sum(total[-width:], axis=1)

    grad_input = finish(y.reshape(1), held.reshape(-1), recv, own)
    return hidden_out, grad_input, grad_w, grad_b


def solution(mesh):
    placed = (
        P("feat", "rows"),
        P("feat", None),
        P("feat"),
        P("rows"),
        P("rows", None, None),
        P("feat", "rows"),
    )
    return jax.shard_map(
        local,
        mesh=mesh,
        in_specs=placed,
        out_specs=(P("feat", "rows"), P("feat", "rows"), P("feat", None), P("feat")),
        check_vma=False,
    )
```

```python
import functools
import math

import jax
import jax.numpy as jnp
from jax import lax
from jax.experimental import pallas as pl
from jax.experimental.pallas import tpu as pltpu
from jax.sharding import PartitionSpec as P

TL = 4
BF = jnp.bfloat16
F32 = jnp.float32
VMEM = pl.BlockSpec(memory_space=pltpu.VMEM)
ANY = pl.BlockSpec(memory_space=pl.ANY)
SMEM = pl.BlockSpec(memory_space=pltpu.SMEM)


def lanes(index, width):
    return pl.ds(pl.multiple_of(index * width, width), width)


NY, NZ, NC = 4, 8, 2
CAP = 2
TAIL = 16
ORDER = (0, 1, 7, 2, 6, 3, 5, 4)
GROUPS = ((0, 3), (3, 5), (5, 8))
PER = NZ * CAP


def shift(x, dy=0, dz=0, dc=0, flip_y=0, flip_z=0):
    pairs = []
    for y in range(NY):
        for z in range(NZ):
            for c in range(NC):
                to_y, to_z = ((y ^ flip_y) + dy) % NY, ((z ^ flip_z) + dz) % NZ
                pairs.append(((y * NZ + z) * NC + c, (to_y * NZ + to_z) * NC + (c + dc) % NC))
    return lax.ppermute(x, "rows", pairs)


def pack_kernel(first, count, split, *refs):
    wanted_ref, sources, outs = refs[0], refs[1 : 1 + count + split], refs[-NY:]
    width, block = outs[0].shape[2], outs[0].shape[3]
    for ys in range(NY):
        for cs in range(NC):
            for q in range(count * CAP):
                w = wanted_ref[(ys * NC + cs) * PER + first * CAP + q]
                where = lanes(jnp.maximum(w, 0), block)
                j = q // CAP
                if split and j == count - 1:
                    outs[ys][cs, q, : width // 2] = sources[j][:, where]
                    outs[ys][cs, q, width // 2 :] = sources[j + 1][:, where]
                else:
                    outs[ys][cs, q] = sources[j][:, where]


def pack(group, wanted, sources, block, after):
    first, last = group
    count = last - first
    width = sources[0].shape[0]
    shape = jax.ShapeDtypeStruct((NC, count * CAP, width, block), BF)
    return pl.pallas_call(
        functools.partial(pack_kernel, first, count, len(sources) > count),
        out_shape=[shape] * NY,
        in_specs=[SMEM] + [VMEM] * len(sources) + [ANY] * len(after),
        out_specs=[VMEM] * NY,
        name="pack",
        cost_estimate=pl.CostEstimate(flops=0, bytes_accessed=3 << 20, transcendentals=0),
    )(wanted, *sources, *after)


def dot(a, b, dims):
    return lax.dot_general(a, b, ((dims[:1], dims[1:]), ((), ())), preferred_element_type=F32)


STEP = 4


def agg_local_kernel(cols_ref, feats_ref, tiles_ref, out_ref):
    i = pl.program_id(0)
    count, block = tiles_ref.shape[1], tiles_ref.shape[2]
    for rr in range(STEP):
        acc = None
        for t in range(0, count, 2):
            base = (i * STEP + rr) * count + t
            lhs = jnp.concatenate(
                [feats_ref[:, lanes(cols_ref[base + k], block)] for k in range(2)], axis=1
            )
            rhs = jnp.concatenate([tiles_ref[rr, t + k] for k in range(2)], axis=1)
            term = dot(lhs, rhs, (1, 1))
            acc = term if acc is None else acc + term
        out_ref[:, rr * block : (rr + 1) * block] = acc


def agg_local(cols, feats, tiles):
    row_blocks, _, block, _ = tiles.shape
    width = feats.shape[0]
    return pl.pallas_call(
        agg_local_kernel,
        grid=(row_blocks // STEP,),
        out_shape=jax.ShapeDtypeStruct((width, row_blocks * block), F32),
        in_specs=[
            SMEM,
            pl.BlockSpec(feats.shape, lambda i: (0, 0)),
            pl.BlockSpec((STEP, TL, block, block), lambda i: (i, 0, 0, 0)),
        ],
        out_specs=pl.BlockSpec((width, STEP * block), lambda i: (0, i)),
        name="agg_local",
        cost_estimate=pl.CostEstimate(
            flops=2 * width * row_blocks * TL * block * block, bytes_accessed=3 << 20, transcendentals=0
        ),
    )(cols, feats, tiles)


def agg_remote_kernel(slots_ref, held_ref, tiles_ref, local_ref, *refs):
    parts, out_ref, held_out_ref, recv_ref = refs[:-3], refs[-3], refs[-2], refs[-1]
    i = pl.program_id(0)
    count, block = tiles_ref.shape[1], tiles_ref.shape[2]

    @pl.when(i == 0)
    def _():
        held_out_ref[...] = held_ref[...]
        n = 0
        for first, last in GROUPS:
            size = (last - first) * CAP
            for ys in range(NY):
                recv_ref[pl.ds(ys * PER + first * CAP, size)] = parts[n + ys][0]
                recv_ref[pl.ds((NY + ys) * PER + first * CAP, size)] = parts[n + NY][ys]
            n += NY + 1

    for rr in range(STEP):
        acc = local_ref[:, rr * block : (rr + 1) * block]
        for t in range(0, count, 2):
            base = (i * STEP + rr) * count + t
            lhs = jnp.concatenate([recv_ref[slots_ref[base + k]] for k in range(2)], axis=1)
            rhs = jnp.concatenate([tiles_ref[rr, t + k] for k in range(2)], axis=1)
            acc = acc + dot(lhs, rhs, (1, 1))
        out_ref[:, rr * block : (rr + 1) * block] = acc.astype(out_ref.dtype)


def agg_remote(slots, held, parts, tiles, local):
    row_blocks, per_block, block, _ = tiles.shape
    rem = per_block - TL
    width = local.shape[0]
    specs = []
    for n, part in enumerate(parts):
        lead = 1 if n % (NY + 1) < NY else NY
        specs.append(pl.BlockSpec((lead,) + part.shape[1:], lambda i: (0, 0, 0, 0)))
    return pl.pallas_call(
        agg_remote_kernel,
        grid=(row_blocks // STEP,),
        out_shape=(jax.ShapeDtypeStruct(local.shape, BF), jax.ShapeDtypeStruct(held.shape, held.dtype)),
        in_specs=[
            SMEM,
            pl.BlockSpec(held.shape, lambda i: (0, 0, 0)),
            pl.BlockSpec((STEP, rem, block, block), lambda i: (i, 1, 0, 0)),
            pl.BlockSpec((width, STEP * block), lambda i: (0, i)),
        ]
        + specs,
        out_specs=(
            pl.BlockSpec((width, STEP * block), lambda i: (0, i)),
            pl.BlockSpec(held.shape, lambda i: (0, 0, 0)),
        ),
        scratch_shapes=[pltpu.VMEM((NY * NC * PER, width, block), BF)],
        name="agg_remote",
        cost_estimate=pl.CostEstimate(
            flops=2 * width * row_blocks * rem * block * block, bytes_accessed=5 << 20, transcendentals=0
        ),
    )(slots, held, tiles, local, *parts)


def mid_kernel(
    me_ref,
    _,
    own_ref,
    low_ref,
    high_ref,
    far_ref,
    cot_ref,
    w_ref,
    bias_ref,
    wown_ref,
    hid_ref,
    g_ref,
    keep_ref,
    give_ref,
    agg_scr,
    hid_scr,
    wt_scr,
    gb_scr,
    sums_scr,
):
    i = pl.program_id(0)
    width = own_ref.shape[0]
    count = agg_scr.shape[0] // width
    me = me_ref[0]

    def rows(ahead):
        return pl.ds(pl.multiple_of(lax.rem(me + ahead, count) * width, width), width)

    @pl.when(i == 0)
    def _():
        wt_scr[...] = w_ref[...].astype(F32).T.astype(BF)
        sums_scr[...] = jnp.zeros_like(sums_scr)
        gb_scr[...] = jnp.zeros_like(gb_scr)

    agg_scr[rows(3)] = low_ref[...]
    agg_scr[rows(1)] = high_ref[...]
    agg_scr[rows(2)] = far_ref[...]
    agg_scr[rows(0)] = own_ref[...]
    pre = dot(wt_scr[...], agg_scr[...], (1, 0))
    bias = bias_ref[:, :3].astype(F32)
    pre = pre + ((bias[:, 2:3] + bias[:, 1:2]) + bias[:, 0:1])
    sigma = jax.nn.sigmoid(pre)
    hid_scr[...] = (pre * sigma).astype(BF)
    hid_ref[...] = hid_scr[rows(0)]
    grad_pre = cot_ref[...].astype(F32) * (sigma * (1.0 + pre * (1.0 - sigma)))
    total = grad_pre[:, :128]
    for k in range(1, grad_pre.shape[1] // 128):
        total = total + grad_pre[:, k * 128 : (k + 1) * 128]
    gb_scr[...] += total
    grad_b = grad_pre.astype(BF)
    g_ref[...] = dot(wown_ref[...], grad_b, (1, 0)).astype(BF)
    grad_w = dot(own_ref[...], grad_b, (1, 1))
    for k in range(grad_w.shape[1] // 128):
        sums_scr[k * width : (k + 1) * width] += grad_w[:, k * 128 : (k + 1) * 128]

    @pl.when(i == pl.num_programs(0) - 1)
    def _():
        half = keep_ref.shape[0]
        own = gb_scr[rows(0)]
        sums_scr[2 * half - TAIL : 2 * half - TAIL + 1, :width] = jnp.sum(own.T, axis=0, keepdims=True)
        keep_ref[...] = sums_scr[pl.ds(pl.multiple_of(me_ref[1] * half, half), half)]
        give_ref[...] = sums_scr[pl.ds(pl.multiple_of((1 - me_ref[1]) * half, half), half)]


def mid(me, pieces, packed, w_own, after):
    own, low, high, far = pieces
    width, nodes = own.shape
    hid_all = packed.shape[0]
    chunk = 512
    half = (width * (hid_all // 128) + TAIL) // NC
    col = lambda i: (0, i)
    return pl.pallas_call(
        mid_kernel,
        grid=(nodes // chunk,),
        out_shape=(
            jax.ShapeDtypeStruct((width, nodes), BF),
            jax.ShapeDtypeStruct((width, nodes), BF),
            jax.ShapeDtypeStruct((half, 128), F32),
            jax.ShapeDtypeStruct((half, 128), F32),
        ),
        in_specs=[
            SMEM,
            ANY,
            pl.BlockSpec((width, chunk), col),
            pl.BlockSpec((width, chunk), col),
            pl.BlockSpec((width, chunk), col),
            pl.BlockSpec((width, chunk), col),
            pl.BlockSpec((hid_all, chunk), col),
            pl.BlockSpec((hid_all, hid_all), lambda i: (0, nodes // hid_all)),
            pl.BlockSpec((hid_all, 128), lambda i: (0, (nodes + hid_all) // 128)),
            pl.BlockSpec((width, hid_all), lambda i: (0, 0)),
        ],
        out_specs=(
            pl.BlockSpec((width, chunk), col),
            pl.BlockSpec((width, chunk), col),
            pl.BlockSpec((half, 128), lambda i: (0, 0)),
            pl.BlockSpec((half, 128), lambda i: (0, 0)),
        ),
        scratch_shapes=[
            pltpu.VMEM((hid_all, chunk), BF),
            pltpu.VMEM((hid_all, chunk), BF),
            pltpu.VMEM((hid_all, hid_all), BF),
            pltpu.VMEM((hid_all, 128), F32),
            pltpu.VMEM((NC * half, 128), F32),
        ],
        name="mid",
        cost_estimate=pl.CostEstimate(
            flops=2 * nodes * hid_all * (hid_all + 2 * width),
            bytes_accessed=3 << 20,
            transcendentals=nodes * hid_all,
        ),
    )(me, after, own, low, high, far, packed, packed, packed, w_own)


def back_remote_kernel(slots_ref, g_ref, tiles_ref, _, out_ref):
    i = pl.program_id(0)
    width = g_ref.shape[0]
    count, block = tiles_ref.shape[1], tiles_ref.shape[2]

    @pl.when(i == 0)
    def _():
        out_ref[...] = jnp.zeros_like(out_ref)

    for rr in range(STEP):
        lhs = g_ref[:, rr * block : (rr + 1) * block]
        for t in range(0, count, 2):
            base = (i * STEP + rr) * count + t
            rhs = jnp.concatenate([tiles_ref[rr, t + k] for k in range(2)], axis=1)
            term = dot(lhs, rhs, (1, 0)).astype(BF)
            for k in range(2):
                slot = slots_ref[base + k]
                row = pl.multiple_of((slot % CAP) * width, width)
                out_ref[slot // CAP, pl.ds(row, width)] = term[:, k * block : (k + 1) * block]


def back_remote(slots, g, tiles, peers, after):
    row_blocks, per_block, block, _ = tiles.shape
    rem = per_block - TL
    width = g.shape[0]
    return pl.pallas_call(
        back_remote_kernel,
        grid=(row_blocks // STEP,),
        out_shape=jax.ShapeDtypeStruct((peers, CAP * width, block), BF),
        in_specs=[
            SMEM,
            pl.BlockSpec((width, STEP * block), lambda i: (0, i)),
            pl.BlockSpec((STEP, rem, block, block), lambda i: (i, 1, 0, 0)),
            ANY,
        ],
        out_specs=pl.BlockSpec((peers, CAP * width, block), lambda i: (0, 0, 0)),
        name="back_remote",
        cost_estimate=pl.CostEstimate(
            flops=2 * width * row_blocks * rem * block * block, bytes_accessed=5 << 20, transcendentals=0
        ),
    )(slots, g, tiles, after)


def back_local_kernel(cols_ref, g_ref, tiles_ref, _, out_ref):
    i = pl.program_id(0)
    count, block = tiles_ref.shape[1], tiles_ref.shape[2]

    @pl.when(i == 0)
    def _():
        out_ref[...] = jnp.zeros_like(out_ref)

    for rr in range(STEP):
        lhs = g_ref[:, rr * block : (rr + 1) * block]
        for t in range(0, count, 2):
            base = (i * STEP + rr) * count + t
            rhs = jnp.concatenate([tiles_ref[rr, t + k] for k in range(2)], axis=1)
            term = dot(lhs, rhs, (1, 0))
            for k in range(2):
                out_ref[:, lanes(cols_ref[base + k], block)] += term[:, k * block : (k + 1) * block]


def back_local(cols, g, tiles, after):
    row_blocks, _, block, _ = tiles.shape
    width = g.shape[0]
    return pl.pallas_call(
        back_local_kernel,
        grid=(row_blocks // STEP,),
        out_shape=jax.ShapeDtypeStruct(g.shape, F32),
        in_specs=[
            SMEM,
            pl.BlockSpec((width, STEP * block), lambda i: (0, i)),
            pl.BlockSpec((STEP, TL, block, block), lambda i: (i, 0, 0, 0)),
            ANY,
        ],
        out_specs=pl.BlockSpec(g.shape, lambda i: (0, 0)),
        name="back_local",
        cost_estimate=pl.CostEstimate(
            flops=2 * width * row_blocks * TL * block * block, bytes_accessed=3 << 20, transcendentals=0
        ),
    )(cols, g, tiles, after)


STREAMS = 4


def finish_kernel(place_ref, held_ref, recv_ref, local_ref, out_ref, odd_scr, recv_scr, sems):
    width, block = out_ref.shape[0], recv_scr.shape[2]
    count = recv_scr.shape[0] // STREAMS

    def stream(n):
        part = pl.ds(n * count, count)
        return pltpu.make_async_copy(recv_ref.at[part], recv_scr.at[part], sems.at[n])

    for n in range(STREAMS):
        stream(n).start()
    out_ref[...] = local_ref[...]
    odd_scr[...] = jnp.zeros_like(odd_scr)
    for n in range(STREAMS):
        stream(n).wait()

        def body(p, carry):
            back = (p // (NZ * NC) - place_ref[0]) & (NY - 1)
            base = (back * NC + ((p ^ place_ref[1]) & 1)) * CAP
            z = p // NC % NZ
            even = lanes(jnp.maximum(held_ref[z, 0, base], 0), block)
            odd = lanes(jnp.maximum(held_ref[z, 0, base + 1], 0), block)
            out_ref[:, even] += recv_scr[p, :width].astype(F32)
            odd_scr[:, odd] += recv_scr[p, width : 2 * width].astype(F32)
            return carry

        lax.fori_loop(n * count, (n + 1) * count, body, 0, unroll=4)
    out_ref[...] += odd_scr[...]


def finish(place, held, recv, local):
    return pl.pallas_call(
        finish_kernel,
        out_shape=jax.ShapeDtypeStruct(local.shape, F32),
        in_specs=[SMEM, SMEM, ANY, VMEM],
        out_specs=VMEM,
        scratch_shapes=[
            pltpu.VMEM(local.shape, F32),
            pltpu.VMEM(recv.shape, recv.dtype),
            pltpu.SemaphoreType.DMA((STREAMS,)),
        ],
        name="finish",
        compiler_params=pltpu.CompilerParams(vmem_limit_bytes=16 << 20),
        cost_estimate=pl.CostEstimate(flops=recv.size, bytes_accessed=4 << 20, transcendentals=0),
    )(place, held, recv, local)


def split_bf16(x, terms):
    parts = []
    for _ in range(terms):
        part = lax.reduce_precision(x, 8, 7)
        parts.append(part.astype(BF))
        x = x - part
    return parts


def local(feats, weight, bias, tile_cols, tile_values, cotangent):
    width, nodes_dev = feats.shape
    hid_all = weight.shape[1]
    block = tile_values.shape[1]
    row_blocks = nodes_dev // block
    peers = lax.axis_size("rows")
    fpeers = lax.axis_size("feat")
    per_block = tile_cols.shape[0] // row_blocks
    remote_count = row_blocks * (per_block - TL)
    place = lax.axis_index("rows")
    y, z, c = place // (NZ * NC), place // NC % NZ, place % NC

    grid = tile_cols.reshape(row_blocks, per_block)
    tiles = tile_values.reshape(row_blocks, per_block, block, block)
    local_cols = (grid[:, :TL] % row_blocks).reshape(-1)
    remote_cols = grid[:, TL:].reshape(-1)
    owner = remote_cols // row_blocks
    inside = remote_cols % row_blocks
    order = jnp.arange(remote_count)
    earlier = (owner[:, None] == owner[None, :]) & (order[None, :] < order[:, None])
    rank = jnp.sum(earlier.astype(jnp.int32), axis=1)
    slots = owner * CAP + rank
    ahead = (owner // NC - z) & (NZ - 1)

    def place_of(ahead):
        return jnp.maximum(jnp.where(ahead <= NZ // 2, 2 * ahead - 1, 2 * (NZ - ahead)), 0)

    pos = place_of(ahead)
    back = (y - owner // (NZ * NC)) & (NY - 1)
    other = (owner ^ c) & 1
    near = ((other * NY + back) * NZ + pos) * CAP + rank

    def table(index):
        hit = index[None, :] == jnp.arange(peers * CAP)[:, None]
        return jnp.max(jnp.where(hit, inside[None, :], -1), axis=1)

    asked = table(near).reshape(NC, NY, PER)
    asked = jnp.stack([asked[0], shift(asked[1], dc=1)], axis=1)
    wanted = [asked[0]] + [shift(asked[ys], dy=-ys) for ys in range(1, NY)]
    wanted = jnp.stack(wanted).reshape(-1)

    up, down, parts = [feats], [feats], []
    for k in range(1, NZ // 2):
        up.append(shift(up[-1], dz=1))
        down.append(shift(down[-1], dz=-1))
    far_up = shift(up[-1][: width // 2], dz=1)
    far_down = shift(down[-1][width // 2 :], dz=-1)
    groups = ((feats, down[1], up[1]), (down[2], up[2]), (down[3], up[3], far_up, far_down))
    after = []
    agg = agg_local(local_cols, feats, tiles)
    for group, sources in zip(GROUPS, groups):
        packs = pack(group, wanted, sources, block, after)
        after = [packs[0], agg]
        moved = [packs[0]] + [shift(packs[ys], dy=ys) for ys in range(1, NY)]
        parts += moved
        parts.append(shift(jnp.concatenate([m[1:] for m in moved]), dc=1))

    bias_cols = jnp.pad(jnp.stack(split_bf16(bias, 3), axis=1), ((0, 0), (0, 125)))
    packed = jnp.concatenate([cotangent, weight, bias_cols], axis=1)
    packed = lax.all_gather(packed, "feat", axis=0, tiled=True)

    by_owner = wanted.reshape(NY * NC, NZ, CAP)
    steps = (jnp.arange(NZ) - z) & (NZ - 1)
    match = (place_of(steps)[:, None] == jnp.arange(NZ)[None, :])[:, None, :, None]
    held = jnp.sum(jnp.where(match, by_owner[None], 0), axis=2).reshape(NZ, 1, NY * NC * CAP)
    agg, held = agg_remote(near, held, parts, tiles, agg)

    pieces = [agg] + [
        lax.ppermute(agg, "feat", [(k, (k + s) % fpeers) for k in range(fpeers)]) for s in (1, 3, 2)
    ]
    along_z = [[(y0 * NZ + z0) * NC + c0 for z0 in range(NZ)] for y0 in range(NY) for c0 in range(NC)]
    held = lax.all_to_all(held, "rows", 0, 0, tiled=True, axis_index_groups=along_z)

    me = jnp.stack([lax.axis_index("feat"), c]).astype(jnp.int32)
    hidden_out, g, keep, give = mid(me, pieces, packed, weight, held)

    part = keep + shift(give, dc=1)
    twin = shift(part, flip_z=1)
    send = back_remote(slots, g, tiles, peers, part)
    send, twin = lax.optimization_barrier((send, twin))
    recv = lax.all_to_all(send, "rows", split_axis=0, concat_axis=0, tiled=True)
    own = back_local(local_cols, g, tiles, send)
    own, part, twin = lax.optimization_barrier((own, part, twin))
    part = part + twin
    pairs = [part] + [shift(part, flip_y=k) for k in (1, 2, 3)]
    part = (pairs[0] + pairs[1]) + (pairs[2] + pairs[3])
    pairs = [part] + [shift(part, flip_z=k) for k in (2, 4, 6)]
    part = (pairs[0] + pairs[1]) + (pairs[2] + pairs[3])
    other = shift(part, dc=1)
    total = jnp.where(c == 0, jnp.concatenate([part, other]), jnp.concatenate([other, part]))
    total = total / math.sqrt(nodes_dev * peers)
    grad_w = jnp.concatenate([total[k * width : (k + 1) * width] for k in range(hid_all // 128)], axis=1)
    grad_b = total[width * (hid_all // 128), :width]

    grad_input = finish(jnp.stack([y, c]).astype(jnp.int32), held, recv, own)
    return hidden_out, grad_input, grad_w, grad_b


def solution(mesh):
    placed = (
        P("feat", "rows"),
        P("feat", None),
        P("feat"),
        P("rows"),
        P("rows", None, None),
        P("feat", "rows"),
    )
    return jax.shard_map(
        local,
        mesh=mesh,
        in_specs=placed,
        out_specs=(P("feat", "rows"), P("feat", "rows"), P("feat", None), P("feat")),
        check_vma=False,
    )
```

```python
import functools
import math

import jax
import jax.numpy as jnp
from jax import lax
from jax.experimental import pallas as pl
from jax.experimental.pallas import tpu as pltpu
from jax.sharding import PartitionSpec as P

TL = 4
BF = jnp.bfloat16
F32 = jnp.float32
VMEM = pl.BlockSpec(memory_space=pltpu.VMEM)
ANY = pl.BlockSpec(memory_space=pl.ANY)
SMEM = pl.BlockSpec(memory_space=pltpu.SMEM)


def lanes(index, width):
    return pl.ds(pl.multiple_of(index * width, width), width)


NY, NZ, NC = 4, 8, 2
CAP = 2
TAIL = 16
ORDER = (0, 1, 7, 2, 6, 3, 5, 4)
GROUPS = ((0, 3), (3, 5), (5, 8))
PER = NZ * CAP


def shift(x, dy=0, dz=0, dc=0, flip_y=0, flip_z=0):
    pairs = []
    for y in range(NY):
        for z in range(NZ):
            for c in range(NC):
                to_y, to_z = ((y ^ flip_y) + dy) % NY, ((z ^ flip_z) + dz) % NZ
                pairs.append(((y * NZ + z) * NC + c, (to_y * NZ + to_z) * NC + (c + dc) % NC))
    return lax.ppermute(x, "rows", pairs)


def pack_kernel(first, count, split, *refs):
    wanted_ref, sources, outs = refs[0], refs[1 : 1 + count + split], refs[-NY:]
    width, block = outs[0].shape[2], outs[0].shape[3]
    for ys in range(NY):
        for cs in range(NC):
            for q in range(count * CAP):
                w = wanted_ref[(ys * NC + cs) * PER + first * CAP + q]
                where = lanes(jnp.maximum(w, 0), block)
                j = q // CAP
                if split and j == count - 1:
                    outs[ys][cs, q, : width // 2] = sources[j][:, where]
                    outs[ys][cs, q, width // 2 :] = sources[j + 1][:, where]
                else:
                    outs[ys][cs, q] = sources[j][:, where]


def pack(group, wanted, sources, block, after):
    first, last = group
    count = last - first
    width = sources[0].shape[0]
    shape = jax.ShapeDtypeStruct((NC, count * CAP, width, block), BF)
    return pl.pallas_call(
        functools.partial(pack_kernel, first, count, len(sources) > count),
        out_shape=[shape] * NY,
        in_specs=[SMEM] + [VMEM] * len(sources) + [ANY] * len(after),
        out_specs=[VMEM] * NY,
        name="pack",
        cost_estimate=pl.CostEstimate(flops=0, bytes_accessed=3 << 20, transcendentals=0),
    )(wanted, *sources, *after)


def dot(a, b, dims):
    return lax.dot_general(a, b, ((dims[:1], dims[1:]), ((), ())), preferred_element_type=F32)


STEP = 4


def agg_local_kernel(cols_ref, asked_ref, feats_ref, tiles_ref, out_ref, own_ref, other_ref):
    i = pl.program_id(0)
    count, block = tiles_ref.shape[1], tiles_ref.shape[2]
    own_ref[...] = asked_ref[0]
    other_ref[...] = asked_ref[1]
    for rr in range(STEP):
        acc = None
        for t in range(0, count, 2):
            base = (i * STEP + rr) * count + t
            lhs = jnp.concatenate(
                [feats_ref[:, lanes(cols_ref[base + k], block)] for k in range(2)], axis=1
            )
            rhs = jnp.concatenate([tiles_ref[rr, t + k] for k in range(2)], axis=1)
            term = dot(lhs, rhs, (1, 1))
            acc = term if acc is None else acc + term
        out_ref[:, rr * block : (rr + 1) * block] = acc


def agg_local(cols, asked, feats, tiles):
    row_blocks, _, block, _ = tiles.shape
    width = feats.shape[0]
    return pl.pallas_call(
        agg_local_kernel,
        grid=(row_blocks // STEP,),
        out_shape=(
            jax.ShapeDtypeStruct((width, row_blocks * block), F32),
            jax.ShapeDtypeStruct(asked.shape[1:], asked.dtype),
            jax.ShapeDtypeStruct(asked.shape[1:], asked.dtype),
        ),
        in_specs=[
            SMEM,
            pl.BlockSpec(asked.shape, lambda i: (0, 0, 0)),
            pl.BlockSpec(feats.shape, lambda i: (0, 0)),
            pl.BlockSpec((STEP, TL, block, block), lambda i: (i, 0, 0, 0)),
        ],
        out_specs=(
            pl.BlockSpec((width, STEP * block), lambda i: (0, i)),
            pl.BlockSpec(asked.shape[1:], lambda i: (0, 0)),
            pl.BlockSpec(asked.shape[1:], lambda i: (0, 0)),
        ),
        name="agg_local",
        cost_estimate=pl.CostEstimate(
            flops=2 * width * row_blocks * TL * block * block, bytes_accessed=3 << 20, transcendentals=0
        ),
    )(cols, asked, feats, tiles)


def agg_remote_kernel(slots_ref, held_ref, tiles_ref, local_ref, *refs):
    parts, out_ref, held_out_ref, recv_ref, sems = refs[:-4], refs[-4], refs[-3], refs[-2], refs[-1]
    i = pl.program_id(0)
    count, block = tiles_ref.shape[1], tiles_ref.shape[2]

    @pl.when(i == 0)
    def _():
        copies = []
        for g, (first, last) in enumerate(GROUPS):
            size = (last - first) * CAP
            own, other = parts[g * (NY + 1) : g * (NY + 1) + NY], parts[g * (NY + 1) + NY]
            sources = [ref.at[0] for ref in own] + [other.at[ys] for ys in range(NY)]
            for k, source in enumerate(sources):
                target = recv_ref.at[pl.ds(k * PER + first * CAP, size)]
                copies.append(pltpu.make_async_copy(source, target, sems.at[len(copies)]))
        for copy in copies:
            copy.start()
        held_out_ref[...] = held_ref[...]
        for copy in copies:
            copy.wait()

    for rr in range(STEP):
        acc = local_ref[:, rr * block : (rr + 1) * block]
        for t in range(0, count, 2):
            base = (i * STEP + rr) * count + t
            lhs = jnp.concatenate([recv_ref[slots_ref[base + k]] for k in range(2)], axis=1)
            rhs = jnp.concatenate([tiles_ref[rr, t + k] for k in range(2)], axis=1)
            acc = acc + dot(lhs, rhs, (1, 1))
        out_ref[:, rr * block : (rr + 1) * block] = acc.astype(out_ref.dtype)


def agg_remote(slots, held, parts, tiles, local):
    row_blocks, per_block, block, _ = tiles.shape
    rem = per_block - TL
    width = local.shape[0]
    return pl.pallas_call(
        agg_remote_kernel,
        grid=(row_blocks // STEP,),
        out_shape=(jax.ShapeDtypeStruct(local.shape, BF), jax.ShapeDtypeStruct(held.shape, held.dtype)),
        in_specs=[
            SMEM,
            pl.BlockSpec(held.shape, lambda i: (0, 0, 0)),
            pl.BlockSpec((STEP, rem, block, block), lambda i: (i, 1, 0, 0)),
            pl.BlockSpec((width, STEP * block), lambda i: (0, i)),
        ]
        + [ANY] * len(parts),
        out_specs=(
            pl.BlockSpec((width, STEP * block), lambda i: (0, i)),
            pl.BlockSpec(held.shape, lambda i: (0, 0, 0)),
        ),
        scratch_shapes=[
            pltpu.VMEM((NY * NC * PER, width, block), BF),
            pltpu.SemaphoreType.DMA((len(GROUPS) * NY * NC,)),
        ],
        name="agg_remote",
        compiler_params=pltpu.CompilerParams(vmem_limit_bytes=49 << 20),
        cost_estimate=pl.CostEstimate(
            flops=2 * width * row_blocks * rem * block * block, bytes_accessed=5 << 20, transcendentals=0
        ),
    )(slots, held, tiles, local, *parts)


def mid_kernel(
    me_ref,
    _,
    own_ref,
    low_ref,
    high_ref,
    far_ref,
    cot_ref,
    w_ref,
    bias_ref,
    wown_ref,
    hid_ref,
    g_ref,
    keep_ref,
    give_ref,
    agg_scr,
    hid_scr,
    wt_scr,
    gb_scr,
    sums_scr,
):
    i = pl.program_id(0)
    width = own_ref.shape[0]
    count = agg_scr.shape[0] // width
    me = me_ref[0]

    def rows(ahead):
        return pl.ds(pl.multiple_of(lax.rem(me + ahead, count) * width, width), width)

    @pl.when(i == 0)
    def _():
        wt_scr[...] = w_ref[...].astype(F32).T.astype(BF)
        sums_scr[...] = jnp.zeros_like(sums_scr)
        gb_scr[...] = jnp.zeros_like(gb_scr)

    agg_scr[rows(3)] = low_ref[...]
    agg_scr[rows(1)] = high_ref[...]
    agg_scr[rows(2)] = far_ref[...]
    agg_scr[rows(0)] = own_ref[...]
    pre = dot(wt_scr[...], agg_scr[...], (1, 0))
    bias = bias_ref[:, :3].astype(F32)
    pre = pre + ((bias[:, 2:3] + bias[:, 1:2]) + bias[:, 0:1])
    sigma = jax.nn.sigmoid(pre)
    hid_scr[...] = (pre * sigma).astype(BF)
    hid_ref[...] = hid_scr[rows(0)]
    grad_pre = cot_ref[...].astype(F32) * (sigma * (1.0 + pre * (1.0 - sigma)))
    total = grad_pre[:, :128]
    for k in range(1, grad_pre.shape[1] // 128):
        total = total + grad_pre[:, k * 128 : (k + 1) * 128]
    gb_scr[...] += total
    grad_b = grad_pre.astype(BF)
    g_ref[...] = dot(wown_ref[...], grad_b, (1, 0)).astype(BF)
    grad_w = dot(own_ref[...], grad_b, (1, 1))
    for k in range(grad_w.shape[1] // 128):
        sums_scr[k * width : (k + 1) * width] += grad_w[:, k * 128 : (k + 1) * 128]

    @pl.when(i == pl.num_programs(0) - 1)
    def _():
        half = keep_ref.shape[0]
        own = gb_scr[rows(0)]
        sums_scr[2 * half - TAIL : 2 * half - TAIL + 1, :width] = jnp.sum(own.T, axis=0, keepdims=True)
        keep_ref[...] = sums_scr[pl.ds(pl.multiple_of(me_ref[1] * half, half), half)]
        give_ref[...] = sums_scr[pl.ds(pl.multiple_of((1 - me_ref[1]) * half, half), half)]


def mid(me, pieces, packed, w_own, after):
    own, low, high, far = pieces
    width, nodes = own.shape
    hid_all = packed.shape[0]
    chunk = 512
    half = (width * (hid_all // 128) + TAIL) // NC
    col = lambda i: (0, i)
    return pl.pallas_call(
        mid_kernel,
        grid=(nodes // chunk,),
        out_shape=(
            jax.ShapeDtypeStruct((width, nodes), BF),
            jax.ShapeDtypeStruct((width, nodes), BF),
            jax.ShapeDtypeStruct((half, 128), F32),
            jax.ShapeDtypeStruct((half, 128), F32),
        ),
        in_specs=[
            SMEM,
            ANY,
            pl.BlockSpec((width, chunk), col),
            pl.BlockSpec((width, chunk), col),
            pl.BlockSpec((width, chunk), col),
            pl.BlockSpec((width, chunk), col),
            pl.BlockSpec((hid_all, chunk), col),
            pl.BlockSpec((hid_all, hid_all), lambda i: (0, nodes // hid_all)),
            pl.BlockSpec((hid_all, 128), lambda i: (0, (nodes + hid_all) // 128)),
            pl.BlockSpec((width, hid_all), lambda i: (0, 0)),
        ],
        out_specs=(
            pl.BlockSpec((width, chunk), col),
            pl.BlockSpec((width, chunk), col),
            pl.BlockSpec((half, 128), lambda i: (0, 0)),
            pl.BlockSpec((half, 128), lambda i: (0, 0)),
        ),
        scratch_shapes=[
            pltpu.VMEM((hid_all, chunk), BF),
            pltpu.VMEM((hid_all, chunk), BF),
            pltpu.VMEM((hid_all, hid_all), BF),
            pltpu.VMEM((hid_all, 128), F32),
            pltpu.VMEM((NC * half, 128), F32),
        ],
        name="mid",
        cost_estimate=pl.CostEstimate(
            flops=2 * nodes * hid_all * (hid_all + 2 * width),
            bytes_accessed=3 << 20,
            transcendentals=nodes * hid_all,
        ),
    )(me, after, own, low, high, far, packed, packed, packed, w_own)


def back_remote_kernel(slots_ref, g_ref, tiles_ref, _, out_ref):
    i = pl.program_id(0)
    width = g_ref.shape[0]
    count, block = tiles_ref.shape[1], tiles_ref.shape[2]

    @pl.when(i == 0)
    def _():
        out_ref[...] = jnp.zeros_like(out_ref)

    for rr in range(STEP):
        lhs = g_ref[:, rr * block : (rr + 1) * block]
        for t in range(0, count, 2):
            base = (i * STEP + rr) * count + t
            rhs = jnp.concatenate([tiles_ref[rr, t + k] for k in range(2)], axis=1)
            term = dot(lhs, rhs, (1, 0)).astype(BF)
            for k in range(2):
                slot = slots_ref[base + k]
                row = pl.multiple_of((slot % CAP) * width, width)
                out_ref[slot // CAP, pl.ds(row, width)] = term[:, k * block : (k + 1) * block]


def back_remote(slots, g, tiles, peers, after):
    row_blocks, per_block, block, _ = tiles.shape
    rem = per_block - TL
    width = g.shape[0]
    return pl.pallas_call(
        back_remote_kernel,
        grid=(row_blocks // STEP,),
        out_shape=jax.ShapeDtypeStruct((peers, CAP * width, block), BF),
        in_specs=[
            SMEM,
            pl.BlockSpec((width, STEP * block), lambda i: (0, i)),
            pl.BlockSpec((STEP, rem, block, block), lambda i: (i, 1, 0, 0)),
            ANY,
        ],
        out_specs=pl.BlockSpec((peers, CAP * width, block), lambda i: (0, 0, 0)),
        name="back_remote",
        cost_estimate=pl.CostEstimate(
            flops=2 * width * row_blocks * rem * block * block, bytes_accessed=5 << 20, transcendentals=0
        ),
    )(slots, g, tiles, after)


def back_local_kernel(cols_ref, g_ref, tiles_ref, _, out_ref):
    i = pl.program_id(0)
    count, block = tiles_ref.shape[1], tiles_ref.shape[2]

    @pl.when(i == 0)
    def _():
        out_ref[...] = jnp.zeros_like(out_ref)

    for rr in range(STEP):
        lhs = g_ref[:, rr * block : (rr + 1) * block]
        for t in range(0, count, 2):
            base = (i * STEP + rr) * count + t
            rhs = jnp.concatenate([tiles_ref[rr, t + k] for k in range(2)], axis=1)
            term = dot(lhs, rhs, (1, 0))
            for k in range(2):
                out_ref[:, lanes(cols_ref[base + k], block)] += term[:, k * block : (k + 1) * block]


def back_local(cols, g, tiles, after):
    row_blocks, _, block, _ = tiles.shape
    width = g.shape[0]
    return pl.pallas_call(
        back_local_kernel,
        grid=(row_blocks // STEP,),
        out_shape=jax.ShapeDtypeStruct(g.shape, F32),
        in_specs=[
            SMEM,
            pl.BlockSpec((width, STEP * block), lambda i: (0, i)),
            pl.BlockSpec((STEP, TL, block, block), lambda i: (i, 0, 0, 0)),
            ANY,
        ],
        out_specs=pl.BlockSpec(g.shape, lambda i: (0, 0)),
        name="back_local",
        cost_estimate=pl.CostEstimate(
            flops=2 * width * row_blocks * TL * block * block, bytes_accessed=3 << 20, transcendentals=0
        ),
    )(cols, g, tiles, after)


STREAMS = 4


def finish_kernel(place_ref, held_ref, recv_ref, local_ref, out_ref, odd_scr, recv_scr, sems):
    width, block = out_ref.shape[0], recv_scr.shape[2]
    count = recv_scr.shape[0] // STREAMS

    def stream(n):
        part = pl.ds(n * count, count)
        return pltpu.make_async_copy(recv_ref.at[part], recv_scr.at[part], sems.at[n])

    for n in range(STREAMS):
        stream(n).start()
    out_ref[...] = local_ref[...]
    odd_scr[...] = jnp.zeros_like(odd_scr)
    for n in range(STREAMS):
        stream(n).wait()

        def body(p, carry):
            back = (p // (NZ * NC) - place_ref[0]) & (NY - 1)
            base = (back * NC + ((p ^ place_ref[1]) & 1)) * CAP
            z = p // NC % NZ
            even = lanes(jnp.maximum(held_ref[z, 0, base], 0), block)
            odd = lanes(jnp.maximum(held_ref[z, 0, base + 1], 0), block)
            out_ref[:, even] += recv_scr[p, :width].astype(F32)
            odd_scr[:, odd] += recv_scr[p, width : 2 * width].astype(F32)
            return carry

        lax.fori_loop(n * count, (n + 1) * count, body, 0, unroll=4)
    out_ref[...] += odd_scr[...]


def finish(place, held, recv, local):
    return pl.pallas_call(
        finish_kernel,
        out_shape=jax.ShapeDtypeStruct(local.shape, F32),
        in_specs=[SMEM, SMEM, ANY, VMEM],
        out_specs=VMEM,
        scratch_shapes=[
            pltpu.VMEM(local.shape, F32),
            pltpu.VMEM(recv.shape, recv.dtype),
            pltpu.SemaphoreType.DMA((STREAMS,)),
        ],
        name="finish",
        compiler_params=pltpu.CompilerParams(vmem_limit_bytes=16 << 20),
        cost_estimate=pl.CostEstimate(flops=recv.size, bytes_accessed=4 << 20, transcendentals=0),
    )(place, held, recv, local)


def join_kernel(a_ref, b_ref, c_ref, d_ref, _, out_ref):
    out_ref[...] = (a_ref[...] + b_ref[...]) + (c_ref[...] + d_ref[...])


def join(terms, after):
    return pl.pallas_call(
        join_kernel,
        out_shape=jax.ShapeDtypeStruct(terms[0].shape, terms[0].dtype),
        in_specs=[VMEM] * 4 + [ANY],
        out_specs=VMEM,
        name="join",
    )(*terms, after)


def split_bf16(x, terms):
    parts = []
    for _ in range(terms):
        part = lax.reduce_precision(x, 8, 7)
        parts.append(part.astype(BF))
        x = x - part
    return parts


def local(feats, weight, bias, tile_cols, tile_values, cotangent):
    width, nodes_dev = feats.shape
    hid_all = weight.shape[1]
    block = tile_values.shape[1]
    row_blocks = nodes_dev // block
    peers = lax.axis_size("rows")
    fpeers = lax.axis_size("feat")
    per_block = tile_cols.shape[0] // row_blocks
    remote_count = row_blocks * (per_block - TL)
    place = lax.axis_index("rows")
    y, z, c = place // (NZ * NC), place // NC % NZ, place % NC

    grid = tile_cols.reshape(row_blocks, per_block)
    tiles = tile_values.reshape(row_blocks, per_block, block, block)
    local_cols = (grid[:, :TL] % row_blocks).reshape(-1)
    remote_cols = grid[:, TL:].reshape(-1)
    owner = remote_cols // row_blocks
    inside = remote_cols % row_blocks
    order = jnp.arange(remote_count)
    earlier = (owner[:, None] == owner[None, :]) & (order[None, :] < order[:, None])
    rank = jnp.sum(earlier.astype(jnp.int32), axis=1)
    slots = owner * CAP + rank
    ahead = (owner // NC - z) & (NZ - 1)

    def place_of(ahead):
        return jnp.maximum(jnp.where(ahead <= NZ // 2, 2 * ahead - 1, 2 * (NZ - ahead)), 0)

    pos = place_of(ahead)
    back = (y - owner // (NZ * NC)) & (NY - 1)
    other = (owner ^ c) & 1
    near = ((other * NY + back) * NZ + pos) * CAP + rank

    def table(index):
        hit = index[None, :] == jnp.arange(peers * CAP)[:, None]
        return jnp.max(jnp.where(hit, inside[None, :], -1), axis=1)

    asked = table(near).reshape(NC, NY, PER)
    agg, asked_own, asked_other = agg_local(local_cols, asked, feats, tiles)
    asked = jnp.stack([asked_own, shift(asked_other, dc=1)], axis=1)
    wanted = [asked[0]] + [shift(asked[ys], dy=-ys) for ys in range(1, NY)]
    wanted = jnp.stack(wanted).reshape(-1)

    up, down, parts = [feats], [feats], []
    for k in range(1, NZ // 2):
        up.append(shift(up[-1], dz=1))
        down.append(shift(down[-1], dz=-1))
    far_up = shift(up[-1][: width // 2], dz=1)
    far_down = shift(down[-1][width // 2 :], dz=-1)
    groups = ((feats, down[1], up[1]), (down[2], up[2]), (down[3], up[3], far_up, far_down))
    after = []
    for group, sources in zip(GROUPS, groups):
        packs = pack(group, wanted, sources, block, after)
        after = [packs[0]]
        moved = [packs[0]] + [shift(packs[ys], dy=ys) for ys in range(1, NY)]
        parts += moved
        parts.append(shift(jnp.concatenate([m[1:] for m in moved]), dc=1))

    bias_cols = jnp.pad(jnp.stack(split_bf16(bias, 3), axis=1), ((0, 0), (0, 125)))
    packed = jnp.concatenate([cotangent, weight, bias_cols], axis=1)
    packed = lax.all_gather(packed, "feat", axis=0, tiled=True)

    by_owner = wanted.reshape(NY * NC, NZ, CAP)
    steps = (jnp.arange(NZ) - z) & (NZ - 1)
    match = (place_of(steps)[:, None] == jnp.arange(NZ)[None, :])[:, None, :, None]
    held = jnp.sum(jnp.where(match, by_owner[None], 0), axis=2).reshape(NZ, 1, NY * NC * CAP)
    agg, held = agg_remote(near, held, parts, tiles, agg)

    pieces = [agg] + [
        lax.ppermute(agg, "feat", [(k, (k + s) % fpeers) for k in range(fpeers)]) for s in (1, 3, 2)
    ]
    along_z = [[(y0 * NZ + z0) * NC + c0 for z0 in range(NZ)] for y0 in range(NY) for c0 in range(NC)]
    held = lax.all_to_all(held, "rows", 0, 0, tiled=True, axis_index_groups=along_z)

    me = jnp.stack([lax.axis_index("feat"), c]).astype(jnp.int32)
    hidden_out, g, keep, give = mid(me, pieces, packed, weight, held)

    part = keep + shift(give, dc=1)
    twin = shift(part, flip_z=1)
    send = back_remote(slots, g, tiles, peers, part)
    send, twin = lax.optimization_barrier((send, twin))
    recv = lax.all_to_all(send, "rows", split_axis=0, concat_axis=0, tiled=True)
    own = back_local(local_cols, g, tiles, send)
    own, part, twin = lax.optimization_barrier((own, part, twin))
    part = part + twin
    pairs = [part] + [shift(part, flip_y=k) for k in (1, 2, 3)]
    part = (pairs[0] + pairs[1]) + (pairs[2] + pairs[3])
    pairs = [part] + [shift(part, flip_z=k) for k in (2, 4, 6)]
    grad_input = finish(jnp.stack([y, c]).astype(jnp.int32), held, recv, own)
    part = join(pairs, grad_input)
    other = shift(part, dc=1)
    total = jnp.where(c == 0, jnp.concatenate([part, other]), jnp.concatenate([other, part]))
    total = total / math.sqrt(nodes_dev * peers)
    grad_w = jnp.concatenate([total[k * width : (k + 1) * width] for k in range(hid_all // 128)], axis=1)
    grad_b = total[width * (hid_all // 128), :width]

    return hidden_out, grad_input, grad_w, grad_b


def solution(mesh):
    placed = (
        P("feat", "rows"),
        P("feat", None),
        P("feat"),
        P("rows"),
        P("rows", None, None),
        P("feat", "rows"),
    )
    return jax.shard_map(
        local,
        mesh=mesh,
        in_specs=placed,
        out_specs=(P("feat", "rows"), P("feat", "rows"), P("feat", None), P("feat")),
        check_vma=False,
    )
```

```python
import functools
import math

import jax
import jax.numpy as jnp
from jax import lax
from jax.experimental import pallas as pl
from jax.experimental.pallas import tpu as pltpu
from jax.sharding import PartitionSpec as P

TL = 4
BF = jnp.bfloat16
F32 = jnp.float32
VMEM = pl.BlockSpec(memory_space=pltpu.VMEM)
ANY = pl.BlockSpec(memory_space=pl.ANY)
SMEM = pl.BlockSpec(memory_space=pltpu.SMEM)


def lanes(index, width):
    return pl.ds(pl.multiple_of(index * width, width), width)


NY, NZ, NC = 4, 8, 2
CAP = 2
TAIL = 16
ORDER = (0, 1, 7, 2, 6, 3, 5, 4)
GROUPS = ((0, 3), (3, 5), (5, 8))
PER = NZ * CAP


def shift(x, dy=0, dz=0, dc=0, flip_y=0, flip_z=0):
    pairs = []
    for y in range(NY):
        for z in range(NZ):
            for c in range(NC):
                to_y, to_z = ((y ^ flip_y) + dy) % NY, ((z ^ flip_z) + dz) % NZ
                pairs.append(((y * NZ + z) * NC + c, (to_y * NZ + to_z) * NC + (c + dc) % NC))
    return lax.ppermute(x, "rows", pairs)


def pack_kernel(first, count, split, *refs):
    wanted_ref, sources, outs = refs[0], refs[1 : 1 + count + split], refs[-NY:]
    width, block = outs[0].shape[2], outs[0].shape[3]
    for ys in range(NY):
        for cs in range(NC):
            for q in range(count * CAP):
                w = wanted_ref[(ys * NC + cs) * PER + first * CAP + q]
                where = lanes(jnp.maximum(w, 0), block)
                j = q // CAP
                if split and j == count - 1:
                    outs[ys][cs, q, : width // 2] = sources[j][:, where]
                    outs[ys][cs, q, width // 2 :] = sources[j + 1][:, where]
                else:
                    outs[ys][cs, q] = sources[j][:, where]


def pack(group, wanted, sources, block, after):
    first, last = group
    count = last - first
    width = sources[0].shape[0]
    shape = jax.ShapeDtypeStruct((NC, count * CAP, width, block), BF)
    return pl.pallas_call(
        functools.partial(pack_kernel, first, count, len(sources) > count),
        out_shape=[shape] * NY,
        in_specs=[SMEM] + [VMEM] * len(sources) + [ANY] * len(after),
        out_specs=[VMEM] * NY,
        name="pack",
        cost_estimate=pl.CostEstimate(flops=0, bytes_accessed=3 << 20, transcendentals=0),
    )(wanted, *sources, *after)


def dot(a, b, dims):
    return lax.dot_general(a, b, ((dims[:1], dims[1:]), ((), ())), preferred_element_type=F32)


STEP = 4


def agg_local_kernel(cols_ref, feats_ref, tiles_ref, out_ref):
    i = pl.program_id(0)
    count, block = tiles_ref.shape[1], tiles_ref.shape[2]
    for rr in range(STEP):
        acc = None
        for t in range(0, count, 2):
            base = (i * STEP + rr) * count + t
            lhs = jnp.concatenate(
                [feats_ref[:, lanes(cols_ref[base + k], block)] for k in range(2)], axis=1
            )
            rhs = jnp.concatenate([tiles_ref[rr, t + k] for k in range(2)], axis=1)
            term = dot(lhs, rhs, (1, 1))
            acc = term if acc is None else acc + term
        out_ref[:, rr * block : (rr + 1) * block] = acc


def agg_local(cols, feats, tiles):
    row_blocks, _, block, _ = tiles.shape
    width = feats.shape[0]
    return pl.pallas_call(
        agg_local_kernel,
        grid=(row_blocks // STEP,),
        out_shape=jax.ShapeDtypeStruct((width, row_blocks * block), F32),
        in_specs=[
            SMEM,
            pl.BlockSpec(feats.shape, lambda i: (0, 0)),
            pl.BlockSpec((STEP, TL, block, block), lambda i: (i, 0, 0, 0)),
        ],
        out_specs=pl.BlockSpec((width, STEP * block), lambda i: (0, i)),
        name="agg_local",
        cost_estimate=pl.CostEstimate(
            flops=2 * width * row_blocks * TL * block * block, bytes_accessed=3 << 20, transcendentals=0
        ),
    )(cols, feats, tiles)


def agg_remote_kernel(slots_ref, held_ref, tiles_ref, local_ref, *refs):
    parts, out_ref, held_out_ref, recv_ref = refs[:-3], refs[-3], refs[-2], refs[-1]
    i = pl.program_id(0)
    count, block = tiles_ref.shape[1], tiles_ref.shape[2]

    @pl.when(i == 0)
    def _():
        held_out_ref[...] = held_ref[...]
        n = 0
        for first, last in GROUPS:
            size = (last - first) * CAP
            for ys in range(NY):
                recv_ref[pl.ds(ys * PER + first * CAP, size)] = parts[n + ys][0]
                recv_ref[pl.ds((NY + ys) * PER + first * CAP, size)] = parts[n + NY][ys]
            n += NY + 1

    for rr in range(STEP):
        acc = local_ref[:, rr * block : (rr + 1) * block]
        for t in range(0, count, 2):
            base = (i * STEP + rr) * count + t
            lhs = jnp.concatenate([recv_ref[slots_ref[base + k]] for k in range(2)], axis=1)
            rhs = jnp.concatenate([tiles_ref[rr, t + k] for k in range(2)], axis=1)
            acc = acc + dot(lhs, rhs, (1, 1))
        out_ref[:, rr * block : (rr + 1) * block] = acc.astype(out_ref.dtype)


def agg_remote(slots, held, parts, tiles, local):
    row_blocks, per_block, block, _ = tiles.shape
    rem = per_block - TL
    width = local.shape[0]
    specs = []
    for n, part in enumerate(parts):
        lead = 1 if n % (NY + 1) < NY else NY
        specs.append(pl.BlockSpec((lead,) + part.shape[1:], lambda i: (0, 0, 0, 0)))
    return pl.pallas_call(
        agg_remote_kernel,
        grid=(row_blocks // STEP,),
        out_shape=(jax.ShapeDtypeStruct(local.shape, BF), jax.ShapeDtypeStruct(held.shape, held.dtype)),
        in_specs=[
            SMEM,
            pl.BlockSpec(held.shape, lambda i: (0, 0, 0)),
            pl.BlockSpec((STEP, rem, block, block), lambda i: (i, 1, 0, 0)),
            pl.BlockSpec((width, STEP * block), lambda i: (0, i)),
        ]
        + specs,
        out_specs=(
            pl.BlockSpec((width, STEP * block), lambda i: (0, i)),
            pl.BlockSpec(held.shape, lambda i: (0, 0, 0)),
        ),
        scratch_shapes=[pltpu.VMEM((NY * NC * PER, width, block), BF)],
        name="agg_remote",
        cost_estimate=pl.CostEstimate(
            flops=2 * width * row_blocks * rem * block * block, bytes_accessed=5 << 20, transcendentals=0
        ),
    )(slots, held, tiles, local, *parts)


def mid_kernel(
    me_ref,
    _,
    own_ref,
    low_ref,
    high_ref,
    far_ref,
    cot_ref,
    w_ref,
    bias_ref,
    wown_ref,
    hid_ref,
    g_ref,
    keep_ref,
    give_ref,
    agg_scr,
    hid_scr,
    wt_scr,
    gb_scr,
    sums_scr,
):
    i = pl.program_id(0)
    width = own_ref.shape[0]
    count = agg_scr.shape[0] // width
    me = me_ref[0]

    def rows(ahead):
        return pl.ds(pl.multiple_of(lax.rem(me + ahead, count) * width, width), width)

    @pl.when(i == 0)
    def _():
        wt_scr[...] = w_ref[...].astype(F32).T.astype(BF)
        sums_scr[...] = jnp.zeros_like(sums_scr)
        gb_scr[...] = jnp.zeros_like(gb_scr)

    agg_scr[rows(3)] = low_ref[...]
    agg_scr[rows(1)] = high_ref[...]
    agg_scr[rows(2)] = far_ref[...]
    agg_scr[rows(0)] = own_ref[...]
    pre = dot(wt_scr[...], agg_scr[...], (1, 0))
    bias = bias_ref[:, :3].astype(F32)
    pre = pre + ((bias[:, 2:3] + bias[:, 1:2]) + bias[:, 0:1])
    sigma = jax.nn.sigmoid(pre)
    hid_scr[...] = (pre * sigma).astype(BF)
    hid_ref[...] = hid_scr[rows(0)]
    grad_pre = cot_ref[...].astype(F32) * (sigma * (1.0 + pre * (1.0 - sigma)))
    total = grad_pre[:, :128]
    for k in range(1, grad_pre.shape[1] // 128):
        total = total + grad_pre[:, k * 128 : (k + 1) * 128]
    gb_scr[...] += total
    grad_b = grad_pre.astype(BF)
    g_ref[...] = dot(wown_ref[...], grad_b, (1, 0)).astype(BF)
    grad_w = dot(own_ref[...], grad_b, (1, 1))
    for k in range(grad_w.shape[1] // 128):
        sums_scr[k * width : (k + 1) * width] += grad_w[:, k * 128 : (k + 1) * 128]

    @pl.when(i == pl.num_programs(0) - 1)
    def _():
        half = keep_ref.shape[0]
        own = gb_scr[rows(0)]
        sums_scr[2 * half - TAIL : 2 * half - TAIL + 1, :width] = jnp.sum(own.T, axis=0, keepdims=True)
        keep_ref[...] = sums_scr[pl.ds(pl.multiple_of(me_ref[1] * half, half), half)]
        give_ref[...] = sums_scr[pl.ds(pl.multiple_of((1 - me_ref[1]) * half, half), half)]


def mid(me, pieces, packed, w_own, after):
    own, low, high, far = pieces
    width, nodes = own.shape
    hid_all = packed.shape[0]
    chunk = 512
    half = (width * (hid_all // 128) + TAIL) // NC
    col = lambda i: (0, i)
    return pl.pallas_call(
        mid_kernel,
        grid=(nodes // chunk,),
        out_shape=(
            jax.ShapeDtypeStruct((width, nodes), BF),
            jax.ShapeDtypeStruct((width, nodes), BF),
            jax.ShapeDtypeStruct((half, 128), F32),
            jax.ShapeDtypeStruct((half, 128), F32),
        ),
        in_specs=[
            SMEM,
            ANY,
            pl.BlockSpec((width, chunk), col),
            pl.BlockSpec((width, chunk), col),
            pl.BlockSpec((width, chunk), col),
            pl.BlockSpec((width, chunk), col),
            pl.BlockSpec((hid_all, chunk), col),
            pl.BlockSpec((hid_all, hid_all), lambda i: (0, nodes // hid_all)),
            pl.BlockSpec((hid_all, 128), lambda i: (0, (nodes + hid_all) // 128)),
            pl.BlockSpec((width, hid_all), lambda i: (0, 0)),
        ],
        out_specs=(
            pl.BlockSpec((width, chunk), col),
            pl.BlockSpec((width, chunk), col),
            pl.BlockSpec((half, 128), lambda i: (0, 0)),
            pl.BlockSpec((half, 128), lambda i: (0, 0)),
        ),
        scratch_shapes=[
            pltpu.VMEM((hid_all, chunk), BF),
            pltpu.VMEM((hid_all, chunk), BF),
            pltpu.VMEM((hid_all, hid_all), BF),
            pltpu.VMEM((hid_all, 128), F32),
            pltpu.VMEM((NC * half, 128), F32),
        ],
        name="mid",
        cost_estimate=pl.CostEstimate(
            flops=2 * nodes * hid_all * (hid_all + 2 * width),
            bytes_accessed=3 << 20,
            transcendentals=nodes * hid_all,
        ),
    )(me, after, own, low, high, far, packed, packed, packed, w_own)


def back_remote_kernel(slots_ref, g_ref, tiles_ref, _, out_ref):
    i = pl.program_id(0)
    width = g_ref.shape[0]
    count, block = tiles_ref.shape[1], tiles_ref.shape[2]

    @pl.when(i == 0)
    def _():
        out_ref[...] = jnp.zeros_like(out_ref)

    for rr in range(STEP):
        lhs = g_ref[:, rr * block : (rr + 1) * block]
        for t in range(0, count, 2):
            base = (i * STEP + rr) * count + t
            rhs = jnp.concatenate([tiles_ref[rr, t + k] for k in range(2)], axis=1)
            term = dot(lhs, rhs, (1, 0)).astype(BF)
            for k in range(2):
                slot = slots_ref[base + k]
                row = pl.multiple_of((slot % CAP) * width, width)
                out_ref[slot // CAP, pl.ds(row, width)] = term[:, k * block : (k + 1) * block]


def back_remote(slots, g, tiles, peers, after):
    row_blocks, per_block, block, _ = tiles.shape
    rem = per_block - TL
    width = g.shape[0]
    return pl.pallas_call(
        back_remote_kernel,
        grid=(row_blocks // STEP,),
        out_shape=jax.ShapeDtypeStruct((peers, CAP * width, block), BF),
        in_specs=[
            SMEM,
            pl.BlockSpec((width, STEP * block), lambda i: (0, i)),
            pl.BlockSpec((STEP, rem, block, block), lambda i: (i, 1, 0, 0)),
            ANY,
        ],
        out_specs=pl.BlockSpec((peers, CAP * width, block), lambda i: (0, 0, 0)),
        name="back_remote",
        cost_estimate=pl.CostEstimate(
            flops=2 * width * row_blocks * rem * block * block, bytes_accessed=5 << 20, transcendentals=0
        ),
    )(slots, g, tiles, after)


def back_local_kernel(cols_ref, g_ref, tiles_ref, _, out_ref):
    i = pl.program_id(0)
    count, block = tiles_ref.shape[1], tiles_ref.shape[2]

    @pl.when(i == 0)
    def _():
        out_ref[...] = jnp.zeros_like(out_ref)

    for rr in range(STEP):
        lhs = g_ref[:, rr * block : (rr + 1) * block]
        for t in range(0, count, 2):
            base = (i * STEP + rr) * count + t
            rhs = jnp.concatenate([tiles_ref[rr, t + k] for k in range(2)], axis=1)
            term = dot(lhs, rhs, (1, 0))
            for k in range(2):
                out_ref[:, lanes(cols_ref[base + k], block)] += term[:, k * block : (k + 1) * block]


def back_local(cols, g, tiles, after):
    row_blocks, _, block, _ = tiles.shape
    width = g.shape[0]
    return pl.pallas_call(
        back_local_kernel,
        grid=(row_blocks // STEP,),
        out_shape=jax.ShapeDtypeStruct(g.shape, F32),
        in_specs=[
            SMEM,
            pl.BlockSpec((width, STEP * block), lambda i: (0, i)),
            pl.BlockSpec((STEP, TL, block, block), lambda i: (i, 0, 0, 0)),
            ANY,
        ],
        out_specs=pl.BlockSpec(g.shape, lambda i: (0, 0)),
        name="back_local",
        cost_estimate=pl.CostEstimate(
            flops=2 * width * row_blocks * TL * block * block, bytes_accessed=3 << 20, transcendentals=0
        ),
    )(cols, g, tiles, after)


STREAMS = 4


def finish_kernel(place_ref, held_ref, recv_ref, local_ref, out_ref, odd_scr, recv_scr, sems):
    width, block = out_ref.shape[0], recv_scr.shape[2]
    count = recv_scr.shape[0] // STREAMS

    def stream(n):
        part = pl.ds(n * count, count)
        return pltpu.make_async_copy(recv_ref.at[part], recv_scr.at[part], sems.at[n])

    for n in range(STREAMS):
        stream(n).start()
    out_ref[...] = local_ref[...]
    odd_scr[...] = jnp.zeros_like(odd_scr)
    for n in range(STREAMS):
        stream(n).wait()

        def body(p, carry):
            back = (p // (NZ * NC) - place_ref[0]) & (NY - 1)
            base = (back * NC + ((p ^ place_ref[1]) & 1)) * CAP
            z = p // NC % NZ
            even = lanes(jnp.maximum(held_ref[z, 0, base], 0), block)
            odd = lanes(jnp.maximum(held_ref[z, 0, base + 1], 0), block)
            out_ref[:, even] += recv_scr[p, :width].astype(F32)
            odd_scr[:, odd] += recv_scr[p, width : 2 * width].astype(F32)
            return carry

        lax.fori_loop(n * count, (n + 1) * count, body, 0, unroll=4)
    out_ref[...] += odd_scr[...]


def finish(place, held, recv, local):
    return pl.pallas_call(
        finish_kernel,
        out_shape=jax.ShapeDtypeStruct(local.shape, F32),
        in_specs=[SMEM, SMEM, ANY, VMEM],
        out_specs=VMEM,
        scratch_shapes=[
            pltpu.VMEM(local.shape, F32),
            pltpu.VMEM(recv.shape, recv.dtype),
            pltpu.SemaphoreType.DMA((STREAMS,)),
        ],
        name="finish",
        compiler_params=pltpu.CompilerParams(vmem_limit_bytes=16 << 20),
        cost_estimate=pl.CostEstimate(flops=recv.size, bytes_accessed=4 << 20, transcendentals=0),
    )(place, held, recv, local)


def split_bf16(x, terms):
    parts = []
    for _ in range(terms):
        part = lax.reduce_precision(x, 8, 7)
        parts.append(part.astype(BF))
        x = x - part
    return parts


def local(feats, weight, bias, tile_cols, tile_values, cotangent):
    width, nodes_dev = feats.shape
    hid_all = weight.shape[1]
    block = tile_values.shape[1]
    row_blocks = nodes_dev // block
    peers = lax.axis_size("rows")
    fpeers = lax.axis_size("feat")
    per_block = tile_cols.shape[0] // row_blocks
    remote_count = row_blocks * (per_block - TL)
    place = lax.axis_index("rows")
    y, z, c = place // (NZ * NC), place // NC % NZ, place % NC

    grid = tile_cols.reshape(row_blocks, per_block)
    tiles = tile_values.reshape(row_blocks, per_block, block, block)
    local_cols = (grid[:, :TL] % row_blocks).reshape(-1)
    remote_cols = grid[:, TL:].reshape(-1)
    owner = remote_cols // row_blocks
    inside = remote_cols % row_blocks
    order = jnp.arange(remote_count)
    earlier = (owner[:, None] == owner[None, :]) & (order[None, :] < order[:, None])
    rank = jnp.sum(earlier.astype(jnp.int32), axis=1)
    slots = owner * CAP + rank
    ahead = (owner // NC - z) & (NZ - 1)

    def place_of(ahead):
        return jnp.maximum(jnp.where(ahead <= NZ // 2, 2 * ahead - 1, 2 * (NZ - ahead)), 0)

    pos = place_of(ahead)
    back = (y - owner // (NZ * NC)) & (NY - 1)
    other = (owner ^ c) & 1
    near = ((other * NY + back) * NZ + pos) * CAP + rank

    def table(index):
        hit = index[None, :] == jnp.arange(peers * CAP)[:, None]
        return jnp.max(jnp.where(hit, inside[None, :], -1), axis=1)

    asked = table(near).reshape(NC, NY, PER)
    asked = jnp.stack([asked[0], shift(asked[1], dc=1)], axis=1)
    wanted = [asked[0]] + [shift(asked[ys], dy=-ys) for ys in range(1, NY)]
    wanted = jnp.stack(wanted).reshape(-1)

    up, down, parts = [feats], [feats], []
    for k in range(1, NZ // 2):
        up.append(shift(up[-1], dz=1))
        down.append(shift(down[-1], dz=-1))
    far_up = shift(up[-1][: width // 2], dz=1)
    far_down = shift(down[-1][width // 2 :], dz=-1)
    groups = ((feats, down[1], up[1]), (down[2], up[2]), (down[3], up[3], far_up, far_down))
    after = []
    agg = agg_local(local_cols, feats, tiles)
    for group, sources in zip(GROUPS, groups):
        packs = pack(group, wanted, sources, block, after)
        after = [packs[0]] if group == GROUPS[0] else [packs[0], agg]
        moved = [packs[0]] + [shift(packs[ys], dy=ys) for ys in range(1, NY)]
        parts += moved
        parts.append(shift(jnp.concatenate([m[1:] for m in moved]), dc=1))

    bias_cols = jnp.pad(jnp.stack(split_bf16(bias, 3), axis=1), ((0, 0), (0, 125)))
    packed = jnp.concatenate([cotangent, weight, bias_cols], axis=1)
    packed = lax.all_gather(packed, "feat", axis=0, tiled=True)

    by_owner = wanted.reshape(NY * NC, NZ, CAP)
    steps = (jnp.arange(NZ) - z) & (NZ - 1)
    match = (place_of(steps)[:, None] == jnp.arange(NZ)[None, :])[:, None, :, None]
    held = jnp.sum(jnp.where(match, by_owner[None], 0), axis=2).reshape(NZ, 1, NY * NC * CAP)
    agg, held = agg_remote(near, held, parts, tiles, agg)

    ahead = [
        lax.ppermute(agg, "feat", [(k, (k + s) % fpeers) for k in range(fpeers)]) for s in (2, 1, 3)
    ]
    pieces = [agg, ahead[1], ahead[2], ahead[0]]
    along_z = [[(y0 * NZ + z0) * NC + c0 for z0 in range(NZ)] for y0 in range(NY) for c0 in range(NC)]
    held = lax.all_to_all(held, "rows", 0, 0, tiled=True, axis_index_groups=along_z)

    me = jnp.stack([lax.axis_index("feat"), c]).astype(jnp.int32)
    hidden_out, g, keep, give = mid(me, pieces, packed, weight, held)

    part = keep + shift(give, dc=1)
    twin = shift(part, flip_z=1)
    send = back_remote(slots, g, tiles, peers, part)
    send, twin = lax.optimization_barrier((send, twin))
    recv = lax.all_to_all(send, "rows", split_axis=0, concat_axis=0, tiled=True)
    own = back_local(local_cols, g, tiles, send)
    own, part, twin = lax.optimization_barrier((own, part, twin))
    part = part + twin
    pairs = [part] + [shift(part, flip_y=k) for k in (1, 2, 3)]
    part = (pairs[0] + pairs[1]) + (pairs[2] + pairs[3])
    pairs = [part] + [shift(part, flip_z=k) for k in (2, 4, 6)]
    part = (pairs[0] + pairs[1]) + (pairs[2] + pairs[3])
    other = shift(part, dc=1)
    total = jnp.where(c == 0, jnp.concatenate([part, other]), jnp.concatenate([other, part]))
    total = total / math.sqrt(nodes_dev * peers)
    grad_w = jnp.concatenate([total[k * width : (k + 1) * width] for k in range(hid_all // 128)], axis=1)
    grad_b = total[width * (hid_all // 128), :width]

    grad_input = finish(jnp.stack([y, c]).astype(jnp.int32), held, recv, own)
    return hidden_out, grad_input, grad_w, grad_b


def solution(mesh):
    placed = (
        P("feat", "rows"),
        P("feat", None),
        P("feat"),
        P("rows"),
        P("rows", None, None),
        P("feat", "rows"),
    )
    return jax.shard_map(
        local,
        mesh=mesh,
        in_specs=placed,
        out_specs=(P("feat", "rows"), P("feat", "rows"), P("feat", None), P("feat")),
        check_vma=False,
    )
```

```python
import functools
import math

import jax
import jax.numpy as jnp
from jax import lax
from jax.experimental import pallas as pl
from jax.experimental.pallas import tpu as pltpu
from jax.sharding import PartitionSpec as P

TL = 4
BF = jnp.bfloat16
F32 = jnp.float32
VMEM = pl.BlockSpec(memory_space=pltpu.VMEM)
ANY = pl.BlockSpec(memory_space=pl.ANY)
SMEM = pl.BlockSpec(memory_space=pltpu.SMEM)


def lanes(index, width):
    return pl.ds(pl.multiple_of(index * width, width), width)


NY, NZ, NC = 4, 8, 2
CAP = 2
TAIL = 16
ORDER = (0, 1, 7, 2, 6, 3, 5, 4)
GROUPS = ((0, 3), (3, 5), (5, 8))
PER = NZ * CAP


def shift(x, dy=0, dz=0, dc=0, flip_y=0, flip_z=0):
    pairs = []
    for y in range(NY):
        for z in range(NZ):
            for c in range(NC):
                to_y, to_z = ((y ^ flip_y) + dy) % NY, ((z ^ flip_z) + dz) % NZ
                pairs.append(((y * NZ + z) * NC + c, (to_y * NZ + to_z) * NC + (c + dc) % NC))
    return lax.ppermute(x, "rows", pairs)


def pack_kernel(first, count, split, *refs):
    wanted_ref, sources, outs = refs[0], refs[1 : 1 + count + split], refs[-NY:]
    width, block = outs[0].shape[2], outs[0].shape[3]
    for ys in range(NY):
        for cs in range(NC):
            for q in range(count * CAP):
                w = wanted_ref[(ys * NC + cs) * PER + first * CAP + q]
                where = lanes(jnp.maximum(w, 0), block)
                j = q // CAP
                if split and j == count - 1:
                    outs[ys][cs, q, : width // 2] = sources[j][:, where]
                    outs[ys][cs, q, width // 2 :] = sources[j + 1][:, where]
                else:
                    outs[ys][cs, q] = sources[j][:, where]


def pack(group, wanted, sources, block, after):
    first, last = group
    count = last - first
    width = sources[0].shape[0]
    shape = jax.ShapeDtypeStruct((NC, count * CAP, width, block), BF)
    return pl.pallas_call(
        functools.partial(pack_kernel, first, count, len(sources) > count),
        out_shape=[shape] * NY,
        in_specs=[SMEM] + [VMEM] * len(sources) + [ANY] * len(after),
        out_specs=[VMEM] * NY,
        name="pack",
        cost_estimate=pl.CostEstimate(flops=0, bytes_accessed=3 << 20, transcendentals=0),
    )(wanted, *sources, *after)


def dot(a, b, dims):
    return lax.dot_general(a, b, ((dims[:1], dims[1:]), ((), ())), preferred_element_type=F32)


STEP = 4


def agg_local_kernel(cols_ref, feats_ref, tiles_ref, out_ref):
    i = pl.program_id(0)
    count, block = tiles_ref.shape[1], tiles_ref.shape[2]
    for rr in range(STEP):
        acc = None
        for t in range(0, count, 2):
            base = (i * STEP + rr) * count + t
            lhs = jnp.concatenate(
                [feats_ref[:, lanes(cols_ref[base + k], block)] for k in range(2)], axis=1
            )
            rhs = jnp.concatenate([tiles_ref[rr, t + k] for k in range(2)], axis=1)
            term = dot(lhs, rhs, (1, 1))
            acc = term if acc is None else acc + term
        out_ref[:, rr * block : (rr + 1) * block] = acc


def agg_local(cols, feats, tiles):
    row_blocks, _, block, _ = tiles.shape
    width = feats.shape[0]
    return pl.pallas_call(
        agg_local_kernel,
        grid=(row_blocks // STEP,),
        out_shape=jax.ShapeDtypeStruct((width, row_blocks * block), F32),
        in_specs=[
            SMEM,
            pl.BlockSpec(feats.shape, lambda i: (0, 0)),
            pl.BlockSpec((STEP, TL, block, block), lambda i: (i, 0, 0, 0)),
        ],
        out_specs=pl.BlockSpec((width, STEP * block), lambda i: (0, i)),
        name="agg_local",
        cost_estimate=pl.CostEstimate(
            flops=2 * width * row_blocks * TL * block * block, bytes_accessed=3 << 20, transcendentals=0
        ),
    )(cols, feats, tiles)


def agg_remote_kernel(slots_ref, held_ref, tiles_ref, local_ref, *refs):
    parts, out_ref, held_out_ref, recv_ref = refs[:-3], refs[-3], refs[-2], refs[-1]
    i = pl.program_id(0)
    count, block = tiles_ref.shape[1], tiles_ref.shape[2]

    @pl.when(i == 0)
    def _():
        held_out_ref[...] = held_ref[...]
        n = 0
        for first, last in GROUPS:
            size = (last - first) * CAP
            for ys in range(NY):
                recv_ref[pl.ds(ys * PER + first * CAP, size)] = parts[n + ys][0]
                recv_ref[pl.ds((NY + ys) * PER + first * CAP, size)] = parts[n + NY][ys]
            n += NY + 1

    for rr in range(STEP):
        acc = local_ref[:, rr * block : (rr + 1) * block]
        for t in range(0, count, 2):
            base = (i * STEP + rr) * count + t
            lhs = jnp.concatenate([recv_ref[slots_ref[base + k]] for k in range(2)], axis=1)
            rhs = jnp.concatenate([tiles_ref[rr, t + k] for k in range(2)], axis=1)
            acc = acc + dot(lhs, rhs, (1, 1))
        out_ref[:, rr * block : (rr + 1) * block] = acc.astype(out_ref.dtype)


def agg_remote(slots, held, parts, tiles, local):
    row_blocks, per_block, block, _ = tiles.shape
    rem = per_block - TL
    width = local.shape[0]
    specs = []
    for n, part in enumerate(parts):
        lead = 1 if n % (NY + 1) < NY else NY
        specs.append(pl.BlockSpec((lead,) + part.shape[1:], lambda i: (0, 0, 0, 0)))
    return pl.pallas_call(
        agg_remote_kernel,
        grid=(row_blocks // STEP,),
        out_shape=(jax.ShapeDtypeStruct(local.shape, BF), jax.ShapeDtypeStruct(held.shape, held.dtype)),
        in_specs=[
            SMEM,
            pl.BlockSpec(held.shape, lambda i: (0, 0, 0)),
            pl.BlockSpec((STEP, rem, block, block), lambda i: (i, 1, 0, 0)),
            pl.BlockSpec((width, STEP * block), lambda i: (0, i)),
        ]
        + specs,
        out_specs=(
            pl.BlockSpec((width, STEP * block), lambda i: (0, i)),
            pl.BlockSpec(held.shape, lambda i: (0, 0, 0)),
        ),
        scratch_shapes=[pltpu.VMEM((NY * NC * PER, width, block), BF)],
        name="agg_remote",
        cost_estimate=pl.CostEstimate(
            flops=2 * width * row_blocks * rem * block * block, bytes_accessed=5 << 20, transcendentals=0
        ),
    )(slots, held, tiles, local, *parts)


def mid_kernel(
    me_ref,
    _,
    own_ref,
    low_ref,
    high_ref,
    far_ref,
    cot_ref,
    w_ref,
    bias_ref,
    wown_ref,
    hid_ref,
    g_ref,
    keep_ref,
    give_ref,
    agg_scr,
    hid_scr,
    wt_scr,
    gb_scr,
    sums_scr,
):
    i = pl.program_id(0)
    width = own_ref.shape[0]
    count = agg_scr.shape[0] // width
    me = me_ref[0]

    def rows(ahead):
        return pl.ds(pl.multiple_of(lax.rem(me + ahead, count) * width, width), width)

    @pl.when(i == 0)
    def _():
        wt_scr[...] = w_ref[...].astype(F32).T.astype(BF)
        sums_scr[...] = jnp.zeros_like(sums_scr)
        gb_scr[...] = jnp.zeros_like(gb_scr)

    agg_scr[rows(3)] = low_ref[...]
    agg_scr[rows(1)] = high_ref[...]
    agg_scr[rows(2)] = far_ref[...]
    agg_scr[rows(0)] = own_ref[...]
    pre = dot(wt_scr[...], agg_scr[...], (1, 0))
    bias = bias_ref[:, :3].astype(F32)
    pre = pre + ((bias[:, 2:3] + bias[:, 1:2]) + bias[:, 0:1])
    sigma = jax.nn.sigmoid(pre)
    hid_scr[...] = (pre * sigma).astype(BF)
    hid_ref[...] = hid_scr[rows(0)]
    grad_pre = cot_ref[...].astype(F32) * (sigma * (1.0 + pre * (1.0 - sigma)))
    total = grad_pre[:, :128]
    for k in range(1, grad_pre.shape[1] // 128):
        total = total + grad_pre[:, k * 128 : (k + 1) * 128]
    gb_scr[...] += total
    grad_b = grad_pre.astype(BF)
    g_ref[...] = dot(wown_ref[...], grad_b, (1, 0)).astype(BF)
    grad_w = dot(own_ref[...], grad_b, (1, 1))
    for k in range(grad_w.shape[1] // 128):
        sums_scr[k * width : (k + 1) * width] += grad_w[:, k * 128 : (k + 1) * 128]

    @pl.when(i == pl.num_programs(0) - 1)
    def _():
        half = keep_ref.shape[0]
        own = gb_scr[rows(0)]
        sums_scr[2 * half - TAIL : 2 * half - TAIL + 1, :width] = jnp.sum(own.T, axis=0, keepdims=True)
        keep_ref[...] = sums_scr[pl.ds(pl.multiple_of(me_ref[1] * half, half), half)]
        give_ref[...] = sums_scr[pl.ds(pl.multiple_of((1 - me_ref[1]) * half, half), half)]


def mid(me, pieces, packed, w_own, after):
    own, low, high, far = pieces
    width, nodes = own.shape
    hid_all = packed.shape[0]
    chunk = 512
    half = (width * (hid_all // 128) + TAIL) // NC
    col = lambda i: (0, i)
    return pl.pallas_call(
        mid_kernel,
        grid=(nodes // chunk,),
        out_shape=(
            jax.ShapeDtypeStruct((width, nodes), BF),
            jax.ShapeDtypeStruct((width, nodes), BF),
            jax.ShapeDtypeStruct((half, 128), F32),
            jax.ShapeDtypeStruct((half, 128), F32),
        ),
        in_specs=[
            SMEM,
            ANY,
            pl.BlockSpec((width, chunk), col),
            pl.BlockSpec((width, chunk), col),
            pl.BlockSpec((width, chunk), col),
            pl.BlockSpec((width, chunk), col),
            pl.BlockSpec((hid_all, chunk), col),
            pl.BlockSpec((hid_all, hid_all), lambda i: (0, nodes // hid_all)),
            pl.BlockSpec((hid_all, 128), lambda i: (0, (nodes + hid_all) // 128)),
            pl.BlockSpec((width, hid_all), lambda i: (0, 0)),
        ],
        out_specs=(
            pl.BlockSpec((width, chunk), col),
            pl.BlockSpec((width, chunk), col),
            pl.BlockSpec((half, 128), lambda i: (0, 0)),
            pl.BlockSpec((half, 128), lambda i: (0, 0)),
        ),
        scratch_shapes=[
            pltpu.VMEM((hid_all, chunk), BF),
            pltpu.VMEM((hid_all, chunk), BF),
            pltpu.VMEM((hid_all, hid_all), BF),
            pltpu.VMEM((hid_all, 128), F32),
            pltpu.VMEM((NC * half, 128), F32),
        ],
        name="mid",
        cost_estimate=pl.CostEstimate(
            flops=2 * nodes * hid_all * (hid_all + 2 * width),
            bytes_accessed=3 << 20,
            transcendentals=nodes * hid_all,
        ),
    )(me, after, own, low, high, far, packed, packed, packed, w_own)


def back_remote_kernel(slots_ref, g_ref, tiles_ref, _, out_ref):
    i = pl.program_id(0)
    width = g_ref.shape[0]
    count, block = tiles_ref.shape[1], tiles_ref.shape[2]

    @pl.when(i == 0)
    def _():
        out_ref[...] = jnp.zeros_like(out_ref)

    for rr in range(STEP):
        lhs = g_ref[:, rr * block : (rr + 1) * block]
        for t in range(0, count, 2):
            base = (i * STEP + rr) * count + t
            rhs = jnp.concatenate([tiles_ref[rr, t + k] for k in range(2)], axis=1)
            term = dot(lhs, rhs, (1, 0)).astype(BF)
            for k in range(2):
                slot = slots_ref[base + k]
                row = pl.multiple_of((slot % CAP) * width, width)
                out_ref[slot // CAP, pl.ds(row, width)] = term[:, k * block : (k + 1) * block]


def back_remote(slots, g, tiles, peers, after):
    row_blocks, per_block, block, _ = tiles.shape
    rem = per_block - TL
    width = g.shape[0]
    return pl.pallas_call(
        back_remote_kernel,
        grid=(row_blocks // STEP,),
        out_shape=jax.ShapeDtypeStruct((peers, CAP * width, block), BF),
        in_specs=[
            SMEM,
            pl.BlockSpec((width, STEP * block), lambda i: (0, i)),
            pl.BlockSpec((STEP, rem, block, block), lambda i: (i, 1, 0, 0)),
            ANY,
        ],
        out_specs=pl.BlockSpec((peers, CAP * width, block), lambda i: (0, 0, 0)),
        name="back_remote",
        cost_estimate=pl.CostEstimate(
            flops=2 * width * row_blocks * rem * block * block, bytes_accessed=5 << 20, transcendentals=0
        ),
    )(slots, g, tiles, after)


def back_local_kernel(cols_ref, g_ref, tiles_ref, _, out_ref):
    i = pl.program_id(0)
    count, block = tiles_ref.shape[1], tiles_ref.shape[2]

    @pl.when(i == 0)
    def _():
        out_ref[...] = jnp.zeros_like(out_ref)

    for rr in range(STEP):
        lhs = g_ref[:, rr * block : (rr + 1) * block]
        for t in range(0, count, 2):
            base = (i * STEP + rr) * count + t
            rhs = jnp.concatenate([tiles_ref[rr, t + k] for k in range(2)], axis=1)
            term = dot(lhs, rhs, (1, 0))
            for k in range(2):
                out_ref[:, lanes(cols_ref[base + k], block)] += term[:, k * block : (k + 1) * block]


def back_local(cols, g, tiles, after):
    row_blocks, _, block, _ = tiles.shape
    width = g.shape[0]
    return pl.pallas_call(
        back_local_kernel,
        grid=(row_blocks // STEP,),
        out_shape=jax.ShapeDtypeStruct(g.shape, F32),
        in_specs=[
            SMEM,
            pl.BlockSpec((width, STEP * block), lambda i: (0, i)),
            pl.BlockSpec((STEP, TL, block, block), lambda i: (i, 0, 0, 0)),
            ANY,
        ],
        out_specs=pl.BlockSpec(g.shape, lambda i: (0, 0)),
        name="back_local",
        cost_estimate=pl.CostEstimate(
            flops=2 * width * row_blocks * TL * block * block, bytes_accessed=3 << 20, transcendentals=0
        ),
    )(cols, g, tiles, after)


STREAMS = 4


def finish_kernel(place_ref, held_ref, recv_ref, local_ref, out_ref, odd_scr, recv_scr, sems):
    width, block = out_ref.shape[0], recv_scr.shape[2]
    count = recv_scr.shape[0] // STREAMS

    def stream(n):
        part = pl.ds(n * count, count)
        return pltpu.make_async_copy(recv_ref.at[part], recv_scr.at[part], sems.at[n])

    for n in range(STREAMS):
        stream(n).start()
    out_ref[...] = local_ref[...]
    odd_scr[...] = jnp.zeros_like(odd_scr)
    for n in range(STREAMS):
        stream(n).wait()

        def body(p, carry):
            back = (p // (NZ * NC) - place_ref[0]) & (NY - 1)
            base = (back * NC + ((p ^ place_ref[1]) & 1)) * CAP
            z = p // NC % NZ
            even = lanes(jnp.maximum(held_ref[z, 0, base], 0), block)
            odd = lanes(jnp.maximum(held_ref[z, 0, base + 1], 0), block)
            out_ref[:, even] += recv_scr[p, :width].astype(F32)
            odd_scr[:, odd] += recv_scr[p, width : 2 * width].astype(F32)
            return carry

        lax.fori_loop(n * count, (n + 1) * count, body, 0, unroll=4)
    out_ref[...] += odd_scr[...]


def finish(place, held, recv, local):
    return pl.pallas_call(
        finish_kernel,
        out_shape=jax.ShapeDtypeStruct(local.shape, F32),
        in_specs=[SMEM, SMEM, ANY, VMEM],
        out_specs=VMEM,
        scratch_shapes=[
            pltpu.VMEM(local.shape, F32),
            pltpu.VMEM(recv.shape, recv.dtype),
            pltpu.SemaphoreType.DMA((STREAMS,)),
        ],
        name="finish",
        compiler_params=pltpu.CompilerParams(vmem_limit_bytes=16 << 20),
        cost_estimate=pl.CostEstimate(flops=recv.size, bytes_accessed=4 << 20, transcendentals=0),
    )(place, held, recv, local)


def split_bf16(x, terms):
    parts = []
    for _ in range(terms):
        part = lax.reduce_precision(x, 8, 7)
        parts.append(part.astype(BF))
        x = x - part
    return parts


def local(feats, weight, bias, tile_cols, tile_values, cotangent):
    width, nodes_dev = feats.shape
    hid_all = weight.shape[1]
    block = tile_values.shape[1]
    row_blocks = nodes_dev // block
    peers = lax.axis_size("rows")
    fpeers = lax.axis_size("feat")
    per_block = tile_cols.shape[0] // row_blocks
    remote_count = row_blocks * (per_block - TL)
    place = lax.axis_index("rows")
    y, z, c = place // (NZ * NC), place // NC % NZ, place % NC

    grid = tile_cols.reshape(row_blocks, per_block)
    tiles = tile_values.reshape(row_blocks, per_block, block, block)
    local_cols = (grid[:, :TL] % row_blocks).reshape(-1)
    remote_cols = grid[:, TL:].reshape(-1)
    owner = remote_cols // row_blocks
    inside = remote_cols % row_blocks
    order = jnp.arange(remote_count)
    earlier = (owner[:, None] == owner[None, :]) & (order[None, :] < order[:, None])
    rank = jnp.sum(earlier.astype(jnp.int32), axis=1)
    slots = owner * CAP + rank
    ahead = (owner // NC - z) & (NZ - 1)

    def place_of(ahead):
        return jnp.maximum(jnp.where(ahead <= NZ // 2, 2 * ahead - 1, 2 * (NZ - ahead)), 0)

    pos = place_of(ahead)
    back = (y - owner // (NZ * NC)) & (NY - 1)
    other = (owner ^ c) & 1
    near = ((other * NY + back) * NZ + pos) * CAP + rank

    def table(index):
        hit = index[None, :] == jnp.arange(peers * CAP)[:, None]
        return jnp.max(jnp.where(hit, inside[None, :], -1), axis=1)

    asked = table(near).reshape(NC, NY, PER)
    asked = jnp.stack([asked[0], shift(asked[1], dc=1)], axis=1)
    wanted = [asked[0]] + [shift(asked[ys], dy=-ys) for ys in range(1, NY)]
    wanted = jnp.stack(wanted).reshape(-1)

    up, down, parts = [feats], [feats], []
    for k in range(1, NZ // 2):
        up.append(shift(up[-1], dz=1))
        down.append(shift(down[-1], dz=-1))
    far_up = shift(up[-1][: width // 2], dz=1)
    far_down = shift(down[-1][width // 2 :], dz=-1)
    groups = ((feats, down[1], up[1]), (down[2], up[2]), (down[3], up[3], far_up, far_down))
    after = []
    agg = agg_local(local_cols, feats, tiles)
    for group, sources in zip(GROUPS, groups):
        packs = pack(group, wanted, sources, block, after)
        after = [packs[0]] if group == GROUPS[0] else [packs[0], agg]
        two, one, three = (shift(packs[ys], dy=ys) for ys in (2, 1, 3))
        moved = [packs[0], one, two, three]
        parts += moved
        parts.append(shift(jnp.concatenate([m[1:] for m in moved]), dc=1))

    bias_cols = jnp.pad(jnp.stack(split_bf16(bias, 3), axis=1), ((0, 0), (0, 125)))
    packed = jnp.concatenate([cotangent, weight, bias_cols], axis=1)
    packed = lax.all_gather(packed, "feat", axis=0, tiled=True)

    by_owner = wanted.reshape(NY * NC, NZ, CAP)
    steps = (jnp.arange(NZ) - z) & (NZ - 1)
    match = (place_of(steps)[:, None] == jnp.arange(NZ)[None, :])[:, None, :, None]
    held = jnp.sum(jnp.where(match, by_owner[None], 0), axis=2).reshape(NZ, 1, NY * NC * CAP)
    agg, held = agg_remote(near, held, parts, tiles, agg)

    ahead = [
        lax.ppermute(agg, "feat", [(k, (k + s) % fpeers) for k in range(fpeers)]) for s in (2, 1, 3)
    ]
    pieces = [agg, ahead[1], ahead[2], ahead[0]]
    along_z = [[(y0 * NZ + z0) * NC + c0 for z0 in range(NZ)] for y0 in range(NY) for c0 in range(NC)]
    held = lax.all_to_all(held, "rows", 0, 0, tiled=True, axis_index_groups=along_z)

    me = jnp.stack([lax.axis_index("feat"), c]).astype(jnp.int32)
    hidden_out, g, keep, give = mid(me, pieces, packed, weight, held)

    part = keep + shift(give, dc=1)
    twin = shift(part, flip_z=1)
    send = back_remote(slots, g, tiles, peers, part)
    send, twin = lax.optimization_barrier((send, twin))
    recv = lax.all_to_all(send, "rows", split_axis=0, concat_axis=0, tiled=True)
    own = back_local(local_cols, g, tiles, send)
    own, part, twin = lax.optimization_barrier((own, part, twin))
    part = part + twin
    pairs = [part] + [shift(part, flip_y=k) for k in (1, 2, 3)]
    part = (pairs[0] + pairs[1]) + (pairs[2] + pairs[3])
    pairs = [part] + [shift(part, flip_z=k) for k in (2, 4, 6)]
    grad_input = finish(jnp.stack([y, c]).astype(jnp.int32), held, recv, own)
    grad_input, pairs = lax.optimization_barrier((grad_input, pairs))
    part = (pairs[0] + pairs[1]) + (pairs[2] + pairs[3])
    other = shift(part, dc=1)
    total = jnp.where(c == 0, jnp.concatenate([part, other]), jnp.concatenate([other, part]))
    total = total / math.sqrt(nodes_dev * peers)
    grad_w = jnp.concatenate([total[k * width : (k + 1) * width] for k in range(hid_all // 128)], axis=1)
    grad_b = total[width * (hid_all // 128), :width]

    return hidden_out, grad_input, grad_w, grad_b


def solution(mesh):
    placed = (
        P("feat", "rows"),
        P("feat", None),
        P("feat"),
        P("rows"),
        P("rows", None, None),
        P("feat", "rows"),
    )
    return jax.shard_map(
        local,
        mesh=mesh,
        in_specs=placed,
        out_specs=(P("feat", "rows"), P("feat", "rows"), P("feat", None), P("feat")),
        check_vma=False,
    )
```

```python
import functools
import math

import jax
import jax.numpy as jnp
from jax import lax
from jax.experimental import pallas as pl
from jax.experimental.pallas import tpu as pltpu
from jax.sharding import PartitionSpec as P

TL = 4
BF = jnp.bfloat16
F32 = jnp.float32
VMEM = pl.BlockSpec(memory_space=pltpu.VMEM)
ANY = pl.BlockSpec(memory_space=pl.ANY)
SMEM = pl.BlockSpec(memory_space=pltpu.SMEM)


def lanes(index, width):
    return pl.ds(pl.multiple_of(index * width, width), width)


NY, NZ, NC = 4, 8, 2
CAP = 2
TAIL = 16
ORDER = (0, 1, 7, 2, 6, 3, 5, 4)
GROUPS = ((0, 3), (3, 5), (5, 8))
PER = NZ * CAP


def shift(x, dy=0, dz=0, dc=0, flip_y=0, flip_z=0):
    pairs = []
    for y in range(NY):
        for z in range(NZ):
            for c in range(NC):
                to_y, to_z = ((y ^ flip_y) + dy) % NY, ((z ^ flip_z) + dz) % NZ
                pairs.append(((y * NZ + z) * NC + c, (to_y * NZ + to_z) * NC + (c + dc) % NC))
    return lax.ppermute(x, "rows", pairs)


def pack_kernel(first, count, split, *refs):
    wanted_ref, sources, outs = refs[0], refs[1 : 1 + count + split], refs[-NY:]
    width, block = outs[0].shape[2], outs[0].shape[3]
    for ys in range(NY):
        for cs in range(NC):
            for q in range(count * CAP):
                w = wanted_ref[(ys * NC + cs) * PER + first * CAP + q]
                where = lanes(jnp.maximum(w, 0), block)
                j = q // CAP
                if split and j == count - 1:
                    outs[ys][cs, q, : width // 2] = sources[j][:, where]
                    outs[ys][cs, q, width // 2 :] = sources[j + 1][:, where]
                else:
                    outs[ys][cs, q] = sources[j][:, where]


def pack(group, wanted, sources, block, after):
    first, last = group
    count = last - first
    width = sources[0].shape[0]
    shape = jax.ShapeDtypeStruct((NC, count * CAP, width, block), BF)
    return pl.pallas_call(
        functools.partial(pack_kernel, first, count, len(sources) > count),
        out_shape=[shape] * NY,
        in_specs=[SMEM] + [VMEM] * len(sources) + [ANY] * len(after),
        out_specs=[VMEM] * NY,
        name="pack",
        cost_estimate=pl.CostEstimate(flops=0, bytes_accessed=3 << 20, transcendentals=0),
    )(wanted, *sources, *after)


def dot(a, b, dims):
    return lax.dot_general(a, b, ((dims[:1], dims[1:]), ((), ())), preferred_element_type=F32)


STEP = 8


def agg_local_kernel(cols_ref, feats_ref, tiles_ref, out_ref):
    i = pl.program_id(0)
    count, block = tiles_ref.shape[1], tiles_ref.shape[2]
    for rr in range(STEP):
        acc = None
        for t in range(0, count, 2):
            base = (i * STEP + rr) * count + t
            lhs = jnp.concatenate(
                [feats_ref[:, lanes(cols_ref[base + k], block)] for k in range(2)], axis=1
            )
            rhs = jnp.concatenate([tiles_ref[rr, t + k] for k in range(2)], axis=1)
            term = dot(lhs, rhs, (1, 1))
            acc = term if acc is None else acc + term
        out_ref[:, rr * block : (rr + 1) * block] = acc


def agg_local(cols, feats, tiles):
    row_blocks, _, block, _ = tiles.shape
    width = feats.shape[0]
    return pl.pallas_call(
        agg_local_kernel,
        grid=(row_blocks // STEP,),
        out_shape=jax.ShapeDtypeStruct((width, row_blocks * block), F32),
        in_specs=[
            SMEM,
            pl.BlockSpec(feats.shape, lambda i: (0, 0)),
            pl.BlockSpec((STEP, TL, block, block), lambda i: (i, 0, 0, 0)),
        ],
        out_specs=pl.BlockSpec((width, STEP * block), lambda i: (0, i)),
        name="agg_local",
        cost_estimate=pl.CostEstimate(
            flops=2 * width * row_blocks * TL * block * block, bytes_accessed=3 << 20, transcendentals=0
        ),
    )(cols, feats, tiles)


def agg_remote_kernel(slots_ref, held_ref, tiles_ref, local_ref, *refs):
    parts, out_ref, held_out_ref, recv_ref = refs[:-3], refs[-3], refs[-2], refs[-1]
    i = pl.program_id(0)
    count, block = tiles_ref.shape[1], tiles_ref.shape[2]

    @pl.when(i == 0)
    def _():
        held_out_ref[...] = held_ref[...]
        n = 0
        for first, last in GROUPS:
            size = (last - first) * CAP
            for ys in range(NY):
                recv_ref[pl.ds(ys * PER + first * CAP, size)] = parts[n + ys][0]
                recv_ref[pl.ds((NY + ys) * PER + first * CAP, size)] = parts[n + NY][ys]
            n += NY + 1

    for rr in range(STEP):
        acc = local_ref[:, rr * block : (rr + 1) * block]
        for t in range(0, count, 2):
            base = (i * STEP + rr) * count + t
            lhs = jnp.concatenate([recv_ref[slots_ref[base + k]] for k in range(2)], axis=1)
            rhs = jnp.concatenate([tiles_ref[rr, t + k] for k in range(2)], axis=1)
            acc = acc + dot(lhs, rhs, (1, 1))
        out_ref[:, rr * block : (rr + 1) * block] = acc.astype(out_ref.dtype)


def agg_remote(slots, held, parts, tiles, local):
    row_blocks, per_block, block, _ = tiles.shape
    rem = per_block - TL
    width = local.shape[0]
    specs = []
    for n, part in enumerate(parts):
        lead = 1 if n % (NY + 1) < NY else NY
        specs.append(pl.BlockSpec((lead,) + part.shape[1:], lambda i: (0, 0, 0, 0)))
    return pl.pallas_call(
        agg_remote_kernel,
        grid=(row_blocks // STEP,),
        out_shape=(jax.ShapeDtypeStruct(local.shape, BF), jax.ShapeDtypeStruct(held.shape, held.dtype)),
        in_specs=[
            SMEM,
            pl.BlockSpec(held.shape, lambda i: (0, 0, 0)),
            pl.BlockSpec((STEP, rem, block, block), lambda i: (i, 1, 0, 0)),
            pl.BlockSpec((width, STEP * block), lambda i: (0, i)),
        ]
        + specs,
        out_specs=(
            pl.BlockSpec((width, STEP * block), lambda i: (0, i)),
            pl.BlockSpec(held.shape, lambda i: (0, 0, 0)),
        ),
        scratch_shapes=[pltpu.VMEM((NY * NC * PER, width, block), BF)],
        name="agg_remote",
        cost_estimate=pl.CostEstimate(
            flops=2 * width * row_blocks * rem * block * block, bytes_accessed=5 << 20, transcendentals=0
        ),
    )(slots, held, tiles, local, *parts)


def mid_kernel(
    me_ref,
    _,
    own_ref,
    low_ref,
    high_ref,
    far_ref,
    cot_ref,
    w_ref,
    bias_ref,
    wown_ref,
    hid_ref,
    g_ref,
    keep_ref,
    give_ref,
    agg_scr,
    hid_scr,
    wt_scr,
    gb_scr,
    sums_scr,
):
    i = pl.program_id(0)
    width = own_ref.shape[0]
    count = agg_scr.shape[0] // width
    me = me_ref[0]

    def rows(ahead):
        return pl.ds(pl.multiple_of(lax.rem(me + ahead, count) * width, width), width)

    @pl.when(i == 0)
    def _():
        wt_scr[...] = w_ref[...].astype(F32).T.astype(BF)
        sums_scr[...] = jnp.zeros_like(sums_scr)
        gb_scr[...] = jnp.zeros_like(gb_scr)

    agg_scr[rows(3)] = low_ref[...]
    agg_scr[rows(1)] = high_ref[...]
    agg_scr[rows(2)] = far_ref[...]
    agg_scr[rows(0)] = own_ref[...]
    pre = dot(wt_scr[...], agg_scr[...], (1, 0))
    bias = bias_ref[:, :3].astype(F32)
    pre = pre + ((bias[:, 2:3] + bias[:, 1:2]) + bias[:, 0:1])
    sigma = jax.nn.sigmoid(pre)
    hid_scr[...] = (pre * sigma).astype(BF)
    hid_ref[...] = hid_scr[rows(0)]
    grad_pre = cot_ref[...].astype(F32) * (sigma * (1.0 + pre * (1.0 - sigma)))
    total = grad_pre[:, :128]
    for k in range(1, grad_pre.shape[1] // 128):
        total = total + grad_pre[:, k * 128 : (k + 1) * 128]
    gb_scr[...] += total
    grad_b = grad_pre.astype(BF)
    g_ref[...] = dot(wown_ref[...], grad_b, (1, 0)).astype(BF)
    grad_w = dot(own_ref[...], grad_b, (1, 1))
    for k in range(grad_w.shape[1] // 128):
        sums_scr[k * width : (k + 1) * width] += grad_w[:, k * 128 : (k + 1) * 128]

    @pl.when(i == pl.num_programs(0) - 1)
    def _():
        half = keep_ref.shape[0]
        own = gb_scr[rows(0)]
        sums_scr[2 * half - TAIL : 2 * half - TAIL + 1, :width] = jnp.sum(own.T, axis=0, keepdims=True)
        keep_ref[...] = sums_scr[pl.ds(pl.multiple_of(me_ref[1] * half, half), half)]
        give_ref[...] = sums_scr[pl.ds(pl.multiple_of((1 - me_ref[1]) * half, half), half)]


def mid(me, pieces, packed, w_own, after):
    own, low, high, far = pieces
    width, nodes = own.shape
    hid_all = packed.shape[0]
    chunk = 512
    half = (width * (hid_all // 128) + TAIL) // NC
    col = lambda i: (0, i)
    return pl.pallas_call(
        mid_kernel,
        grid=(nodes // chunk,),
        out_shape=(
            jax.ShapeDtypeStruct((width, nodes), BF),
            jax.ShapeDtypeStruct((width, nodes), BF),
            jax.ShapeDtypeStruct((half, 128), F32),
            jax.ShapeDtypeStruct((half, 128), F32),
        ),
        in_specs=[
            SMEM,
            ANY,
            pl.BlockSpec((width, chunk), col),
            pl.BlockSpec((width, chunk), col),
            pl.BlockSpec((width, chunk), col),
            pl.BlockSpec((width, chunk), col),
            pl.BlockSpec((hid_all, chunk), col),
            pl.BlockSpec((hid_all, hid_all), lambda i: (0, nodes // hid_all)),
            pl.BlockSpec((hid_all, 128), lambda i: (0, (nodes + hid_all) // 128)),
            pl.BlockSpec((width, hid_all), lambda i: (0, 0)),
        ],
        out_specs=(
            pl.BlockSpec((width, chunk), col),
            pl.BlockSpec((width, chunk), col),
            pl.BlockSpec((half, 128), lambda i: (0, 0)),
            pl.BlockSpec((half, 128), lambda i: (0, 0)),
        ),
        scratch_shapes=[
            pltpu.VMEM((hid_all, chunk), BF),
            pltpu.VMEM((hid_all, chunk), BF),
            pltpu.VMEM((hid_all, hid_all), BF),
            pltpu.VMEM((hid_all, 128), F32),
            pltpu.VMEM((NC * half, 128), F32),
        ],
        name="mid",
        cost_estimate=pl.CostEstimate(
            flops=2 * nodes * hid_all * (hid_all + 2 * width),
            bytes_accessed=3 << 20,
            transcendentals=nodes * hid_all,
        ),
    )(me, after, own, low, high, far, packed, packed, packed, w_own)


def back_remote_kernel(slots_ref, g_ref, tiles_ref, _, out_ref):
    i = pl.program_id(0)
    width = g_ref.shape[0]
    count, block = tiles_ref.shape[1], tiles_ref.shape[2]

    @pl.when(i == 0)
    def _():
        out_ref[...] = jnp.zeros_like(out_ref)

    for rr in range(STEP):
        lhs = g_ref[:, rr * block : (rr + 1) * block]
        for t in range(0, count, 2):
            base = (i * STEP + rr) * count + t
            rhs = jnp.concatenate([tiles_ref[rr, t + k] for k in range(2)], axis=1)
            term = dot(lhs, rhs, (1, 0)).astype(BF)
            for k in range(2):
                slot = slots_ref[base + k]
                row = pl.multiple_of((slot % CAP) * width, width)
                out_ref[slot // CAP, pl.ds(row, width)] = term[:, k * block : (k + 1) * block]


def back_remote(slots, g, tiles, peers, after):
    row_blocks, per_block, block, _ = tiles.shape
    rem = per_block - TL
    width = g.shape[0]
    return pl.pallas_call(
        back_remote_kernel,
        grid=(row_blocks // STEP,),
        out_shape=jax.ShapeDtypeStruct((peers, CAP * width, block), BF),
        in_specs=[
            SMEM,
            pl.BlockSpec((width, STEP * block), lambda i: (0, i)),
            pl.BlockSpec((STEP, rem, block, block), lambda i: (i, 1, 0, 0)),
            ANY,
        ],
        out_specs=pl.BlockSpec((peers, CAP * width, block), lambda i: (0, 0, 0)),
        name="back_remote",
        cost_estimate=pl.CostEstimate(
            flops=2 * width * row_blocks * rem * block * block, bytes_accessed=5 << 20, transcendentals=0
        ),
    )(slots, g, tiles, after)


def back_local_kernel(cols_ref, g_ref, tiles_ref, _, out_ref):
    i = pl.program_id(0)
    count, block = tiles_ref.shape[1], tiles_ref.shape[2]

    @pl.when(i == 0)
    def _():
        out_ref[...] = jnp.zeros_like(out_ref)

    for rr in range(STEP):
        lhs = g_ref[:, rr * block : (rr + 1) * block]
        for t in range(0, count, 2):
            base = (i * STEP + rr) * count + t
            rhs = jnp.concatenate([tiles_ref[rr, t + k] for k in range(2)], axis=1)
            term = dot(lhs, rhs, (1, 0))
            for k in range(2):
                out_ref[:, lanes(cols_ref[base + k], block)] += term[:, k * block : (k + 1) * block]


def back_local(cols, g, tiles, after):
    row_blocks, _, block, _ = tiles.shape
    width = g.shape[0]
    return pl.pallas_call(
        back_local_kernel,
        grid=(row_blocks // STEP,),
        out_shape=jax.ShapeDtypeStruct(g.shape, F32),
        in_specs=[
            SMEM,
            pl.BlockSpec((width, STEP * block), lambda i: (0, i)),
            pl.BlockSpec((STEP, TL, block, block), lambda i: (i, 0, 0, 0)),
            ANY,
        ],
        out_specs=pl.BlockSpec(g.shape, lambda i: (0, 0)),
        name="back_local",
        cost_estimate=pl.CostEstimate(
            flops=2 * width * row_blocks * TL * block * block, bytes_accessed=3 << 20, transcendentals=0
        ),
    )(cols, g, tiles, after)


STREAMS = 4


def finish_kernel(place_ref, held_ref, recv_ref, local_ref, out_ref, odd_scr, recv_scr, sems):
    width, block = out_ref.shape[0], recv_scr.shape[2]
    count = recv_scr.shape[0] // STREAMS

    def stream(n):
        part = pl.ds(n * count, count)
        return pltpu.make_async_copy(recv_ref.at[part], recv_scr.at[part], sems.at[n])

    for n in range(STREAMS):
        stream(n).start()
    out_ref[...] = local_ref[...]
    odd_scr[...] = jnp.zeros_like(odd_scr)
    for n in range(STREAMS):
        stream(n).wait()

        def body(p, carry):
            back = (p // (NZ * NC) - place_ref[0]) & (NY - 1)
            base = (back * NC + ((p ^ place_ref[1]) & 1)) * CAP
            z = p // NC % NZ
            even = lanes(jnp.maximum(held_ref[z, 0, base], 0), block)
            odd = lanes(jnp.maximum(held_ref[z, 0, base + 1], 0), block)
            out_ref[:, even] += recv_scr[p, :width].astype(F32)
            odd_scr[:, odd] += recv_scr[p, width : 2 * width].astype(F32)
            return carry

        lax.fori_loop(n * count, (n + 1) * count, body, 0, unroll=4)
    out_ref[...] += odd_scr[...]


def finish(place, held, recv, local):
    return pl.pallas_call(
        finish_kernel,
        out_shape=jax.ShapeDtypeStruct(local.shape, F32),
        in_specs=[SMEM, SMEM, ANY, VMEM],
        out_specs=VMEM,
        scratch_shapes=[
            pltpu.VMEM(local.shape, F32),
            pltpu.VMEM(recv.shape, recv.dtype),
            pltpu.SemaphoreType.DMA((STREAMS,)),
        ],
        name="finish",
        compiler_params=pltpu.CompilerParams(vmem_limit_bytes=16 << 20),
        cost_estimate=pl.CostEstimate(flops=recv.size, bytes_accessed=4 << 20, transcendentals=0),
    )(place, held, recv, local)


def split_bf16(x, terms):
    parts = []
    for _ in range(terms):
        part = lax.reduce_precision(x, 8, 7)
        parts.append(part.astype(BF))
        x = x - part
    return parts


def local(feats, weight, bias, tile_cols, tile_values, cotangent):
    width, nodes_dev = feats.shape
    hid_all = weight.shape[1]
    block = tile_values.shape[1]
    row_blocks = nodes_dev // block
    peers = lax.axis_size("rows")
    fpeers = lax.axis_size("feat")
    per_block = tile_cols.shape[0] // row_blocks
    remote_count = row_blocks * (per_block - TL)
    place = lax.axis_index("rows")
    y, z, c = place // (NZ * NC), place // NC % NZ, place % NC

    grid = tile_cols.reshape(row_blocks, per_block)
    tiles = tile_values.reshape(row_blocks, per_block, block, block)
    local_cols = (grid[:, :TL] % row_blocks).reshape(-1)
    remote_cols = grid[:, TL:].reshape(-1)
    owner = remote_cols // row_blocks
    inside = remote_cols % row_blocks
    order = jnp.arange(remote_count)
    earlier = (owner[:, None] == owner[None, :]) & (order[None, :] < order[:, None])
    rank = jnp.sum(earlier.astype(jnp.int32), axis=1)
    slots = owner * CAP + rank
    ahead = (owner // NC - z) & (NZ - 1)

    def place_of(ahead):
        return jnp.maximum(jnp.where(ahead <= NZ // 2, 2 * ahead - 1, 2 * (NZ - ahead)), 0)

    pos = place_of(ahead)
    back = (y - owner // (NZ * NC)) & (NY - 1)
    other = (owner ^ c) & 1
    near = ((other * NY + back) * NZ + pos) * CAP + rank

    def table(index):
        hit = index[None, :] == jnp.arange(peers * CAP)[:, None]
        return jnp.max(jnp.where(hit, inside[None, :], -1), axis=1)

    asked = table(near).reshape(NC, NY, PER)
    asked = jnp.stack([asked[0], shift(asked[1], dc=1)], axis=1)
    wanted = [asked[0]] + [shift(asked[ys], dy=-ys) for ys in range(1, NY)]
    wanted = jnp.stack(wanted).reshape(-1)

    up, down, parts = [feats], [feats], []
    for k in range(1, NZ // 2):
        up.append(shift(up[-1], dz=1))
        down.append(shift(down[-1], dz=-1))
    far_up = shift(up[-1][: width // 2], dz=1)
    far_down = shift(down[-1][width // 2 :], dz=-1)
    groups = ((feats, down[1], up[1]), (down[2], up[2]), (down[3], up[3], far_up, far_down))
    after = []
    agg = agg_local(local_cols, feats, tiles)
    for group, sources in zip(GROUPS, groups):
        packs = pack(group, wanted, sources, block, after)
        after = [packs[0]] if group == GROUPS[0] else [packs[0], agg]
        two, one, three = (shift(packs[ys], dy=ys) for ys in (2, 1, 3))
        moved = [packs[0], one, two, three]
        parts += moved
        parts.append(shift(jnp.concatenate([m[1:] for m in moved]), dc=1))

    bias_cols = jnp.pad(jnp.stack(split_bf16(bias, 3), axis=1), ((0, 0), (0, 125)))
    packed = jnp.concatenate([cotangent, weight, bias_cols], axis=1)
    packed = lax.all_gather(packed, "feat", axis=0, tiled=True)

    by_owner = wanted.reshape(NY * NC, NZ, CAP)
    steps = (jnp.arange(NZ) - z) & (NZ - 1)
    match = (place_of(steps)[:, None] == jnp.arange(NZ)[None, :])[:, None, :, None]
    held = jnp.sum(jnp.where(match, by_owner[None], 0), axis=2).reshape(NZ, 1, NY * NC * CAP)
    agg, held = agg_remote(near, held, parts, tiles, agg)

    ahead = [
        lax.ppermute(agg, "feat", [(k, (k + s) % fpeers) for k in range(fpeers)]) for s in (2, 1, 3)
    ]
    pieces = [agg, ahead[1], ahead[2], ahead[0]]
    along_z = [[(y0 * NZ + z0) * NC + c0 for z0 in range(NZ)] for y0 in range(NY) for c0 in range(NC)]
    held = lax.all_to_all(held, "rows", 0, 0, tiled=True, axis_index_groups=along_z)

    me = jnp.stack([lax.axis_index("feat"), c]).astype(jnp.int32)
    hidden_out, g, keep, give = mid(me, pieces, packed, weight, held)

    part = keep + shift(give, dc=1)
    twin = shift(part, flip_z=1)
    send = back_remote(slots, g, tiles, peers, part)
    send, twin = lax.optimization_barrier((send, twin))
    recv = lax.all_to_all(send, "rows", split_axis=0, concat_axis=0, tiled=True)
    own = back_local(local_cols, g, tiles, send)
    own, part, twin = lax.optimization_barrier((own, part, twin))
    part = part + twin
    pairs = [part] + [shift(part, flip_y=k) for k in (1, 2, 3)]
    part = (pairs[0] + pairs[1]) + (pairs[2] + pairs[3])
    pairs = [part] + [shift(part, flip_z=k) for k in (2, 4, 6)]
    grad_input = finish(jnp.stack([y, c]).astype(jnp.int32), held, recv, own)
    grad_input, pairs = lax.optimization_barrier((grad_input, pairs))
    part = (pairs[0] + pairs[1]) + (pairs[2] + pairs[3])
    other = shift(part, dc=1)
    total = jnp.where(c == 0, jnp.concatenate([part, other]), jnp.concatenate([other, part]))
    total = total / math.sqrt(nodes_dev * peers)
    grad_w = jnp.concatenate([total[k * width : (k + 1) * width] for k in range(hid_all // 128)], axis=1)
    grad_b = total[width * (hid_all // 128), :width]

    return hidden_out, grad_input, grad_w, grad_b


def solution(mesh):
    placed = (
        P("feat", "rows"),
        P("feat", None),
        P("feat"),
        P("rows"),
        P("rows", None, None),
        P("feat", "rows"),
    )
    return jax.shard_map(
        local,
        mesh=mesh,
        in_specs=placed,
        out_specs=(P("feat", "rows"), P("feat", "rows"), P("feat", None), P("feat")),
        check_vma=False,
    )
```
